128 devices in a mesh: expert: 8 (over y, core), tok: 16 (over z, x).
Axes of the slice: x: 4, y: 4, z: 4, core: 2. Of those that a mesh axis runs over, the one named last changes fastest.
Arguments:
- hidden: bfloat16 [8, 4096, 2048], P('expert', 'tok'), may hold values from -40 to 40, as said below
- token_ids: int32 [8, 4096], P('expert', 'tok'), may hold values from 0 to 128004, as said below
- weights: bfloat16 [8, 2048, 8192], P('expert', None, 'tok'), may hold values from -6 to 6
Outputs:
- merged: float32 [2048, 8192], P(None, 'tok')
The draws below stay inside these ranges and needn't reach their ends.
Inputs may be any that keep to these rules, and one draw needn't show every extreme that they name: `token_ids`: each expert's tokens come in sequences of 128 slots: slot 0 holds 128000, then between 63 and 126 further token ids below 128000, then the padding id 128004 in the remaining slots (one or more). `hidden`: channel scales differ by up to a factor of ten.
All inputs are finite; a program needn't handle non-finite values.
Results may differ from the reference program's by a relative error of at most 0.0017.
Values may be sent and summed in bfloat16 or wider, within the bound.
A program may use at most 256 MiB of HBM per device.

```python
import math
import jax
import jax.numpy as jnp
from jax import lax

D = 2048
FF = 8192
SEQ = 128
EXPERTS = 8
TOKENS = 4096


def draw_hidden(key, part):
    first, second = jax.random.split(key, 2)
    base = jax.random.normal(first, (EXPERTS, TOKENS, D), jnp.float32)
    scales = jnp.exp(jax.random.uniform(second, (EXPERTS, 1, D), jnp.float32) * math.log(10.0))
    mixed = jnp.clip(base, -4.0, 4.0)
    return (mixed * scales).astype(jnp.bfloat16)


def draw_token_ids(key, part):
    first, second = jax.random.split(key)
    blocks = TOKENS // SEQ
    lengths = jax.random.randint(first, (EXPERTS, blocks, 1), SEQ // 2, SEQ)
    words = jax.random.randint(second, (EXPERTS, blocks, SEQ), 0, 128000)
    position = jnp.arange(SEQ)[None, None, :]
    ids = jnp.where(position == 0, 128000, jnp.where(position < lengths, words, 128004))
    return ids.reshape(EXPERTS, TOKENS).astype(jnp.int32)


def levels(own_key, shape, cuts, smallest, top_value):
    def one(dim, parts):
        steps = jax.random.uniform(jax.random.fold_in(jax.random.fold_in(own_key, 6), dim), (parts,), jnp.float32, smallest / len(cuts), top_value / len(cuts))
        return jnp.repeat(jnp.exp(steps), shape[dim] // parts).reshape((-1,) + (1,) * (len(shape) - dim - 1))

    level = one(*cuts[0])
    for cut in cuts[1:]:
        level = level * one(*cut)
    return level


def gaussian(stream_key, shape, deviation, most, cuts=(), held_as=jnp.bfloat16):
    gain = levels(stream_key, shape, cuts, -0.22, 0.18) if cuts else 1.0
    result = jax.random.normal(stream_key, shape, jnp.float32) * deviation * gain
    return jnp.minimum(jnp.maximum(result, -most), most).astype(held_as)


def setup_inputs(seed: int = 0) -> dict:
    streams_of = jax.random.split(jax.random.key(seed), 4)
    hidden = draw_hidden(jax.random.fold_in(streams_of[3], 71), 0)
    token_ids = draw_token_ids(jax.random.fold_in(streams_of[3], 71), 0)
    weights = gaussian(streams_of[2], (EXPERTS, D, FF), 1.0, 6.0, ((0, 8), (2, 16)))
    return dict(hidden=hidden, token_ids=token_ids, weights=weights)


def reference(hidden, token_ids, weights):
    live = token_ids != 128004
    masked = jnp.where(live[:, :, None], hidden, 0).astype(jnp.bfloat16)
    counts = jnp.sum(live.astype(jnp.float32), axis=1)
    width = hidden.shape[2]

    def one_expert(carry, inputs):
        tokens, weight, count = inputs
        gram = jnp.dot(tokens.T.astype(jnp.float32), tokens.astype(jnp.float32), preferred_element_type=jnp.float32)
        upward = jnp.dot(tokens.astype(jnp.float32), weight.astype(jnp.float32), preferred_element_type=jnp.float32).astype(jnp.bfloat16)
        projected = jnp.dot(tokens.T.astype(jnp.float32), upward.astype(jnp.float32), preferred_element_type=jnp.float32)
        squares = jnp.diagonal(gram)
        terms = (0.9 * projected + 0.1 * squares[:, None] * weight.astype(jnp.float32)) / count
        return ((carry[0] + gram / count, carry[1] + terms), None)
    start = (jnp.zeros((width, width), jnp.float32), jnp.zeros((width, weights.shape[2]), jnp.float32))
    (total, rhs), _ = lax.scan(one_expert, start, (masked, weights, counts))
    system = jnp.where(jnp.eye(width, dtype=bool), total, 0.9 * total)
    factor = jnp.linalg.cholesky(system)
    middle = jax.scipy.linalg.solve_triangular(factor, rhs, lower=True)
    return jax.scipy.linalg.solve_triangular(factor, middle, lower=True, trans=1)
```

```python
import functools

import jax
import jax.numpy as jnp
from jax import lax
from jax.experimental import pallas as pl
from jax.experimental.pallas import tpu as pltpu
from jax.sharding import PartitionSpec as P

F32, BF16 = jnp.float32, jnp.bfloat16
CHUNKS = 4
INNER_TOL = 2e-3
OUTER_TOL = 2e-5
ROWS = 16


def tdot(left, right):
    return lax.dot_general(left, right, (((0,), (0,)), ((), ())), preferred_element_type=F32)


def solve_kernel(width, cols, s_hbm, b_ref, x_ref, sh, sm, sl, stage, stack, r, ri, p, d, q, rr, target, nn, flag, sems):
    blk = stage.shape[1]
    count = width // blk

    def fetch(i, slot):
        return pltpu.make_async_copy(s_hbm.at[pl.ds(i * blk, blk)], stage.at[slot], sems.at[slot])

    fetch(0, 0).start()

    def load(i, carry):
        slot = lax.rem(i, 2)
        fetch(i, slot).wait()

        @pl.when(i + 1 < count)
        def _():
            fetch(i + 1, 1 - slot).start()

        def split(j, c):
            rows = stage[slot, pl.ds(pl.multiple_of(j * ROWS, ROWS), ROWS), :]
            at = pl.ds(pl.multiple_of(i * blk + j * ROWS, ROWS), ROWS)
            high = rows.astype(BF16)
            rest = rows - high.astype(F32)
            mid = rest.astype(BF16)
            sh[at, :] = high
            sm[at, :] = mid
            sl[at, :] = (rest - mid.astype(F32)).astype(BF16)
            return c

        lax.fori_loop(0, blk // ROWS, split, 0)
        return carry

    lax.fori_loop(0, count, load, 0)

    parts = cols // ROWS

    def at(i):
        return slice(i * ROWS, (i + 1) * ROWS)

    def lanes(v):
        return jnp.broadcast_to(v, (ROWS, 128))

    for i in range(parts):
        b = b_ref[at(i), :]
        x_ref[at(i), :] = jnp.zeros_like(b)
        r[at(i), :] = b
        nn[at(i), :] = lanes(jnp.sum(b * b, axis=1, keepdims=True))

    def outer(carry):
        k, _ = carry
        for i in range(parts):
            v = r[at(i), :]
            ri[at(i), :] = v
            p[at(i), :] = v
            d[at(i), :] = jnp.zeros_like(v)
            rr[at(i), :] = nn[at(i), :]
            target[at(i), :] = nn[at(i), :] * (INNER_TOL * INNER_TOL)

        def inner(carry):
            it, _ = carry
            for i in range(parts):
                v = p[at(i), :]
                high = v.astype(BF16)
                stack[at(i), :] = high
                stack[cols + i * ROWS : cols + (i + 1) * ROWS, :] = (v - high.astype(F32)).astype(BF16)
            wide = jnp.dot(stack[: 2 * cols, :], sh[...], preferred_element_type=F32)
            q[...] = wide[:cols] + wide[cols:]

            @pl.when(k >= 2)
            def _():
                q[...] += jnp.dot(stack[:cols, :], sm[...], preferred_element_type=F32)

            worst = jnp.float32(-1.0)
            for i in range(parts):
                v, w = p[at(i), :], q[at(i), :]
                old = rr[at(i), :1]
                pq = jnp.sum(v * w, axis=1, keepdims=True)
                alpha = jnp.where(pq > 0, old / jnp.where(pq > 0, pq, 1.0), 0.0)
                d[at(i), :] += alpha * v
                res = ri[at(i), :] - alpha * w
                ri[at(i), :] = res
                new = jnp.sum(res * res, axis=1, keepdims=True)
                beta = jnp.where(old > 0, new / jnp.where(old > 0, old, 1.0), 0.0)
                p[at(i), :] = res + beta * v
                rr[at(i), :] = lanes(new)
                worst = jnp.maximum(worst, jnp.max(new - target[at(i), :1]))
            return it + 1, worst

        cap = jnp.where(k < 2, 64, 4000)
        lax.while_loop(lambda c: jnp.logical_and(c[0] < cap, c[1] > 0), inner, (jnp.int32(0), jnp.float32(1.0)))

        for i in range(parts):
            v = x_ref[at(i), :] + d[at(i), :]
            d[at(i), :] = v
            high = v.astype(BF16)
            rest = v - high.astype(F32)
            mid = rest.astype(BF16)
            stack[at(i), :] = high
            stack[cols + i * ROWS : cols + (i + 1) * ROWS, :] = mid
            stack[2 * cols + i * ROWS : 2 * cols + (i + 1) * ROWS, :] = (rest - mid.astype(F32)).astype(BF16)
        wide = jnp.dot(stack[...], sh[...], preferred_element_type=F32)
        q[...] = wide[:cols] + wide[cols : 2 * cols] + wide[2 * cols :]
        wide = jnp.dot(stack[: 2 * cols, :], sm[...], preferred_element_type=F32)
        q[...] += wide[:cols] + wide[cols:]
        q[...] += jnp.dot(stack[:cols, :], sl[...], preferred_element_type=F32)
        worst = jnp.float32(-1.0)
        for i in range(parts):
            new = b_ref[at(i), :] - q[at(i), :]
            size = jnp.sum(new * new, axis=1, keepdims=True)
            better = size < nn[at(i), :1]
            x = jnp.where(better, d[at(i), :], x_ref[at(i), :])
            x_ref[at(i), :] = x
            r[at(i), :] = jnp.where(better, new, r[at(i), :])
            kept = jnp.where(better, size, nn[at(i), :1])
            nn[at(i), :] = lanes(kept)
            norm = jnp.sum(x * x, axis=1, keepdims=True)
            worst = jnp.maximum(worst, jnp.max(kept - (OUTER_TOL * OUTER_TOL) * norm))
        return k + 1, worst

    lax.while_loop(lambda c: jnp.logical_and(c[0] < 20, c[1] > 0), outer, (jnp.int32(0), jnp.float32(1.0)))


def solve(system, right):
    width = system.shape[0]
    cols = right.shape[0]
    vec = pltpu.VMEM((cols, width), F32)
    col = pltpu.VMEM((cols, 128), F32)
    piece = pltpu.VMEM((width, width), BF16)

    def body(s_hbm, b_ref, x_ref, sh, sm, sl, stage, stack, r, ri, p, d, q, rr, target, nn, sems):
        solve_kernel(width, cols, s_hbm, b_ref, x_ref, sh, sm, sl, stage, stack, r, ri, p, d, q, rr, target, nn, None, sems)

    return pl.pallas_call(
        body,
        out_shape=jax.ShapeDtypeStruct((cols, width), F32),
        in_specs=[pl.BlockSpec(memory_space=pl.ANY), pl.BlockSpec(memory_space=pltpu.VMEM)],
        out_specs=pl.BlockSpec(memory_space=pltpu.VMEM),
        scratch_shapes=[
            piece, piece, piece,
            pltpu.VMEM((2, 256, width), F32),
            pltpu.VMEM((3 * cols, width), BF16),
            vec, vec, vec, vec, vec,
            col, col, col,
            pltpu.SemaphoreType.DMA((2,)),
        ],
        compiler_params=pltpu.CompilerParams(vmem_limit_bytes=60 << 20),
        name="solve",
    )(system, right)


def local(hidden, token_ids, weights):
    tokens = hidden[0]
    weight = weights[0]
    live = token_ids[0] != 128004
    masked = jnp.where(live[:, None], tokens, 0)
    count, width = masked.shape
    cols = weight.shape[1]
    wide = masked.astype(F32)
    stats = jnp.concatenate([
        jnp.sum(wide * wide, axis=0),
        jnp.full((128,), jnp.sum(live.astype(F32))),
    ]).reshape(1, -1, 128)
    gathered = lax.all_gather(stats, ("expert", "tok"), axis=0, tiled=True)
    experts = lax.axis_size("expert")
    toks = lax.axis_size("tok")
    per_expert = jnp.sum(gathered.reshape(experts, toks, -1), axis=1)
    squares = per_expert[:, :width]
    counts = per_expert[:, width]
    diagonal = jnp.sum(squares / counts[:, None], axis=0)
    scale = 1.0 / jnp.sqrt(diagonal)
    mine = lax.axis_index("expert")
    band = lax.axis_index("tok")
    my_squares = lax.dynamic_index_in_dim(squares, mine, 0, keepdims=False)
    my_count = lax.dynamic_index_in_dim(counts, mine, 0, keepdims=False)

    band_rows = width // toks
    step = count // CHUNKS
    gram = jnp.zeros((band_rows, width), F32)
    projected = jnp.zeros((cols, width), F32)
    for c in range(CHUNKS):
        piece = lax.all_gather(masked[c * step : (c + 1) * step], "tok", axis=0, tiled=True)
        own = lax.dynamic_slice_in_dim(piece, band * band_rows, band_rows, axis=1)
        gram = gram + tdot(own, piece)
        upward = jnp.dot(piece, weight, preferred_element_type=F32).astype(BF16)
        projected = projected + tdot(upward, piece)

    rows = lax.psum(gram / my_count, "expert")
    row_scale = lax.dynamic_slice_in_dim(scale, band * band_rows, band_rows, axis=0)
    at_row = lax.broadcasted_iota(jnp.int32, rows.shape, 0) + band * band_rows
    at_col = lax.broadcasted_iota(jnp.int32, rows.shape, 1)
    rows = jnp.where(at_row == at_col, 1.0, 0.9 * rows * row_scale[:, None] * scale[None, :])
    system = lax.all_gather(rows, "tok", axis=0, tiled=True)

    terms = (0.9 * projected + 0.1 * my_squares[None, :] * weight.T.astype(F32)) / my_count
    right = lax.psum_scatter(terms * scale[None, :], "expert", scatter_dimension=0, tiled=True)
    answer = solve(system, right) * scale[None, :]
    return lax.all_gather(answer, "expert", axis=0, tiled=True).T


def solution(mesh):
    return jax.shard_map(
        local,
        mesh=mesh,
        in_specs=(P("expert", "tok", None), P("expert", "tok"), P("expert", None, "tok")),
        out_specs=P(None, "tok"),
        check_vma=False,
    )
```

```python
import functools

import jax
import jax.numpy as jnp
from jax import lax
from jax.experimental import pallas as pl
from jax.experimental.pallas import tpu as pltpu
from jax.sharding import PartitionSpec as P

F32, BF16 = jnp.float32, jnp.bfloat16
MESH = pl.DeviceIdType.MESH
SIDE = 4
INNER_TOL = 2e-3
OUTER_TOL = 2e-5
ROWS = 16


def near(i, step):
    return (i + step + SIDE) % SIDE


def remote(sems, index, source, target, device):
    send, recv = sems
    return pltpu.make_async_remote_copy(
        src_ref=source, dst_ref=target, send_sem=send.at[index], recv_sem=recv.at[index],
        device_id=device, device_id_type=MESH,
    )


def meet(devices):
    barrier = pltpu.get_barrier_semaphore()
    for device in devices:
        pl.semaphore_signal(barrier, inc=1, device_id=device, device_id_type=MESH)
    pl.semaphore_wait(barrier, len(devices))


def gather_kernel(toks, x_hbm, ids_ref, w_ref, terms_ref, gram_ref, X, cat, acc, wt, stat, stats, send, recv, own, stat_send, stat_recv):
    t = lax.axis_index("tok")
    z, x = t // SIDE, t % SIDE
    width, cols = w_ref.shape
    band = width // toks
    half = x_hbm.shape[0] // 2

    def tok(zz, xx):
        return {"tok": zz * SIDE + xx}

    meet([{"tok": (t + k) % toks} for k in range(1, toks)])
    mine = (X.at[z, x], X.at[SIDE + x, z])
    loads = [pltpu.make_async_copy(x_hbm.at[pl.ds(k * half, half)], mine[k], own.at[k]) for k in range(2)]
    for load in loads:
        load.start()

    rc = functools.partial(remote, (send, recv))

    def steps(base, block_of, part, to, here):
        up, down = near(here, 1), near(here, -1)
        first = [
            rc(base, block_of(here), block_of(here), to(up)),
            rc(base + 1, block_of(here), block_of(here), to(down)),
        ]
        onward = [
            rc(base + 2, part(down, 0), part(down, 0), to(up)),
            rc(base + 3, part(up, 1), part(up, 1), to(down)),
        ]
        return first, onward

    a_first, a_onward = steps(
        0, lambda i: X.at[z, i], lambda i, h: X.at[z, i, pl.ds(h * (half // 2), half // 2)], lambda i: tok(z, i), x)
    b_first, b_onward = steps(
        4, lambda i: X.at[SIDE + x, i], lambda i, h: X.at[SIDE + x, i, pl.ds(h * (half // 2), half // 2)], lambda i: tok(i, x), z)

    loads[0].wait()
    for copy in a_first:
        copy.start()
    loads[1].wait()
    for copy in b_first:
        copy.start()

    def clear(i, c):
        at = pl.ds(pl.multiple_of(i * ROWS, ROWS), ROWS)
        acc[at, :] = jnp.zeros((ROWS, width), F32)
        return c

    lax.fori_loop(0, acc.shape[0] // ROWS, clear, 0)

    live = jnp.sum(jnp.where(ids_ref[...] != 128004, 1.0, 0.0), axis=(0, 1), keepdims=True)

    def square(i, total):
        at = pl.ds(pl.multiple_of(i * ROWS, ROWS), ROWS)
        a = X[z, x, at, :].astype(F32)
        b = X[SIDE + x, z, at, :].astype(F32)
        return total + jnp.sum(a * a + b * b, axis=0, keepdims=True)

    stat[:, :width] = lax.fori_loop(0, half // ROWS, square, jnp.zeros((1, width), F32))
    stat[:, width:] = jnp.broadcast_to(live, (1, 128))

    def turn(i, c):
        at = pl.ds(pl.multiple_of(i * 256, 256), 256)
        wt[:, at] = w_ref[at, :].T
        return c

    lax.fori_loop(0, width // 256, turn, 0)

    for first, onward in ((a_first, a_onward), (b_first, b_onward)):
        for got, copy in zip(first, onward):
            got.wait_recv()
            copy.start()

    def share(k):
        return pltpu.make_async_remote_copy(
            src_ref=stat, dst_ref=stats.at[k], send_sem=stat_send.at[k], recv_sem=stat_recv.at[k],
            device_id={"tok": (t + k) % toks}, device_id_type=MESH,
        )

    for copy in a_onward + b_onward:
        copy.wait_recv()

    def group(base, g_of, to, here):
        up, down = near(here, 1), near(here, -1)

        def part(i, h):
            return X.at[g_of(i), pl.ds(2 * h, 2)]

        first = {}
        for h in range(2):
            first["up", h] = rc(base + h, part(here, h), part(here, h), to(up))
            first["down", h] = rc(base + 2 + h, part(here, h), part(here, h), to(down))
        onward = [
            rc(base + 4, part(down, 0), part(down, 0), to(up)),
            rc(base + 5, part(up, 1), part(up, 1), to(down)),
        ]
        return first, onward

    a_near, a_far = group(8, lambda i: i, lambda i: tok(i, x), z)
    b_near, b_far = group(14, lambda i: SIDE + i, lambda i: tok(z, i), x)
    for h in range(2):
        for copies in (a_near, b_near):
            copies["up", h].start()
            copies["down", 1 - h].start()

    lax.fori_loop(1, toks, lambda k, c: (share(k).start(), c)[1], 0)

    arrivals = {}
    for k, (first, far) in enumerate(((a_near, a_far), (b_near, b_far))):
        arrivals[4 + 2 * k] = (first["up", 0], far[0])
        arrivals[5 + 2 * k] = (first["down", 1], far[1])
        arrivals[8 + 2 * k] = (first["up", 1], None)
        arrivals[9 + 2 * k] = (first["down", 0], None)
        arrivals[12 + 2 * k] = (far[0], None)
        arrivals[13 + 2 * k] = (far[1], None)

    pair = 2 * half

    def step(s, c):
        @pl.when(s == 4)
        def _():
            for at in range(4, 8):
                got, copy = arrivals[at]
                got.wait_recv()
                copy.start()

        for at in range(8, 16):
            @pl.when(s == at)
            def _(at=at):
                arrivals[at][0].wait_recv()

        q, m = s // 4, s % 4
        kind, a = m // 2, m % 2
        close = (q % 3 + 1) // 2
        off = close * (3 - 2 * a) + 2 * (q // 3)
        h = a + (q // 2) * (1 - q // 3) * (1 - 2 * a)
        here = z * (1 - kind) + x * kind
        g = kind * SIDE + (here + off) % SIDE
        block = X.at[g, pl.ds(2 * h, 2)]
        rows = block[...].reshape(pair, width)
        upward = jnp.dot(rows, w_ref[...], preferred_element_type=F32).astype(BF16)
        cat[:cols, :] = upward.T
        cat[cols:, :] = block[:, :, pl.ds(pl.multiple_of(t * band, band), band)].reshape(pair, band).T

        def tile(n, c):
            at = pl.ds(pl.multiple_of(n * 512, 512), 512)
            acc[:, at] += jnp.dot(cat[...], block[:, :, at].reshape(pair, 512), preferred_element_type=F32)
            return c

        lax.fori_loop(0, width // 512, tile, 0)
        return c

    lax.fori_loop(0, 16, step, 0)

    lax.fori_loop(1, toks, lambda k, c: (share(k).wait_recv(), c)[1], 0)
    total = stat[...]
    for k in range(1, toks):
        total = total + stats[k]
    inverse = 1.0 / total[:, width : width + 1]
    squares = total[:, :width] * (0.1 * inverse)

    def finish(i, c):
        at = pl.ds(pl.multiple_of(i * ROWS, ROWS), ROWS)
        terms_ref[at, :] = acc[at, :] * (0.9 * inverse) + squares * wt[at, :].astype(F32)
        return c

    lax.fori_loop(0, cols // ROWS, finish, 0)

    def finish_gram(i, c):
        at = pl.ds(pl.multiple_of(i * ROWS, ROWS), ROWS)
        gram_ref[at, :] = acc[pl.ds(pl.multiple_of(cols + i * ROWS, ROWS), ROWS), :] * inverse
        return c

    lax.fori_loop(0, band // ROWS, finish_gram, 0)

    for copy in a_first + b_first + a_onward + b_onward + list(a_near.values()) + list(b_near.values()) + a_far + b_far:
        copy.wait_send()
    lax.fori_loop(1, toks, lambda k, c: (share(k).wait_send(), c)[1], 0)


def gather(masked, ids, weight, toks):
    count, width = masked.shape
    cols = weight.shape[1]
    band = width // toks
    half = count // 2
    vmem = pl.BlockSpec(memory_space=pltpu.VMEM)
    return pl.pallas_call(
        functools.partial(gather_kernel, toks),
        out_shape=(jax.ShapeDtypeStruct((cols, width), F32), jax.ShapeDtypeStruct((band, width), F32)),
        in_specs=[pl.BlockSpec(memory_space=pl.ANY), vmem, vmem],
        out_specs=(vmem, vmem),
        scratch_shapes=[
            pltpu.VMEM((2 * SIDE, SIDE, half, width), BF16),
            pltpu.VMEM((cols + band, 2 * half), BF16),
            pltpu.VMEM((cols + band, width), F32),
            pltpu.VMEM((cols, width), BF16),
            pltpu.VMEM((1, width + 128), F32),
            pltpu.VMEM((toks, 1, width + 128), F32),
            pltpu.SemaphoreType.DMA((20,)),
            pltpu.SemaphoreType.DMA((20,)),
            pltpu.SemaphoreType.DMA((2,)),
            pltpu.SemaphoreType.DMA((toks,)),
            pltpu.SemaphoreType.DMA((toks,)),
        ],
        compiler_params=pltpu.CompilerParams(collective_id=0, has_side_effects=True, vmem_limit_bytes=60 << 20),
        name="gather",
    )(masked, ids, weight)


def combine_kernel(g_ref, terms_ref, s, b_ref, pg, hg, rg, sg, pt, ht, far, close, send, recv, own):
    e, t = lax.axis_index("expert"), lax.axis_index("tok")
    y, c = e // 2, e % 2
    z, x = t // SIDE, t % SIDE
    rc = functools.partial(remote, (send, recv))

    def tok(zz, xx):
        return {"tok": zz * SIDE + xx}

    def chip(yy):
        return {"expert": yy * 2 + c}

    partner = {"expert": e + 1 - 2 * c}
    up, down, across = near(y, 1), near(y, -1), near(y, 2)
    meet([partner, chip(up), chip(down), chip(across), tok(near(z, 1), x), tok(near(z, -1), x), tok(z, near(x, 1)), tok(z, near(x, -1))])

    swap_g = rc(0, g_ref.at[1 - c], pg, partner)
    swap_t = rc(1, terms_ref.at[:, 1 - c], pt, partner)
    swap_g.start()
    swap_t.start()

    swap_g.wait_recv()
    for k in range(4):
        hg[k] = g_ref[c, k] + pg[k]
    scatter = [rc(1 + k, hg.at[near(y, k)], rg.at[k - 1], chip(near(y, k))) for k in range(1, 4)]
    for copy in scatter:
        copy.start()
    for copy in scatter:
        copy.wait_recv()
    sg[...] = hg[y] + rg[0] + rg[1] + rg[2]
    rows = s.at[z, x, c, y // 2, pl.ds((y % 2) * 16, 16)]
    keep = pltpu.make_async_copy(sg, rows, own.at[0])
    keep.start()
    spread = [rc(4 + k, sg, rows, chip(near(y, k))) for k in range(1, 4)]
    for copy in spread:
        copy.start()

    swap_t.wait_recv()
    for k in range(4):
        ht[k] = terms_ref[k, c] + pt[k]
    first_t = [
        rc(8, ht.at[across, pl.ds(0, 32)], far.at[0], chip(up)),
        rc(9, ht.at[across, pl.ds(32, 32)], far.at[1], chip(down)),
    ]
    for copy in first_t:
        copy.start()

    keep.wait()
    for copy in spread:
        copy.wait_recv()

    def stage(base, block, part, to, here):
        above, below = near(here, 1), near(here, -1)
        first = [rc(base, block(here), block(here), to(above)), rc(base + 1, block(here), block(here), to(below))]
        onward = [rc(base + 2, part(below, 0), part(below, 0), to(above)), rc(base + 3, part(above, 1), part(above, 1), to(below))]
        return first, onward

    a_first, a_onward = stage(10, lambda i: s.at[z, i, c, 0], lambda i, h: s.at[z, i, c, 0, pl.ds(16 * h, 16)], lambda i: tok(z, i), x)
    b_first, b_onward = stage(14, lambda i: s.at[i, x, c, 1], lambda i, h: s.at[i, x, c, 1, pl.ds(16 * h, 16)], lambda i: tok(i, x), z)
    for copy in a_first + b_first:
        copy.start()

    first_t[0].wait_recv()
    ht[up, :32] = ht[up, :32] + far[0]
    first_t[1].wait_recv()
    ht[down, 32:] = ht[down, 32:] + far[1]

    for got, copy in zip(a_first + b_first, a_onward + b_onward):
        got.wait_recv()
        copy.start()

    second_t = [rc(18, ht.at[up], close.at[0], chip(up)), rc(19, ht.at[down], close.at[1], chip(down))]
    for copy in second_t:
        copy.start()

    for copy in a_onward + b_onward:
        copy.wait_recv()

    a_near, a_far = stage(20, lambda i: s.at[i, :, c, 0], lambda i, h: s.at[i, pl.ds(2 * h, 2), c, 0], lambda i: tok(i, x), z)
    b_near, b_far = stage(24, lambda i: s.at[:, i, c, 1], lambda i, h: s.at[pl.ds(2 * h, 2), i, c, 1], lambda i: tok(z, i), x)
    for copy in a_near + b_near:
        copy.start()

    def pair(index, block):
        copy = rc(28 + index, block, block, partner)
        copy.start()
        return copy

    pairs = [pair(0, s.at[z, :, c, 0]), pair(1, s.at[:, x, c, 1])]

    for copy in second_t:
        copy.wait_recv()
    b_ref[...] = ht[y] + close[0] + close[1]

    for got, copy in zip(a_near + b_near, a_far + b_far):
        got.wait_recv()
        copy.start()
    pairs += [pair(2, s.at[near(z, -1), :, c, 0]), pair(3, s.at[near(z, 1), :, c, 0])]
    pairs += [pair(4, s.at[:, near(x, -1), c, 1]), pair(5, s.at[:, near(x, 1), c, 1])]
    for copy in a_far + b_far:
        copy.wait_recv()
    pairs += [pair(6, s.at[near(z, 2), :, c, 0]), pair(7, s.at[:, near(x, 2), c, 1])]
    for copy in pairs:
        copy.wait_recv()
    for copy in [swap_g, swap_t] + scatter + spread + first_t + second_t + a_first + b_first + a_onward + b_onward + a_near + b_near + a_far + b_far + pairs:
        copy.wait_send()


def combine(gram, terms):
    band, width = gram.shape
    cols = terms.shape[0]
    part, share = band // 8, cols // 8
    vmem = pl.BlockSpec(memory_space=pltpu.VMEM)
    system, right = pl.pallas_call(
        combine_kernel,
        out_shape=(
            jax.ShapeDtypeStruct((SIDE, SIDE, 2, 2, 2 * part, width), F32),
            jax.ShapeDtypeStruct((share, width), F32),
        ),
        in_specs=[vmem, vmem],
        out_specs=(pl.BlockSpec(memory_space=pl.ANY), vmem),
        scratch_shapes=[
            pltpu.VMEM((4, part, width), F32),
            pltpu.VMEM((4, part, width), F32),
            pltpu.VMEM((3, part, width), F32),
            pltpu.VMEM((part, width), F32),
            pltpu.VMEM((4, share, width), F32),
            pltpu.VMEM((4, share, width), F32),
            pltpu.VMEM((2, share // 2, width), F32),
            pltpu.VMEM((2, share, width), F32),
            pltpu.SemaphoreType.DMA((36,)),
            pltpu.SemaphoreType.DMA((36,)),
            pltpu.SemaphoreType.DMA((1,)),
        ],
        compiler_params=pltpu.CompilerParams(collective_id=1, has_side_effects=True, vmem_limit_bytes=60 << 20),
        name="combine",
    )(gram.reshape(2, 4, part, width), terms.reshape(4, 2, share, width))
    return system.reshape(width, width), right


def spread_kernel(a_ref, out, send, recv, own):
    e = lax.axis_index("expert")
    y, c = e // 2, e % 2
    share = a_ref.shape[0]
    rc = functools.partial(remote, (send, recv))

    def chip(yy):
        return {"expert": yy * 2 + c}

    partner = {"expert": e + 1 - 2 * c}
    up, down, across = near(y, 1), near(y, -1), near(y, 2)
    meet([partner, chip(up), chip(down)])
    half = share // 2
    first = [rc(0, a_ref, out.at[y, c], chip(up)), rc(1, a_ref, out.at[y, c], chip(down))]
    pairs = [rc(2, a_ref, out.at[y, c], partner)]
    for copy in first + pairs:
        copy.start()
    keep = pltpu.make_async_copy(a_ref, out.at[y, c], own.at[0])
    keep.start()
    lower, upper = out.at[down, c, pl.ds(0, half)], out.at[up, c, pl.ds(half, half)]
    onward = [rc(3, lower, lower, chip(up)), rc(4, upper, upper, chip(down))]
    for k, (got, copy, at) in enumerate(zip(first, onward, (down, up))):
        got.wait_recv()
        copy.start()
        forward = rc(5 + k, out.at[at, c], out.at[at, c], partner)
        forward.start()
        pairs.append(forward)
    for k, copy in enumerate(onward):
        copy.wait_recv()
        part = out.at[across, c, pl.ds(half * k, half)]
        forward = rc(7 + k, part, part, partner)
        forward.start()
        pairs.append(forward)
    keep.wait()
    for copy in pairs:
        copy.wait_recv()
    for copy in first + onward + pairs:
        copy.wait_send()


def spread(answer):
    share, width = answer.shape
    out = pl.pallas_call(
        spread_kernel,
        out_shape=jax.ShapeDtypeStruct((4, 2, share, width), F32),
        in_specs=[pl.BlockSpec(memory_space=pltpu.VMEM)],
        out_specs=pl.BlockSpec(memory_space=pl.ANY),
        scratch_shapes=[pltpu.SemaphoreType.DMA((9,)), pltpu.SemaphoreType.DMA((9,)), pltpu.SemaphoreType.DMA((1,))],
        compiler_params=pltpu.CompilerParams(collective_id=2, has_side_effects=True),
        name="spread",
    )(answer)
    return out.reshape(8 * share, width)


def solve_kernel(width, cols, s_hbm, b_in, x_ref, sh, sm, sl, stage, diag, srow, scol, b_ref, stack, r, ri, p, d, q, rr, target, nn, sems, dsems):
    blk = stage.shape[1]
    count = width // blk

    def fetch(i, slot):
        return pltpu.make_async_copy(s_hbm.at[pl.ds(i * blk, blk)], stage.at[slot], sems.at[slot])

    fetch(0, 0).start()

    corners = [
        pltpu.make_async_copy(s_hbm.at[pl.ds(k * 128, 128), pl.ds(k * 128, 128)], diag.at[k], dsems.at[k])
        for k in range(width // 128)
    ]
    for corner in corners:
        corner.start()
    eye = lax.broadcasted_iota(jnp.int32, (128, 128), 0) == lax.broadcasted_iota(jnp.int32, (128, 128), 1)
    for k, corner in enumerate(corners):
        corner.wait()
        only = jnp.where(eye, diag[k], 0.0)
        srow[:, k * 128 : (k + 1) * 128] = 1.0 / jnp.sqrt(jnp.sum(only, axis=0, keepdims=True))
        scol[k * 128 : (k + 1) * 128, :] = jnp.broadcast_to(
            1.0 / jnp.sqrt(jnp.sum(only, axis=1, keepdims=True)), (128, 128))

    def load(i, carry):
        slot = lax.rem(i, 2)
        fetch(i, slot).wait()

        @pl.when(i + 1 < count)
        def _():
            fetch(i + 1, 1 - slot).start()

        def split(j, c):
            rows = stage[slot, pl.ds(pl.multiple_of(j * ROWS, ROWS), ROWS), :]
            at = pl.ds(pl.multiple_of(i * blk + j * ROWS, ROWS), ROWS)
            row = lax.broadcasted_iota(jnp.int32, rows.shape, 0) + (i * blk + j * ROWS)
            factor = jnp.where(row == lax.broadcasted_iota(jnp.int32, rows.shape, 1), 1.0, 0.9)
            rows = rows * factor * srow[...] * scol[at, :1]
            high = rows.astype(BF16)
            rest = rows - high.astype(F32)
            mid = rest.astype(BF16)
            sh[at, :] = high
            sm[at, :] = mid
            sl[at, :] = (rest - mid.astype(F32)).astype(BF16)
            return c

        lax.fori_loop(0, blk // ROWS, split, 0)
        return carry

    lax.fori_loop(0, count, load, 0)

    parts = cols // ROWS

    def at(i):
        return slice(i * ROWS, (i + 1) * ROWS)

    def lanes(v):
        return jnp.broadcast_to(v, (ROWS, 128))

    for i in range(parts):
        b = b_in[at(i), :] * srow[...]
        b_ref[at(i), :] = b
        x_ref[at(i), :] = jnp.zeros_like(b)
        r[at(i), :] = b
        nn[at(i), :] = lanes(jnp.sum(b * b, axis=1, keepdims=True))

    def outer(carry):
        k, _ = carry
        for i in range(parts):
            v = r[at(i), :]
            ri[at(i), :] = v
            p[at(i), :] = v
            d[at(i), :] = jnp.zeros_like(v)
            rr[at(i), :] = nn[at(i), :]
            target[at(i), :] = nn[at(i), :] * (INNER_TOL * INNER_TOL)

        def inner(carry):
            it, _ = carry
            for i in range(parts):
                v = p[at(i), :]
                high = v.astype(BF16)
                stack[at(i), :] = high
                stack[cols + i * ROWS : cols + (i + 1) * ROWS, :] = (v - high.astype(F32)).astype(BF16)
            wide = jnp.dot(stack[: 2 * cols, :], sh[...], preferred_element_type=F32)
            q[...] = wide[:cols] + wide[cols:]

            @pl.when(k >= 2)
            def _():
                q[...] += jnp.dot(stack[:cols, :], sm[...], preferred_element_type=F32)

            worst = jnp.float32(-1.0)
            for i in range(parts):
                v, w = p[at(i), :], q[at(i), :]
                old = rr[at(i), :1]
                pq = jnp.sum(v * w, axis=1, keepdims=True)
                alpha = jnp.where(pq > 0, old / jnp.where(pq > 0, pq, 1.0), 0.0)
                d[at(i), :] += alpha * v
                res = ri[at(i), :] - alpha * w
                ri[at(i), :] = res
                new = jnp.sum(res * res, axis=1, keepdims=True)
                beta = jnp.where(old > 0, new / jnp.where(old > 0, old, 1.0), 0.0)
                p[at(i), :] = res + beta * v
                rr[at(i), :] = lanes(new)
                worst = jnp.maximum(worst, jnp.max(new - target[at(i), :1]))
            return it + 1, worst

        cap = jnp.where(k < 2, 64, 4000)
        lax.while_loop(lambda c: jnp.logical_and(c[0] < cap, c[1] > 0), inner, (jnp.int32(0), jnp.float32(1.0)))

        for i in range(parts):
            v = x_ref[at(i), :] + d[at(i), :]
            d[at(i), :] = v
            high = v.astype(BF16)
            rest = v - high.astype(F32)
            mid = rest.astype(BF16)
            stack[at(i), :] = high
            stack[cols + i * ROWS : cols + (i + 1) * ROWS, :] = mid
            stack[2 * cols + i * ROWS : 2 * cols + (i + 1) * ROWS, :] = (rest - mid.astype(F32)).astype(BF16)
        wide = jnp.dot(stack[...], sh[...], preferred_element_type=F32)
        q[...] = wide[:cols] + wide[cols : 2 * cols] + wide[2 * cols :]
        wide = jnp.dot(stack[: 2 * cols, :], sm[...], preferred_element_type=F32)
        q[...] += wide[:cols] + wide[cols:]
        q[...] += jnp.dot(stack[:cols, :], sl[...], preferred_element_type=F32)
        worst = jnp.float32(-1.0)
        for i in range(parts):
            new = b_ref[at(i), :] - q[at(i), :]
            size = jnp.sum(new * new, axis=1, keepdims=True)
            better = size < nn[at(i), :1]
            x = jnp.where(better, d[at(i), :], x_ref[at(i), :])
            x_ref[at(i), :] = x
            r[at(i), :] = jnp.where(better, new, r[at(i), :])
            kept = jnp.where(better, size, nn[at(i), :1])
            nn[at(i), :] = lanes(kept)
            norm = jnp.sum(x * x, axis=1, keepdims=True)
            worst = jnp.maximum(worst, jnp.max(kept - (OUTER_TOL * OUTER_TOL) * norm))
        return k + 1, worst

    lax.while_loop(lambda c: jnp.logical_and(c[0] < 20, c[1] > 0), outer, (jnp.int32(0), jnp.float32(1.0)))
    for i in range(parts):
        x_ref[at(i), :] = x_ref[at(i), :] * srow[...]


def solve(system, right):
    width = system.shape[0]
    cols = right.shape[0]
    vec = pltpu.VMEM((cols, width), F32)
    col = pltpu.VMEM((cols, 128), F32)
    piece = pltpu.VMEM((width, width), BF16)

    return pl.pallas_call(
        functools.partial(solve_kernel, width, cols),
        out_shape=jax.ShapeDtypeStruct((cols, width), F32),
        in_specs=[pl.BlockSpec(memory_space=pl.ANY), pl.BlockSpec(memory_space=pltpu.VMEM)],
        out_specs=pl.BlockSpec(memory_space=pltpu.VMEM),
        scratch_shapes=[
            piece, piece, piece,
            pltpu.VMEM((2, 256, width), F32),
            pltpu.VMEM((width // 128, 128, 128), F32),
            pltpu.VMEM((1, width), F32),
            pltpu.VMEM((width, 128), F32),
            vec,
            pltpu.VMEM((3 * cols, width), BF16),
            vec, vec, vec, vec, vec,
            col, col, col,
            pltpu.SemaphoreType.DMA((2,)),
            pltpu.SemaphoreType.DMA((width // 128,)),
        ],
        compiler_params=pltpu.CompilerParams(vmem_limit_bytes=60 << 20),
        name="solve",
    )(system, right)


def local(hidden, token_ids, weights):
    live = token_ids[0] != 128004
    masked = jnp.where(live[:, None], hidden[0], 0)
    terms, gram = gather(masked, token_ids.reshape(-1, 128), weights[0], lax.axis_size("tok"))
    system, right = combine(gram, terms)
    return spread(solve(system, right)).T


def solution(mesh):
    return jax.shard_map(
        local,
        mesh=mesh,
        in_specs=(P("expert", "tok", None), P("expert", "tok"), P("expert", None, "tok")),
        out_specs=P(None, "tok"),
        check_vma=False,
    )
```

```python
import functools

import jax
import jax.numpy as jnp
from jax import lax
from jax.experimental import pallas as pl
from jax.experimental.pallas import tpu as pltpu
from jax.sharding import PartitionSpec as P

F32, BF16 = jnp.float32, jnp.bfloat16
MESH = pl.DeviceIdType.MESH
SIDE = 4
INNER_TOL = 4e-3
OUTER_TOL = 2e-5
ROWS = 16


def near(i, step):
    return (i + step + SIDE) % SIDE


def remote(sems, index, source, target, device):
    send, recv = sems
    return pltpu.make_async_remote_copy(
        src_ref=source, dst_ref=target, send_sem=send.at[index], recv_sem=recv.at[index],
        device_id=device, device_id_type=MESH,
    )


def meet(devices):
    barrier = pltpu.get_barrier_semaphore()
    for device in devices:
        pl.semaphore_signal(barrier, inc=1, device_id=device, device_id_type=MESH)
    pl.semaphore_wait(barrier, len(devices))


def gather_kernel(toks, x_hbm, ids_ref, w_ref, terms_ref, gram_ref, X, cat, acc, wt, stat, stats, send, recv, own, stat_send, stat_recv):
    t = lax.axis_index("tok")
    z, x = t // SIDE, t % SIDE
    width, cols = w_ref.shape
    band = width // toks
    half = x_hbm.shape[0] // 2

    def tok(zz, xx):
        return {"tok": zz * SIDE + xx}

    meet([{"tok": (t + k) % toks} for k in range(1, toks)])
    mine = (X.at[z, x], X.at[SIDE + x, z])
    loads = [pltpu.make_async_copy(x_hbm.at[pl.ds(k * half, half)], mine[k], own.at[k]) for k in range(2)]
    for load in loads:
        load.start()

    rc = functools.partial(remote, (send, recv))

    def steps(base, block_of, part, to, here):
        up, down = near(here, 1), near(here, -1)
        first = [
            rc(base, block_of(here), block_of(here), to(up)),
            rc(base + 1, block_of(here), block_of(here), to(down)),
        ]
        onward = [
            rc(base + 2, part(down, 0), part(down, 0), to(up)),
            rc(base + 3, part(up, 1), part(up, 1), to(down)),
        ]
        return first, onward

    a_first, a_onward = steps(
        0, lambda i: X.at[z, i], lambda i, h: X.at[z, i, pl.ds(h * (half // 2), half // 2)], lambda i: tok(z, i), x)
    b_first, b_onward = steps(
        4, lambda i: X.at[SIDE + x, i], lambda i, h: X.at[SIDE + x, i, pl.ds(h * (half // 2), half // 2)], lambda i: tok(i, x), z)

    loads[0].wait()
    for copy in a_first:
        copy.start()
    loads[1].wait()
    for copy in b_first:
        copy.start()

    def clear(i, c):
        at = pl.ds(pl.multiple_of(i * ROWS, ROWS), ROWS)
        acc[at, :] = jnp.zeros((ROWS, width), F32)
        return c

    lax.fori_loop(0, acc.shape[0] // ROWS, clear, 0)

    live = jnp.sum(jnp.where(ids_ref[...] != 128004, 1.0, 0.0), axis=(0, 1), keepdims=True)

    def square(i, total):
        at = pl.ds(pl.multiple_of(i * ROWS, ROWS), ROWS)
        a = X[z, x, at, :].astype(F32)
        b = X[SIDE + x, z, at, :].astype(F32)
        return total + jnp.sum(a * a + b * b, axis=0, keepdims=True)

    stat[:, :width] = lax.fori_loop(0, half // ROWS, square, jnp.zeros((1, width), F32))
    stat[:, width:] = jnp.broadcast_to(live, (1, 128))

    def turn(i, c):
        at = pl.ds(pl.multiple_of(i * 256, 256), 256)
        wt[:, at] = w_ref[at, :].T
        return c

    lax.fori_loop(0, width // 256, turn, 0)

    for first, onward in ((a_first, a_onward), (b_first, b_onward)):
        for got, copy in zip(first, onward):
            got.wait_recv()
            copy.start()

    def share(k):
        return pltpu.make_async_remote_copy(
            src_ref=stat, dst_ref=stats.at[k], send_sem=stat_send.at[k], recv_sem=stat_recv.at[k],
            device_id={"tok": (t + k) % toks}, device_id_type=MESH,
        )

    for copy in a_onward + b_onward:
        copy.wait_recv()

    def group(base, g_of, to, here):
        up, down = near(here, 1), near(here, -1)

        def part(i, h):
            return X.at[g_of(i), pl.ds(2 * h, 2)]

        first = {}
        for h in range(2):
            first["up", h] = rc(base + h, part(here, h), part(here, h), to(up))
            first["down", h] = rc(base + 2 + h, part(here, h), part(here, h), to(down))
        onward = [
            rc(base + 4, part(down, 0), part(down, 0), to(up)),
            rc(base + 5, part(up, 1), part(up, 1), to(down)),
        ]
        return first, onward

    a_near, a_far = group(8, lambda i: i, lambda i: tok(i, x), z)
    b_near, b_far = group(14, lambda i: SIDE + i, lambda i: tok(z, i), x)
    for h in range(2):
        for copies in (a_near, b_near):
            copies["up", h].start()
            copies["down", 1 - h].start()

    lax.fori_loop(1, toks, lambda k, c: (share(k).start(), c)[1], 0)

    arrivals = {}
    for k, (first, far) in enumerate(((a_near, a_far), (b_near, b_far))):
        arrivals[4 + 2 * k] = (first["up", 0], far[0])
        arrivals[5 + 2 * k] = (first["down", 1], far[1])
        arrivals[8 + 2 * k] = (first["up", 1], None)
        arrivals[9 + 2 * k] = (first["down", 0], None)
        arrivals[12 + 2 * k] = (far[0], None)
        arrivals[13 + 2 * k] = (far[1], None)

    pair = 2 * half

    def step(s, c):
        @pl.when(s == 4)
        def _():
            for at in range(4, 8):
                got, copy = arrivals[at]
                got.wait_recv()
                copy.start()

        for at in range(8, 16):
            @pl.when(s == at)
            def _(at=at):
                arrivals[at][0].wait_recv()

        q, m = s // 4, s % 4
        kind, a = m // 2, m % 2
        close = (q % 3 + 1) // 2
        off = close * (3 - 2 * a) + 2 * (q // 3)
        h = a + (q // 2) * (1 - q // 3) * (1 - 2 * a)
        here = z * (1 - kind) + x * kind
        g = kind * SIDE + (here + off) % SIDE
        block = X.at[g, pl.ds(2 * h, 2)]
        rows = block[...].reshape(pair, width)
        upward = jnp.dot(rows, w_ref[...], preferred_element_type=F32).astype(BF16)
        cat[:cols, :] = upward.T
        cat[cols:, :] = block[:, :, pl.ds(pl.multiple_of(t * band, band), band)].reshape(pair, band).T

        def tile(n, c):
            at = pl.ds(pl.multiple_of(n * 512, 512), 512)
            acc[:, at] += jnp.dot(cat[...], block[:, :, at].reshape(pair, 512), preferred_element_type=F32)
            return c

        lax.fori_loop(0, width // 512, tile, 0)
        return c

    lax.fori_loop(0, 16, step, 0)

    lax.fori_loop(1, toks, lambda k, c: (share(k).wait_recv(), c)[1], 0)
    total = stat[...]
    for k in range(1, toks):
        total = total + stats[k]
    inverse = 1.0 / total[:, width : width + 1]
    squares = total[:, :width] * (0.1 * inverse)

    def finish(i, c):
        at = pl.ds(pl.multiple_of(i * ROWS, ROWS), ROWS)
        terms_ref[at, :] = acc[at, :] * (0.9 * inverse) + squares * wt[at, :].astype(F32)
        return c

    lax.fori_loop(0, cols // ROWS, finish, 0)

    def finish_gram(i, c):
        at = pl.ds(pl.multiple_of(i * ROWS, ROWS), ROWS)
        from_rows = pl.ds(pl.multiple_of(cols + i * ROWS, ROWS), ROWS)
        for o in range(toks // 2 + 1):
            block = pl.ds(pl.multiple_of((t + o) % toks * band, band), band)
            gram_ref[at, o * band : (o + 1) * band] = acc[from_rows, block] * inverse
        return c

    lax.fori_loop(0, band // ROWS, finish_gram, 0)

    for copy in a_first + b_first + a_onward + b_onward + list(a_near.values()) + list(b_near.values()) + a_far + b_far:
        copy.wait_send()
    lax.fori_loop(1, toks, lambda k, c: (share(k).wait_send(), c)[1], 0)


def gather(masked, ids, weight, toks):
    count, width = masked.shape
    cols = weight.shape[1]
    band = width // toks
    half = count // 2
    vmem = pl.BlockSpec(memory_space=pltpu.VMEM)
    return pl.pallas_call(
        functools.partial(gather_kernel, toks),
        out_shape=(jax.ShapeDtypeStruct((cols, width), F32), jax.ShapeDtypeStruct((band, (toks // 2 + 1) * band), F32)),
        in_specs=[pl.BlockSpec(memory_space=pl.ANY), vmem, vmem],
        out_specs=(vmem, vmem),
        scratch_shapes=[
            pltpu.VMEM((2 * SIDE, SIDE, half, width), BF16),
            pltpu.VMEM((cols + band, 2 * half), BF16),
            pltpu.VMEM((cols + band, width), F32),
            pltpu.VMEM((cols, width), BF16),
            pltpu.VMEM((1, width + 128), F32),
            pltpu.VMEM((toks, 1, width + 128), F32),
            pltpu.SemaphoreType.DMA((20,)),
            pltpu.SemaphoreType.DMA((20,)),
            pltpu.SemaphoreType.DMA((2,)),
            pltpu.SemaphoreType.DMA((toks,)),
            pltpu.SemaphoreType.DMA((toks,)),
        ],
        compiler_params=pltpu.CompilerParams(collective_id=0, has_side_effects=True, vmem_limit_bytes=60 << 20),
        name="gather",
    )(masked, ids, weight)


def combine_kernel(g_ref, terms_ref, s, b_ref, pg, hg, rg, sg, pt, ht, far, close, send, recv, own):
    e, t = lax.axis_index("expert"), lax.axis_index("tok")
    y, c = e // 2, e % 2
    z, x = t // SIDE, t % SIDE
    rc = functools.partial(remote, (send, recv))

    def tok(zz, xx):
        return {"tok": zz * SIDE + xx}

    def chip(yy):
        return {"expert": yy * 2 + c}

    partner = {"expert": e + 1 - 2 * c}
    up, down, across = near(y, 1), near(y, -1), near(y, 2)
    meet([partner, chip(up), chip(down), chip(across), tok(near(z, 1), x), tok(near(z, -1), x), tok(z, near(x, 1)), tok(z, near(x, -1))])

    swap_g = rc(0, g_ref.at[1 - c], pg, partner)
    swap_t = rc(1, terms_ref.at[:, 1 - c], pt, partner)
    swap_g.start()
    swap_t.start()

    swap_g.wait_recv()
    for k in range(4):
        hg[k] = g_ref[c, k] + pg[k]
    scatter = [rc(1 + k, hg.at[near(y, k)], rg.at[k - 1], chip(near(y, k))) for k in range(1, 4)]
    for copy in scatter:
        copy.start()
    for copy in scatter:
        copy.wait_recv()
    sg[...] = hg[y] + rg[0] + rg[1] + rg[2]
    rows = s.at[z, x, c, y // 2, pl.ds((y % 2) * 16, 16)]
    keep = pltpu.make_async_copy(sg, rows, own.at[0])
    keep.start()
    spread = [rc(4 + k, sg, rows, chip(near(y, k))) for k in range(1, 4)]
    for copy in spread:
        copy.start()

    swap_t.wait_recv()
    for k in range(4):
        ht[k] = terms_ref[k, c] + pt[k]
    first_t = [
        rc(8, ht.at[across, pl.ds(0, 32)], far.at[0], chip(up)),
        rc(9, ht.at[across, pl.ds(32, 32)], far.at[1], chip(down)),
    ]
    for copy in first_t:
        copy.start()

    keep.wait()
    for copy in spread:
        copy.wait_recv()

    def stage(base, block, part, to, here):
        above, below = near(here, 1), near(here, -1)
        first = [rc(base, block(here), block(here), to(above)), rc(base + 1, block(here), block(here), to(below))]
        onward = [rc(base + 2, part(below, 0), part(below, 0), to(above)), rc(base + 3, part(above, 1), part(above, 1), to(below))]
        return first, onward

    a_first, a_onward = stage(10, lambda i: s.at[z, i, c, 0], lambda i, h: s.at[z, i, c, 0, pl.ds(16 * h, 16)], lambda i: tok(z, i), x)
    b_first, b_onward = stage(14, lambda i: s.at[i, x, c, 1], lambda i, h: s.at[i, x, c, 1, pl.ds(16 * h, 16)], lambda i: tok(i, x), z)
    for copy in a_first + b_first:
        copy.start()

    first_t[0].wait_recv()
    ht[up, :32] = ht[up, :32] + far[0]
    first_t[1].wait_recv()
    ht[down, 32:] = ht[down, 32:] + far[1]

    for got, copy in zip(a_first + b_first, a_onward + b_onward):
        got.wait_recv()
        copy.start()

    second_t = [rc(18, ht.at[up], close.at[0], chip(up)), rc(19, ht.at[down], close.at[1], chip(down))]
    for copy in second_t:
        copy.start()

    for copy in a_onward + b_onward:
        copy.wait_recv()

    a_near, a_far = stage(20, lambda i: s.at[i, :, c, 0], lambda i, h: s.at[i, pl.ds(2 * h, 2), c, 0], lambda i: tok(i, x), z)
    b_near, b_far = stage(24, lambda i: s.at[:, i, c, 1], lambda i, h: s.at[pl.ds(2 * h, 2), i, c, 1], lambda i: tok(z, i), x)
    for copy in a_near + b_near:
        copy.start()

    def pair(index, block):
        copy = rc(28 + index, block, block, partner)
        copy.start()
        return copy

    pairs = [pair(0, s.at[z, :, c, 0]), pair(1, s.at[:, x, c, 1])]

    for copy in second_t:
        copy.wait_recv()
    b_ref[...] = ht[y] + close[0] + close[1]

    for got, copy in zip(a_near + b_near, a_far + b_far):
        got.wait_recv()
        copy.start()
    pairs += [pair(2, s.at[near(z, -1), :, c, 0]), pair(3, s.at[near(z, 1), :, c, 0])]
    pairs += [pair(4, s.at[:, near(x, -1), c, 1]), pair(5, s.at[:, near(x, 1), c, 1])]
    for copy in a_far + b_far:
        copy.wait_recv()
    pairs += [pair(6, s.at[near(z, 2), :, c, 0]), pair(7, s.at[:, near(x, 2), c, 1])]
    for copy in pairs:
        copy.wait_recv()
    for copy in [swap_g, swap_t] + scatter + spread + first_t + second_t + a_first + b_first + a_onward + b_onward + a_near + b_near + a_far + b_far + pairs:
        copy.wait_send()


def combine(gram, terms):
    band, keep = gram.shape
    cols, width = terms.shape
    part, share = band // 8, cols // 8
    vmem = pl.BlockSpec(memory_space=pltpu.VMEM)
    system, right = pl.pallas_call(
        combine_kernel,
        out_shape=(
            jax.ShapeDtypeStruct((SIDE, SIDE, 2, 2, 2 * part, keep), F32),
            jax.ShapeDtypeStruct((share, width), F32),
        ),
        in_specs=[vmem, vmem],
        out_specs=(pl.BlockSpec(memory_space=pl.ANY), vmem),
        scratch_shapes=[
            pltpu.VMEM((4, part, keep), F32),
            pltpu.VMEM((4, part, keep), F32),
            pltpu.VMEM((3, part, keep), F32),
            pltpu.VMEM((part, keep), F32),
            pltpu.VMEM((4, share, width), F32),
            pltpu.VMEM((4, share, width), F32),
            pltpu.VMEM((2, share // 2, width), F32),
            pltpu.VMEM((2, share, width), F32),
            pltpu.SemaphoreType.DMA((36,)),
            pltpu.SemaphoreType.DMA((36,)),
            pltpu.SemaphoreType.DMA((1,)),
        ],
        compiler_params=pltpu.CompilerParams(collective_id=1, has_side_effects=True, vmem_limit_bytes=60 << 20),
        name="combine",
    )(gram.reshape(2, 4, part, keep), terms.reshape(4, 2, share, width))
    return system.reshape(width, keep), right


def spread_kernel(a_ref, out, send, recv, own):
    e = lax.axis_index("expert")
    y, c = e // 2, e % 2
    share = a_ref.shape[0]
    rc = functools.partial(remote, (send, recv))

    def chip(yy):
        return {"expert": yy * 2 + c}

    partner = {"expert": e + 1 - 2 * c}
    up, down, across = near(y, 1), near(y, -1), near(y, 2)
    meet([partner, chip(up), chip(down)])
    half = share // 2
    first = [rc(0, a_ref, out.at[y, c], chip(up)), rc(1, a_ref, out.at[y, c], chip(down))]
    pairs = [rc(2, a_ref, out.at[y, c], partner)]
    for copy in first + pairs:
        copy.start()
    keep = pltpu.make_async_copy(a_ref, out.at[y, c], own.at[0])
    keep.start()
    lower, upper = out.at[down, c, pl.ds(0, half)], out.at[up, c, pl.ds(half, half)]
    onward = [rc(3, lower, lower, chip(up)), rc(4, upper, upper, chip(down))]
    for k, (got, copy, at) in enumerate(zip(first, onward, (down, up))):
        got.wait_recv()
        copy.start()
        forward = rc(5 + k, out.at[at, c], out.at[at, c], partner)
        forward.start()
        pairs.append(forward)
    for k, copy in enumerate(onward):
        copy.wait_recv()
        part = out.at[across, c, pl.ds(half * k, half)]
        forward = rc(7 + k, part, part, partner)
        forward.start()
        pairs.append(forward)
    keep.wait()
    for copy in pairs:
        copy.wait_recv()
    for copy in first + onward + pairs:
        copy.wait_send()


def spread(answer):
    share, width = answer.shape
    out = pl.pallas_call(
        spread_kernel,
        out_shape=jax.ShapeDtypeStruct((4, 2, share, width), F32),
        in_specs=[pl.BlockSpec(memory_space=pltpu.VMEM)],
        out_specs=pl.BlockSpec(memory_space=pl.ANY),
        scratch_shapes=[pltpu.SemaphoreType.DMA((9,)), pltpu.SemaphoreType.DMA((9,)), pltpu.SemaphoreType.DMA((1,))],
        compiler_params=pltpu.CompilerParams(collective_id=2, has_side_effects=True),
        name="spread",
    )(answer)
    return out.reshape(8 * share, width)


def solve_kernel(width, cols, t_hbm, b_ref, x_ref, stage, full, sh, sm, sl, dvec, dinv, stack, r, ri, p, d, q, rz, goal, nn, xx, sems):
    blk = width // sems.shape[0]
    loads = [
        pltpu.make_async_copy(t_hbm.at[pl.ds(i * blk, blk)], stage.at[pl.ds(i * blk, blk)], sems.at[i])
        for i in range(width // blk)
    ]
    for load in loads:
        load.start()
    band = 128
    bands = width // band
    eye = lax.broadcasted_iota(jnp.int32, (band, band), 0) == lax.broadcasted_iota(jnp.int32, (band, band), 1)

    def block(i):
        return pl.ds(pl.multiple_of(i * band, band), band)

    for i, load in enumerate(loads):
        load.wait()

        def unfold(t, c):
            for o in range(bands // 2 + 1):
                j = (t + o) % bands
                tile = stage[block(t), o * band : (o + 1) * band]
                full[block(t), block(j)] = tile
                sh[block(t), block(j)] = tile.astype(BF16)
                if o == 0:
                    dvec[:, block(t)] = jnp.sum(jnp.where(eye, tile, 0.0), axis=0, keepdims=True)
                elif o < bands // 2:
                    turned = tile.T
                    full[block(j), block(t)] = turned
                    sh[block(j), block(t)] = turned.astype(BF16)
            return c

        lax.fori_loop(i * blk // band, (i + 1) * blk // band, unfold, 0)
    dinv[...] = 1.0 / dvec[...]

    parts = cols // ROWS

    def at(i, which=0):
        return slice(which * cols + i * ROWS, which * cols + (i + 1) * ROWS)

    def lanes(v):
        return jnp.broadcast_to(v, (ROWS, 128))

    def total(v):
        return jnp.sum(v, axis=1, keepdims=True)

    def halves(i, v):
        high = v.astype(BF16)
        low = (v - high.astype(F32)).astype(BF16)
        stack[at(i), :] = high
        stack[at(i, 1), :] = low
        return high.astype(F32) + low.astype(F32)

    def dot(rows, piece):
        return jnp.dot(stack[:rows, :], piece[...], preferred_element_type=F32)

    for i in range(parts):
        b = b_ref[at(i), :]
        x_ref[at(i), :] = jnp.zeros_like(b)
        r[at(i), :] = b
        nn[at(i), :] = lanes(total(b * b * dinv[...]))
        xx[at(i), :] = jnp.zeros((ROWS, 128), F32)

    def outer(carry):
        k, _ = carry
        for i in range(parts):
            v = r[at(i), :]
            ri[at(i), :] = v
            p[at(i), :] = halves(i, v * dinv[...])
            d[at(i), :] = jnp.zeros_like(v)
            rz[at(i), :] = nn[at(i), :]
            goal[at(i), :] = jnp.maximum(nn[at(i), :] * (INNER_TOL * INNER_TOL), xx[at(i), :] * (0.25 * OUTER_TOL * OUTER_TOL))

        def inner(carry):
            it, _ = carry
            wide = dot(2 * cols, sh)
            q[...] = 0.9 * (wide[:cols] + wide[cols:])

            @pl.when(k >= 2)
            def _():
                q[...] += 0.9 * dot(cols, sm)

            worst = jnp.float32(-1.0)
            for i in range(parts):
                v = p[at(i), :]
                w = q[at(i), :] + 0.1 * dvec[...] * v
                old = rz[at(i), :1]
                pq = total(v * w)
                alpha = jnp.where(pq > 0, old / jnp.where(pq > 0, pq, 1.0), 0.0)
                d[at(i), :] += alpha * v
                res = ri[at(i), :] - alpha * w
                ri[at(i), :] = res
                z = res * dinv[...]
                new = total(res * z)
                beta = jnp.where(old > 0, new / jnp.where(old > 0, old, 1.0), 0.0)
                p[at(i), :] = halves(i, z + beta * v)
                rz[at(i), :] = lanes(new)
                worst = jnp.maximum(worst, jnp.max(new - goal[at(i), :1]))
            return it + 1, worst

        cap = jnp.where(k < 2, 64, 4000)
        lax.while_loop(lambda c: jnp.logical_and(c[0] < cap, c[1] > 0), inner, (jnp.int32(0), jnp.float32(1.0)))

        @pl.when(k == 0)
        def _():
            def rest(j, c):
                at = pl.ds(pl.multiple_of(j * 32, 32), 32)
                left = full[at, :] - sh[at, :].astype(F32)
                mid = left.astype(BF16)
                sm[at, :] = mid
                sl[at, :] = (left - mid.astype(F32)).astype(BF16)
                return c

            lax.fori_loop(0, width // 32, rest, 0)

        for i in range(parts):
            halves(i, d[at(i), :])
            d[at(i), :] += x_ref[at(i), :]

        @pl.when(k < 2)
        def _():
            wide = dot(2 * cols, sm)
            q[...] = ri[...] - 0.9 * (wide[:cols] + wide[cols:])

            @pl.when(k == 1)
            def _():
                for i in range(parts):
                    stack[at(i), :] = d[at(i), :].astype(BF16)
                q[...] -= 0.9 * dot(cols, sl)

        @pl.when(k >= 2)
        def _():
            for i in range(parts):
                v = d[at(i), :]
                stack[at(i, 2), :] = (v - halves(i, v)).astype(BF16)
                q[at(i), :] = b_ref[at(i), :] - 0.1 * dvec[...] * v
            wide = dot(3 * cols, sh)
            q[...] -= 0.9 * (wide[:cols] + wide[cols : 2 * cols] + wide[2 * cols :])
            wide = dot(2 * cols, sm)
            q[...] -= 0.9 * (wide[:cols] + wide[cols:])
            q[...] -= 0.9 * dot(cols, sl)

        worst = jnp.float32(-1.0)
        for i in range(parts):
            new = q[at(i), :]
            size = total(new * new * dinv[...])
            better = size < nn[at(i), :1]
            x = jnp.where(better, d[at(i), :], x_ref[at(i), :])
            x_ref[at(i), :] = x
            r[at(i), :] = jnp.where(better, new, r[at(i), :])
            kept = jnp.where(better, size, nn[at(i), :1])
            nn[at(i), :] = lanes(kept)
            norm = total(x * x * dvec[...])
            xx[at(i), :] = lanes(norm)
            worst = jnp.maximum(worst, jnp.max(kept - (OUTER_TOL * OUTER_TOL) * norm))
        return k + 1, worst

    def more(carry):
        return jnp.logical_or(carry[0] < 2, jnp.logical_and(carry[0] < 20, carry[1] > 0))

    lax.while_loop(more, outer, (jnp.int32(0), jnp.float32(1.0)))


def solve(system, right):
    width, keep = system.shape
    cols = right.shape[0]
    vec = pltpu.VMEM((cols, width), F32)
    col = pltpu.VMEM((cols, 128), F32)
    piece = pltpu.VMEM((width, width), BF16)
    row = pltpu.VMEM((1, width), F32)
    return pl.pallas_call(
        functools.partial(solve_kernel, width, cols),
        out_shape=jax.ShapeDtypeStruct((cols, width), F32),
        in_specs=[pl.BlockSpec(memory_space=pl.ANY), pl.BlockSpec(memory_space=pltpu.VMEM)],
        out_specs=pl.BlockSpec(memory_space=pltpu.VMEM),
        scratch_shapes=[
            pltpu.VMEM((width, keep), F32),
            pltpu.VMEM((width, width), F32),
            piece, piece, piece,
            row, row,
            pltpu.VMEM((3 * cols, width), BF16),
            vec, vec, vec, vec, vec,
            col, col, col, col,
            pltpu.SemaphoreType.DMA((8,)),
        ],
        compiler_params=pltpu.CompilerParams(vmem_limit_bytes=60 << 20),
        name="solve",
    )(system, right)


def local(hidden, token_ids, weights):
    live = token_ids[0] != 128004
    masked = jnp.where(live[:, None], hidden[0], 0)
    terms, gram = gather(masked, token_ids.reshape(-1, 128), weights[0], lax.axis_size("tok"))
    system, right = combine(gram, terms)
    return spread(solve(system, right)).T


def solution(mesh):
    return jax.shard_map(
        local,
        mesh=mesh,
        in_specs=(P("expert", "tok", None), P("expert", "tok"), P("expert", None, "tok")),
        out_specs=P(None, "tok"),
        check_vma=False,
    )
```

```python
import functools

import jax
import jax.numpy as jnp
from jax import lax
from jax.experimental import pallas as pl
from jax.experimental.pallas import tpu as pltpu
from jax.sharding import PartitionSpec as P

F32, BF16 = jnp.float32, jnp.bfloat16
MESH = pl.DeviceIdType.MESH
SIDE = 4
INNER_TOL = 4e-3
OUTER_TOL = 2e-5
ROWS = 16


def near(i, step):
    return (i + step + SIDE) % SIDE


def remote(sems, index, source, target, device):
    send, recv = sems
    return pltpu.make_async_remote_copy(
        src_ref=source, dst_ref=target, send_sem=send.at[index], recv_sem=recv.at[index],
        device_id=device, device_id_type=MESH,
    )


def meet(devices):
    barrier = pltpu.get_barrier_semaphore()
    for device in devices:
        pl.semaphore_signal(barrier, inc=1, device_id=device, device_id_type=MESH)
    pl.semaphore_wait(barrier, len(devices))


def build_kernel(toks, x_hbm, ids_ref, w_ref, s, b_ref, X, cat, acc, wt, stat, stats, gr, pg, hg, rg, sg, pt, ht, far, close,
                 send, recv, own, stat_send, stat_recv):
    e, t = lax.axis_index("expert"), lax.axis_index("tok")
    y, c = e // 2, e % 2
    z, x = t // SIDE, t % SIDE
    width, cols = w_ref.shape
    band = width // toks
    half = x_hbm.shape[0] // 2
    count = iter(range(send.shape[0]))

    def rc(source, target, device):
        return remote((send, recv), next(count), source, target, device)

    def tok(zz, xx):
        return {"tok": zz * SIDE + xx}

    def chip(yy):
        return {"expert": yy * 2 + c}

    partner = {"expert": e + 1 - 2 * c}
    up, down, across = near(y, 1), near(y, -1), near(y, 2)
    meet([{"tok": (t + k) % toks} for k in range(1, toks)] + [partner, chip(up), chip(down), chip(across)])
    mine = (X.at[z, x], X.at[SIDE + x, z])
    loads = [pltpu.make_async_copy(x_hbm.at[pl.ds(k * half, half)], mine[k], own.at[k]) for k in range(2)]
    for load in loads:
        load.start()

    def stage(block, part, to, here):
        above, below = near(here, 1), near(here, -1)
        first = [rc(block(here), block(here), to(above)), rc(block(here), block(here), to(below))]
        onward = [rc(part(below, 0), part(below, 0), to(above)), rc(part(above, 1), part(above, 1), to(below))]
        return first, onward

    quarter = half // 2
    a_first, a_onward = stage(
        lambda i: X.at[z, i], lambda i, h: X.at[z, i, pl.ds(h * quarter, quarter)], lambda i: tok(z, i), x)
    b_first, b_onward = stage(
        lambda i: X.at[SIDE + x, i], lambda i, h: X.at[SIDE + x, i, pl.ds(h * quarter, quarter)], lambda i: tok(i, x), z)

    loads[0].wait()
    for copy in a_first:
        copy.start()
    loads[1].wait()
    for copy in b_first:
        copy.start()

    def clear(i, k):
        at = pl.ds(pl.multiple_of(i * ROWS, ROWS), ROWS)
        acc[at, :] = jnp.zeros((ROWS, width), F32)
        return k

    lax.fori_loop(0, acc.shape[0] // ROWS, clear, 0)

    live = jnp.sum(jnp.where(ids_ref[...] != 128004, 1.0, 0.0), axis=(0, 1), keepdims=True)

    def square(i, total):
        at = pl.ds(pl.multiple_of(i * ROWS, ROWS), ROWS)
        a = X[z, x, at, :].astype(F32)
        b = X[SIDE + x, z, at, :].astype(F32)
        return total + jnp.sum(a * a + b * b, axis=0, keepdims=True)

    stat[:, :width] = lax.fori_loop(0, half // ROWS, square, jnp.zeros((1, width), F32))
    stat[:, width:] = jnp.broadcast_to(live, (1, 128))

    def turn(i, k):
        at = pl.ds(pl.multiple_of(i * 256, 256), 256)
        wt[:, at] = w_ref[at, :].T
        return k

    lax.fori_loop(0, width // 256, turn, 0)

    for got, copy in zip(a_first + b_first, a_onward + b_onward):
        got.wait_recv()
        copy.start()

    def share(k):
        return pltpu.make_async_remote_copy(
            src_ref=stat, dst_ref=stats.at[k], send_sem=stat_send.at[k], recv_sem=stat_recv.at[k],
            device_id={"tok": (t + k) % toks}, device_id_type=MESH,
        )

    for copy in a_onward + b_onward:
        copy.wait_recv()

    def group(g_of, to, here):
        above, below = near(here, 1), near(here, -1)
        first, onward = [], []
        for h in range(2):
            part = X.at[g_of(here), pl.ds(2 * h, 2)]
            first.append([rc(part, part, to(above)), rc(part, part, to(below))])
            lower, upper = X.at[g_of(below), 2 * h], X.at[g_of(above), 2 * h + 1]
            onward.append([rc(lower, lower, to(above)), rc(upper, upper, to(below))])
        return first, onward

    a_near, a_far = group(lambda i: i, lambda i: tok(i, x), z)
    b_near, b_far = group(lambda i: SIDE + i, lambda i: tok(z, i), x)
    for h in range(2):
        for copy in a_near[h] + b_near[h]:
            copy.start()

    lax.fori_loop(1, toks, lambda k, v: (share(k).start(), v)[1], 0)

    pair = 2 * half

    def blocks(kind, off, h):
        here = z * (1 - kind) + x * kind
        return X.at[kind * SIDE + (here + off) % SIDE, pl.ds(2 * h, 2)]

    def put_up(block):
        rows = block[...].reshape(pair, width)
        cat[:cols, :] = jnp.dot(rows, w_ref[...], preferred_element_type=F32).astype(BF16).T

    def put_own(block):
        cat[cols:, :] = block[:, :, pl.ds(pl.multiple_of(t * band, band), band)].reshape(pair, band).T

    def add(block, low, high):
        def tile(n, k):
            at = pl.ds(pl.multiple_of(n * 512, 512), 512)
            acc[low:high, at] += jnp.dot(cat[low:high, :], block[:, :, at].reshape(pair, 512), preferred_element_type=F32)
            return k

        lax.fori_loop(0, width // 512, tile, 0)

    def both(block):
        put_up(block)
        put_own(block)
        add(block, 0, cols + band)

    def step(i, k):
        for h in range(2):
            @pl.when(i == 4 + 4 * h)
            def _(h=h):
                for got, copy in zip(a_near[h] + b_near[h], a_far[h] + b_far[h]):
                    got.wait_recv()
                    copy.start()

        q, m = i // 4, i % 4
        a = m % 2
        close_by = (q + 1) // 2
        both(blocks(m // 2, close_by * (3 - 2 * a), (1 - close_by) * a + close_by * (q // 2)))
        return k

    lax.fori_loop(0, 12, step, 0)

    def last(i, k):
        for kind, copies in enumerate((a_far[0], b_far[0])):
            @pl.when(i == kind)
            def _(copies=copies):
                for copy in copies:
                    copy.wait_recv()

        both(blocks(i, 2, 0))
        return k

    lax.fori_loop(0, 2, last, 0)

    lax.fori_loop(1, toks, lambda k, v: (share(k).wait_recv(), v)[1], 0)
    total = stat[...]
    for k in range(1, toks):
        total = total + stats[k]
    inverse = 1.0 / total[:, width : width + 1]
    squares = total[:, :width] * (0.1 * inverse)

    for kind, copies in enumerate((a_far[1], b_far[1])):
        for copy in copies:
            copy.wait_recv()
        put_own(blocks(kind, 2, 1))
        add(blocks(kind, 2, 1), cols, cols + band)

    def pack(i, k):
        at = pl.ds(pl.multiple_of(cols + i * ROWS, ROWS), ROWS)
        for o in range(toks // 2 + 1):
            block = pl.ds(pl.multiple_of((t + o) % toks * band, band), band)
            gr[i // 4, i % 4, :, o * band : (o + 1) * band] = acc[at, block] * inverse
        return k

    lax.fori_loop(0, band // ROWS, pack, 0)

    swap_g = rc(gr.at[1 - c], pg, partner)
    swap_g.start()

    def finish_up(kind):
        put_up(blocks(kind, 2, 1))
        add(blocks(kind, 2, 1), 0, cols)

    finish_up(0)

    swap_g.wait_recv()
    for k in range(4):
        hg[k] = gr[c, k] + pg[k]
    scatter = [rc(hg.at[near(y, k)], rg.at[k - 1], chip(near(y, k))) for k in range(1, 4)]
    for copy in scatter:
        copy.start()

    finish_up(1)

    for copy in scatter:
        copy.wait_recv()
    sg[...] = hg[y] + rg[0] + rg[1] + rg[2]
    rows = s.at[z, x, c, y // 2, pl.ds((y % 2) * ROWS, ROWS)]
    keep = pltpu.make_async_copy(sg, rows, own.at[0])
    keep.start()
    spread_g = [rc(sg, rows, chip(near(y, k))) for k in range(1, 4)]
    for copy in spread_g:
        copy.start()

    share_rows = cols // 8

    def rows_of(yy, cc):
        return pl.ds(pl.multiple_of(yy * 2 * share_rows + cc * share_rows, share_rows), share_rows)

    def finish(cc):
        def tile(i, k):
            per = share_rows // ROWS
            at = pl.ds(pl.multiple_of(i // per * 2 * share_rows + cc * share_rows + i % per * ROWS, ROWS), ROWS)
            acc[at, :] = acc[at, :] * (0.9 * inverse) + squares * wt[at, :].astype(F32)
            return k

        lax.fori_loop(0, 4 * share_rows // ROWS, tile, 0)

    finish(1 - c)
    swap_t = [rc(acc.at[rows_of(k, 1 - c)], pt.at[k], partner) for k in range(4)]
    for copy in swap_t:
        copy.start()

    keep.wait()
    for copy in spread_g:
        copy.wait_recv()

    a_first_g, a_onward_g = stage(lambda i: s.at[z, i, c, 0], lambda i, h: s.at[z, i, c, 0, pl.ds(16 * h, 16)], lambda i: tok(z, i), x)
    b_first_g, b_onward_g = stage(lambda i: s.at[i, x, c, 1], lambda i, h: s.at[i, x, c, 1, pl.ds(16 * h, 16)], lambda i: tok(i, x), z)
    for copy in a_first_g + b_first_g:
        copy.start()

    finish(c)

    for k in range(4):
        swap_t[k].wait_recv()
        ht[k] = acc[rows_of(k, c), :] + pt[k]
    mid = share_rows // 2
    first_t = [
        rc(ht.at[across, pl.ds(0, mid)], far.at[0], chip(up)),
        rc(ht.at[across, pl.ds(mid, mid)], far.at[1], chip(down)),
    ]
    for copy in first_t:
        copy.start()

    for got, copy in zip(a_first_g + b_first_g, a_onward_g + b_onward_g):
        got.wait_recv()
        copy.start()
    for copy in a_onward_g + b_onward_g:
        copy.wait_recv()

    a_near_g, a_far_g = stage(lambda i: s.at[i, :, c, 0], lambda i, h: s.at[i, pl.ds(2 * h, 2), c, 0], lambda i: tok(i, x), z)
    b_near_g, b_far_g = stage(lambda i: s.at[:, i, c, 1], lambda i, h: s.at[pl.ds(2 * h, 2), i, c, 1], lambda i: tok(z, i), x)
    for copy in a_near_g + b_near_g:
        copy.start()

    def hand(block):
        copy = rc(block, block, partner)
        copy.start()
        return copy

    hands = [hand(s.at[z, :, c, 0]), hand(s.at[:, x, c, 1])]

    first_t[0].wait_recv()
    ht[up, :mid] = ht[up, :mid] + far[0]
    first_t[1].wait_recv()
    ht[down, mid:] = ht[down, mid:] + far[1]
    second_t = [rc(ht.at[up], close.at[0], chip(up)), rc(ht.at[down], close.at[1], chip(down))]
    for copy in second_t:
        copy.start()

    for got, copy in zip(a_near_g + b_near_g, a_far_g + b_far_g):
        got.wait_recv()
        copy.start()
    hands += [hand(s.at[near(z, -1), :, c, 0]), hand(s.at[near(z, 1), :, c, 0])]
    hands += [hand(s.at[:, near(x, -1), c, 1]), hand(s.at[:, near(x, 1), c, 1])]

    for copy in second_t:
        copy.wait_recv()
    b_ref[...] = ht[y] + close[0] + close[1]

    for copy in a_far_g + b_far_g:
        copy.wait_recv()
    hands += [hand(s.at[near(z, 2), :, c, 0]), hand(s.at[:, near(x, 2), c, 1])]
    for copy in hands:
        copy.wait_recv()

    sent = a_first + b_first + a_onward + b_onward
    for h in range(2):
        sent += a_near[h] + b_near[h] + a_far[h] + b_far[h]
    sent += [swap_g] + scatter + spread_g + swap_t + first_t + second_t
    sent += a_first_g + b_first_g + a_onward_g + b_onward_g + a_near_g + b_near_g + a_far_g + b_far_g + hands
    for copy in sent:
        copy.wait_send()
    lax.fori_loop(1, toks, lambda k, v: (share(k).wait_send(), v)[1], 0)


def build(masked, ids, weight, toks):
    count, width = masked.shape
    cols = weight.shape[1]
    band = width // toks
    half = count // 2
    keep = (toks // 2 + 1) * band
    part, share = band // 8, cols // 8
    copies = 67
    vmem = pl.BlockSpec(memory_space=pltpu.VMEM)
    system, right = pl.pallas_call(
        functools.partial(build_kernel, toks),
        out_shape=(
            jax.ShapeDtypeStruct((SIDE, SIDE, 2, 2, 2 * part, keep), F32),
            jax.ShapeDtypeStruct((share, width), F32),
        ),
        in_specs=[pl.BlockSpec(memory_space=pl.ANY), vmem, vmem],
        out_specs=(pl.BlockSpec(memory_space=pl.ANY), vmem),
        scratch_shapes=[
            pltpu.VMEM((2 * SIDE, SIDE, half, width), BF16),
            pltpu.VMEM((cols + band, 2 * half), BF16),
            pltpu.VMEM((cols + band, width), F32),
            pltpu.VMEM((cols, width), BF16),
            pltpu.VMEM((1, width + 128), F32),
            pltpu.VMEM((toks, 1, width + 128), F32),
            pltpu.VMEM((2, 4, part, keep), F32),
            pltpu.VMEM((4, part, keep), F32),
            pltpu.VMEM((4, part, keep), F32),
            pltpu.VMEM((3, part, keep), F32),
            pltpu.VMEM((part, keep), F32),
            pltpu.VMEM((4, share, width), F32),
            pltpu.VMEM((4, share, width), F32),
            pltpu.VMEM((2, share // 2, width), F32),
            pltpu.VMEM((2, share, width), F32),
            pltpu.SemaphoreType.DMA((copies,)),
            pltpu.SemaphoreType.DMA((copies,)),
            pltpu.SemaphoreType.DMA((2,)),
            pltpu.SemaphoreType.DMA((toks,)),
            pltpu.SemaphoreType.DMA((toks,)),
        ],
        compiler_params=pltpu.CompilerParams(collective_id=0, has_side_effects=True, vmem_limit_bytes=60 << 20),
        name="build",
    )(masked, ids, weight)
    return system.reshape(width, keep), right


def spread_kernel(a_ref, out, send, recv, own):
    e = lax.axis_index("expert")
    y, c = e // 2, e % 2
    share = a_ref.shape[0]
    rc = functools.partial(remote, (send, recv))

    def chip(yy):
        return {"expert": yy * 2 + c}

    partner = {"expert": e + 1 - 2 * c}
    up, down, across = near(y, 1), near(y, -1), near(y, 2)
    meet([partner, chip(up), chip(down)])
    half = share // 2
    first = [rc(0, a_ref, out.at[y, c], chip(up)), rc(1, a_ref, out.at[y, c], chip(down))]
    pairs = [rc(2, a_ref, out.at[y, c], partner)]
    for copy in first + pairs:
        copy.start()
    keep = pltpu.make_async_copy(a_ref, out.at[y, c], own.at[0])
    keep.start()
    lower, upper = out.at[down, c, pl.ds(0, half)], out.at[up, c, pl.ds(half, half)]
    onward = [rc(3, lower, lower, chip(up)), rc(4, upper, upper, chip(down))]
    for k, (got, copy, at) in enumerate(zip(first, onward, (down, up))):
        got.wait_recv()
        copy.start()
        forward = rc(5 + k, out.at[at, c], out.at[at, c], partner)
        forward.start()
        pairs.append(forward)
    for k, copy in enumerate(onward):
        copy.wait_recv()
        part = out.at[across, c, pl.ds(half * k, half)]
        forward = rc(7 + k, part, part, partner)
        forward.start()
        pairs.append(forward)
    keep.wait()
    for copy in pairs:
        copy.wait_recv()
    for copy in first + onward + pairs:
        copy.wait_send()


def spread(answer):
    share, width = answer.shape
    out = pl.pallas_call(
        spread_kernel,
        out_shape=jax.ShapeDtypeStruct((4, 2, share, width), F32),
        in_specs=[pl.BlockSpec(memory_space=pltpu.VMEM)],
        out_specs=pl.BlockSpec(memory_space=pl.ANY),
        scratch_shapes=[pltpu.SemaphoreType.DMA((9,)), pltpu.SemaphoreType.DMA((9,)), pltpu.SemaphoreType.DMA((1,))],
        compiler_params=pltpu.CompilerParams(collective_id=1, has_side_effects=True),
        name="spread",
    )(answer)
    return out.reshape(8 * share, width)


def solve_kernel(width, cols, t_hbm, b_ref, x_ref, stage, full, sh, sm, sl, dvec, dinv, stack, r, ri, p, d, q, rz, goal, nn, xx, sems):
    blk = width // sems.shape[0]
    loads = [
        pltpu.make_async_copy(t_hbm.at[pl.ds(i * blk, blk)], stage.at[pl.ds(i * blk, blk)], sems.at[i])
        for i in range(width // blk)
    ]
    for load in loads:
        load.start()
    band = 128
    bands = width // band
    eye = lax.broadcasted_iota(jnp.int32, (band, band), 0) == lax.broadcasted_iota(jnp.int32, (band, band), 1)

    def block(i):
        return pl.ds(pl.multiple_of(i * band, band), band)

    for i, load in enumerate(loads):
        load.wait()

        def unfold(t, c):
            for o in range(bands // 2 + 1):
                j = (t + o) % bands
                tile = stage[block(t), o * band : (o + 1) * band]
                full[block(t), block(j)] = tile
                sh[block(t), block(j)] = tile.astype(BF16)
                if o == 0:
                    dvec[:, block(t)] = jnp.sum(jnp.where(eye, tile, 0.0), axis=0, keepdims=True)
                elif o < bands // 2:
                    turned = tile.T
                    full[block(j), block(t)] = turned
                    sh[block(j), block(t)] = turned.astype(BF16)
            return c

        lax.fori_loop(i * blk // band, (i + 1) * blk // band, unfold, 0)
    dinv[...] = 1.0 / dvec[...]

    parts = cols // ROWS

    def at(i, which=0):
        return slice(which * cols + i * ROWS, which * cols + (i + 1) * ROWS)

    def lanes(v):
        return jnp.broadcast_to(v, (ROWS, 128))

    def total(v):
        return jnp.sum(v, axis=1, keepdims=True)

    def halves(i, v):
        high = v.astype(BF16)
        low = (v - high.astype(F32)).astype(BF16)
        stack[at(i), :] = high
        stack[at(i, 1), :] = low
        return high.astype(F32) + low.astype(F32)

    def dot(rows, piece):
        return jnp.dot(stack[:rows, :], piece[...], preferred_element_type=F32)

    for i in range(parts):
        b = b_ref[at(i), :]
        x_ref[at(i), :] = jnp.zeros_like(b)
        r[at(i), :] = b
        nn[at(i), :] = lanes(total(b * b * dinv[...]))
        xx[at(i), :] = jnp.zeros((ROWS, 128), F32)

    def outer(carry):
        k, _ = carry
        for i in range(parts):
            v = r[at(i), :]
            ri[at(i), :] = v
            p[at(i), :] = halves(i, v * dinv[...])
            d[at(i), :] = jnp.zeros_like(v)
            rz[at(i), :] = nn[at(i), :]
            goal[at(i), :] = jnp.maximum(nn[at(i), :] * (INNER_TOL * INNER_TOL), xx[at(i), :] * (0.25 * OUTER_TOL * OUTER_TOL))

        def inner(carry):
            it, _ = carry
            wide = dot(2 * cols, sh)
            q[...] = 0.9 * (wide[:cols] + wide[cols:])

            @pl.when(k >= 2)
            def _():
                q[...] += 0.9 * dot(cols, sm)

            worst = jnp.float32(-1.0)
            for i in range(parts):
                v = p[at(i), :]
                w = q[at(i), :] + 0.1 * dvec[...] * v
                old = rz[at(i), :1]
                pq = total(v * w)
                alpha = jnp.where(pq > 0, old / jnp.where(pq > 0, pq, 1.0), 0.0)
                d[at(i), :] += alpha * v
                res = ri[at(i), :] - alpha * w
                ri[at(i), :] = res
                z = res * dinv[...]
                new = total(res * z)
                beta = jnp.where(old > 0, new / jnp.where(old > 0, old, 1.0), 0.0)
                p[at(i), :] = halves(i, z + beta * v)
                rz[at(i), :] = lanes(new)
                worst = jnp.maximum(worst, jnp.max(new - goal[at(i), :1]))
            return it + 1, worst

        cap = jnp.where(k < 2, 64, 4000)
        lax.while_loop(lambda c: jnp.logical_and(c[0] < cap, c[1] > 0), inner, (jnp.int32(0), jnp.float32(1.0)))

        @pl.when(k == 0)
        def _():
            def rest(j, c):
                at = pl.ds(pl.multiple_of(j * 32, 32), 32)
                left = full[at, :] - sh[at, :].astype(F32)
                mid = left.astype(BF16)
                sm[at, :] = mid
                sl[at, :] = (left - mid.astype(F32)).astype(BF16)
                return c

            lax.fori_loop(0, width // 32, rest, 0)

        for i in range(parts):
            halves(i, d[at(i), :])
            d[at(i), :] += x_ref[at(i), :]

        @pl.when(k < 2)
        def _():
            wide = dot(2 * cols, sm)
            q[...] = ri[...] - 0.9 * (wide[:cols] + wide[cols:])

            @pl.when(k == 1)
            def _():
                for i in range(parts):
                    stack[at(i), :] = d[at(i), :].astype(BF16)
                q[...] -= 0.9 * dot(cols, sl)

        @pl.when(k >= 2)
        def _():
            for i in range(parts):
                v = d[at(i), :]
                stack[at(i, 2), :] = (v - halves(i, v)).astype(BF16)
                q[at(i), :] = b_ref[at(i), :] - 0.1 * dvec[...] * v
            wide = dot(3 * cols, sh)
            q[...] -= 0.9 * (wide[:cols] + wide[cols : 2 * cols] + wide[2 * cols :])
            wide = dot(2 * cols, sm)
            q[...] -= 0.9 * (wide[:cols] + wide[cols:])
            q[...] -= 0.9 * dot(cols, sl)

        worst = jnp.float32(-1.0)
        for i in range(parts):
            new = q[at(i), :]
            size = total(new * new * dinv[...])
            better = size < nn[at(i), :1]
            x = jnp.where(better, d[at(i), :], x_ref[at(i), :])
            x_ref[at(i), :] = x
            r[at(i), :] = jnp.where(better, new, r[at(i), :])
            kept = jnp.where(better, size, nn[at(i), :1])
            nn[at(i), :] = lanes(kept)
            norm = total(x * x * dvec[...])
            xx[at(i), :] = lanes(norm)
            worst = jnp.maximum(worst, jnp.max(kept - (OUTER_TOL * OUTER_TOL) * norm))
        return k + 1, worst

    def more(carry):
        return jnp.logical_or(carry[0] < 2, jnp.logical_and(carry[0] < 20, carry[1] > 0))

    lax.while_loop(more, outer, (jnp.int32(0), jnp.float32(1.0)))


def solve(system, right):
    width, keep = system.shape
    cols = right.shape[0]
    vec = pltpu.VMEM((cols, width), F32)
    col = pltpu.VMEM((cols, 128), F32)
    piece = pltpu.VMEM((width, width), BF16)
    row = pltpu.VMEM((1, width), F32)
    return pl.pallas_call(
        functools.partial(solve_kernel, width, cols),
        out_shape=jax.ShapeDtypeStruct((cols, width), F32),
        in_specs=[pl.BlockSpec(memory_space=pl.ANY), pl.BlockSpec(memory_space=pltpu.VMEM)],
        out_specs=pl.BlockSpec(memory_space=pltpu.VMEM),
        scratch_shapes=[
            pltpu.VMEM((width, keep), F32),
            pltpu.VMEM((width, width), F32),
            piece, piece, piece,
            row, row,
            pltpu.VMEM((3 * cols, width), BF16),
            vec, vec, vec, vec, vec,
            col, col, col, col,
            pltpu.SemaphoreType.DMA((8,)),
        ],
        compiler_params=pltpu.CompilerParams(vmem_limit_bytes=60 << 20),
        name="solve",
    )(system, right)


def local(hidden, token_ids, weights):
    live = token_ids[0] != 128004
    masked = jnp.where(live[:, None], hidden[0], 0)
    system, right = build(masked, token_ids.reshape(-1, 128), weights[0], lax.axis_size("tok"))
    return spread(solve(system, right)).T


def solution(mesh):
    return jax.shard_map(
        local,
        mesh=mesh,
        in_specs=(P("expert", "tok", None), P("expert", "tok"), P("expert", None, "tok")),
        out_specs=P(None, "tok"),
        check_vma=False,
    )
```

```python
import functools

import jax
import jax.numpy as jnp
from jax import lax
from jax.experimental import pallas as pl
from jax.experimental.pallas import tpu as pltpu
from jax.sharding import PartitionSpec as P

F32, BF16 = jnp.float32, jnp.bfloat16
MESH = pl.DeviceIdType.MESH
SIDE = 4
INNER_TOL = 8e-3
OUTER_TOL = 5e-5
ROWS = 16


def near(i, step):
    return (i + step + SIDE) % SIDE


def remote(sems, index, source, target, device):
    send, recv = sems
    return pltpu.make_async_remote_copy(
        src_ref=source, dst_ref=target, send_sem=send.at[index], recv_sem=recv.at[index],
        device_id=device, device_id_type=MESH,
    )


def meet(devices):
    barrier = pltpu.get_barrier_semaphore()
    for device in devices:
        pl.semaphore_signal(barrier, inc=1, device_id=device, device_id_type=MESH)
    pl.semaphore_wait(barrier, len(devices))


def build_kernel(toks, x_hbm, ids_ref, w_ref, s, b_ref, raw, X, cat, acc, wt, stat, stats, gr, pg, hg, rg, sg, pt, ht, far, close,
                 send, recv, own, stat_send, stat_recv):
    e, t = lax.axis_index("expert"), lax.axis_index("tok")
    y, c = e // 2, e % 2
    z, x = t // SIDE, t % SIDE
    width, cols = w_ref.shape
    band = width // toks
    half = x_hbm.shape[0] // 2
    count = iter(range(send.shape[0]))

    def rc(source, target, device):
        return remote((send, recv), next(count), source, target, device)

    def tok(zz, xx):
        return {"tok": zz * SIDE + xx}

    def chip(yy):
        return {"expert": yy * 2 + c}

    partner = {"expert": e + 1 - 2 * c}
    up, down, across = near(y, 1), near(y, -1), near(y, 2)
    loads = [pltpu.make_async_copy(x_hbm.at[pl.ds(k * half, half)], raw.at[k], own.at[k]) for k in range(2)]
    for load in loads:
        load.start()
    eye = lax.broadcasted_iota(jnp.int32, (half, half), 0) == lax.broadcasted_iota(jnp.int32, (half, half), 1)
    alive = [
        jnp.sum(jnp.where(eye, jnp.where(ids_ref[k : k + 1, :] != 128004, 1.0, 0.0), 0.0), axis=1, keepdims=True)
        for k in range(2)
    ]
    meet([{"tok": (t + k) % toks} for k in range(1, toks)] + [partner, chip(up), chip(down), chip(across)])
    mine = (X.at[z, x], X.at[SIDE + x, z])

    def stage(block, part, to, here):
        above, below = near(here, 1), near(here, -1)
        first = [rc(block(here), block(here), to(above)), rc(block(here), block(here), to(below))]
        onward = [rc(part(below, 0), part(below, 0), to(above)), rc(part(above, 1), part(above, 1), to(below))]
        return first, onward

    quarter = half // 2
    a_first, a_onward = stage(
        lambda i: X.at[z, i], lambda i, h: X.at[z, i, pl.ds(h * quarter, quarter)], lambda i: tok(z, i), x)
    b_first, b_onward = stage(
        lambda i: X.at[SIDE + x, i], lambda i, h: X.at[SIDE + x, i, pl.ds(h * quarter, quarter)], lambda i: tok(i, x), z)

    for k in range(2):
        loads[k].wait()
        for i in range(0, half, 2 * ROWS):
            keep = alive[k][i : i + 2 * ROWS] > 0
            mine[k][i : i + 2 * ROWS, :] = jnp.where(keep, raw[k, i : i + 2 * ROWS, :].astype(F32), 0.0).astype(BF16)
    for copy in a_first + b_first:
        copy.start()

    def clear(i, k):
        at = pl.ds(pl.multiple_of(i * ROWS, ROWS), ROWS)
        acc[at, :] = jnp.zeros((ROWS, width), F32)
        return k

    lax.fori_loop(0, acc.shape[0] // ROWS, clear, 0)

    live = jnp.sum(jnp.where(ids_ref[...] != 128004, 1.0, 0.0), axis=(0, 1), keepdims=True)

    def square(i, total):
        at = pl.ds(pl.multiple_of(i * ROWS, ROWS), ROWS)
        a = X[z, x, at, :].astype(F32)
        b = X[SIDE + x, z, at, :].astype(F32)
        return total + jnp.sum(a * a + b * b, axis=0, keepdims=True)

    stat[:, :width] = lax.fori_loop(0, half // ROWS, square, jnp.zeros((1, width), F32))
    stat[:, width:] = jnp.broadcast_to(live, (1, 128))

    def turn(i, k):
        at = pl.ds(pl.multiple_of(i * 256, 256), 256)
        wt[:, at] = w_ref[at, :].T
        return k

    lax.fori_loop(0, width // 256, turn, 0)

    for got, copy in zip(a_first + b_first, a_onward + b_onward):
        got.wait_recv()
        copy.start()

    def share(k):
        return pltpu.make_async_remote_copy(
            src_ref=stat, dst_ref=stats.at[k], send_sem=stat_send.at[k], recv_sem=stat_recv.at[k],
            device_id={"tok": (t + k) % toks}, device_id_type=MESH,
        )

    for copy in a_onward + b_onward:
        copy.wait_recv()

    def group(g_of, to, here):
        above, below = near(here, 1), near(here, -1)
        first, onward = [], []
        for h in range(2):
            part = X.at[g_of(here), pl.ds(2 * h, 2)]
            first.append([rc(part, part, to(above)), rc(part, part, to(below))])
            lower, upper = X.at[g_of(below), 2 * h], X.at[g_of(above), 2 * h + 1]
            onward.append([rc(lower, lower, to(above)), rc(upper, upper, to(below))])
        return first, onward

    a_near, a_far = group(lambda i: i, lambda i: tok(i, x), z)
    b_near, b_far = group(lambda i: SIDE + i, lambda i: tok(z, i), x)
    for h in range(2):
        for copy in a_near[h] + b_near[h]:
            copy.start()

    lax.fori_loop(1, toks, lambda k, v: (share(k).start(), v)[1], 0)

    pair = 2 * half

    def blocks(kind, off, h):
        here = z * (1 - kind) + x * kind
        return X.at[kind * SIDE + (here + off) % SIDE, pl.ds(2 * h, 2)]

    def put_up(block):
        rows = block[...].reshape(pair, width)
        cat[:cols, :] = jnp.dot(rows, w_ref[...], preferred_element_type=F32).astype(BF16).T

    def put_own(block):
        cat[cols:, :] = block[:, :, pl.ds(pl.multiple_of(t * band, band), band)].reshape(pair, band).T

    def add(block, low, high):
        def tile(n, k):
            at = pl.ds(pl.multiple_of(n * 512, 512), 512)
            acc[low:high, at] += jnp.dot(cat[low:high, :], block[:, :, at].reshape(pair, 512), preferred_element_type=F32)
            return k

        lax.fori_loop(0, width // 512, tile, 0)

    def both(block):
        put_up(block)
        put_own(block)
        add(block, 0, cols + band)

    def step(i, k):
        for h in range(2):
            @pl.when(i == 4 + 4 * h)
            def _(h=h):
                for got, copy in zip(a_near[h] + b_near[h], a_far[h] + b_far[h]):
                    got.wait_recv()
                    copy.start()

        q, m = i // 4, i % 4
        a = m % 2
        close_by = (q + 1) // 2
        both(blocks(m // 2, close_by * (3 - 2 * a), (1 - close_by) * a + close_by * (q // 2)))
        return k

    lax.fori_loop(0, 12, step, 0)

    def last(i, k):
        for kind, copies in enumerate((a_far[0], b_far[0])):
            @pl.when(i == kind)
            def _(copies=copies):
                for copy in copies:
                    copy.wait_recv()

        both(blocks(i, 2, 0))
        return k

    lax.fori_loop(0, 2, last, 0)

    lax.fori_loop(1, toks, lambda k, v: (share(k).wait_recv(), v)[1], 0)
    total = stat[...]
    for k in range(1, toks):
        total = total + stats[k]
    inverse = 1.0 / total[:, width : width + 1]
    squares = total[:, :width] * (0.1 * inverse)

    for kind, copies in enumerate((a_far[1], b_far[1])):
        for copy in copies:
            copy.wait_recv()
        put_own(blocks(kind, 2, 1))
        add(blocks(kind, 2, 1), cols, cols + band)

    def pack(i, k):
        at = pl.ds(pl.multiple_of(cols + i * ROWS, ROWS), ROWS)
        for o in range(toks // 2 + 1):
            block = pl.ds(pl.multiple_of((t + o) % toks * band, band), band)
            gr[i // 4, i % 4, :, o * band : (o + 1) * band] = acc[at, block] * inverse
        return k

    lax.fori_loop(0, band // ROWS, pack, 0)

    swap_g = rc(gr.at[1 - c], pg, partner)
    swap_g.start()

    def finish_up(kind):
        put_up(blocks(kind, 2, 1))
        add(blocks(kind, 2, 1), 0, cols)

    finish_up(0)

    swap_g.wait_recv()
    for k in range(4):
        hg[k] = gr[c, k] + pg[k]
    scatter = [rc(hg.at[near(y, k)], rg.at[k - 1], chip(near(y, k))) for k in range(1, 4)]
    for copy in scatter:
        copy.start()

    finish_up(1)

    for copy in scatter:
        copy.wait_recv()
    sg[...] = hg[y] + rg[0] + rg[1] + rg[2]
    rows = s.at[z, x, c, y // 2, pl.ds((y % 2) * ROWS, ROWS)]
    keep = pltpu.make_async_copy(sg, rows, own.at[0])
    keep.start()
    spread_g = [rc(sg, rows, chip(near(y, k))) for k in range(1, 4)]
    for copy in spread_g:
        copy.start()

    share_rows = cols // 8

    def rows_of(yy, cc):
        return pl.ds(pl.multiple_of(yy * 2 * share_rows + cc * share_rows, share_rows), share_rows)

    def finish(cc):
        def tile(i, k):
            per = share_rows // ROWS
            at = pl.ds(pl.multiple_of(i // per * 2 * share_rows + cc * share_rows + i % per * ROWS, ROWS), ROWS)
            acc[at, :] = acc[at, :] * (0.9 * inverse) + squares * wt[at, :].astype(F32)
            return k

        lax.fori_loop(0, 4 * share_rows // ROWS, tile, 0)

    finish(1 - c)
    swap_t = [rc(acc.at[rows_of(k, 1 - c)], pt.at[k], partner) for k in range(4)]
    for copy in swap_t:
        copy.start()

    keep.wait()
    for copy in spread_g:
        copy.wait_recv()

    a_first_g, a_onward_g = stage(lambda i: s.at[z, i, c, 0], lambda i, h: s.at[z, i, c, 0, pl.ds(16 * h, 16)], lambda i: tok(z, i), x)
    b_first_g, b_onward_g = stage(lambda i: s.at[i, x, c, 1], lambda i, h: s.at[i, x, c, 1, pl.ds(16 * h, 16)], lambda i: tok(i, x), z)
    for copy in a_first_g + b_first_g:
        copy.start()

    finish(c)

    for got, copy in zip(a_first_g + b_first_g, a_onward_g + b_onward_g):
        got.wait_recv()
        copy.start()

    for k in range(4):
        swap_t[k].wait_recv()
        ht[k] = acc[rows_of(k, c), :] + pt[k]
    mid = share_rows // 2
    first_t = [
        rc(ht.at[across, pl.ds(0, mid)], far.at[0], chip(up)),
        rc(ht.at[across, pl.ds(mid, mid)], far.at[1], chip(down)),
    ]
    for copy in first_t:
        copy.start()

    for copy in a_onward_g + b_onward_g:
        copy.wait_recv()

    a_near_g, a_far_g = stage(lambda i: s.at[i, :, c, 0], lambda i, h: s.at[i, pl.ds(2 * h, 2), c, 0], lambda i: tok(i, x), z)
    b_near_g, b_far_g = stage(lambda i: s.at[:, i, c, 1], lambda i, h: s.at[pl.ds(2 * h, 2), i, c, 1], lambda i: tok(z, i), x)
    for copy in a_near_g + b_near_g:
        copy.start()

    def hand(block):
        copy = rc(block, block, partner)
        copy.start()
        return copy

    hands = [hand(s.at[z, :, c, 0]), hand(s.at[:, x, c, 1])]

    first_t[0].wait_recv()
    ht[up, :mid] = ht[up, :mid] + far[0]
    first_t[1].wait_recv()
    ht[down, mid:] = ht[down, mid:] + far[1]
    second_t = [rc(ht.at[up], close.at[0], chip(up)), rc(ht.at[down], close.at[1], chip(down))]
    for copy in second_t:
        copy.start()

    for got, copy in zip(a_near_g + b_near_g, a_far_g + b_far_g):
        got.wait_recv()
        copy.start()
    hands += [hand(s.at[near(z, -1), :, c, 0]), hand(s.at[near(z, 1), :, c, 0])]
    hands += [hand(s.at[:, near(x, -1), c, 1]), hand(s.at[:, near(x, 1), c, 1])]

    for copy in second_t:
        copy.wait_recv()
    b_ref[...] = ht[y] + close[0] + close[1]

    for copy in a_far_g + b_far_g:
        copy.wait_recv()
    hands += [hand(s.at[near(z, 2), :, c, 0]), hand(s.at[:, near(x, 2), c, 1])]
    for copy in hands:
        copy.wait_recv()

    sent = a_first + b_first + a_onward + b_onward
    for h in range(2):
        sent += a_near[h] + b_near[h] + a_far[h] + b_far[h]
    sent += [swap_g] + scatter + spread_g + swap_t + first_t + second_t
    sent += a_first_g + b_first_g + a_onward_g + b_onward_g + a_near_g + b_near_g + a_far_g + b_far_g + hands
    for copy in sent:
        copy.wait_send()
    lax.fori_loop(1, toks, lambda k, v: (share(k).wait_send(), v)[1], 0)


def build(tokens, ids, weight, toks):
    count, width = tokens.shape
    cols = weight.shape[1]
    band = width // toks
    half = count // 2
    keep = (toks // 2 + 1) * band
    part, share = band // 8, cols // 8
    copies = 67
    vmem = pl.BlockSpec(memory_space=pltpu.VMEM)
    system, right = pl.pallas_call(
        functools.partial(build_kernel, toks),
        out_shape=(
            jax.ShapeDtypeStruct((SIDE, SIDE, 2, 2, 2 * part, keep), F32),
            jax.ShapeDtypeStruct((share, width), F32),
        ),
        in_specs=[pl.BlockSpec(memory_space=pl.ANY), vmem, vmem],
        out_specs=(pl.BlockSpec(memory_space=pl.ANY), vmem),
        scratch_shapes=[
            pltpu.VMEM((2, half, width), BF16),
            pltpu.VMEM((2 * SIDE, SIDE, half, width), BF16),
            pltpu.VMEM((cols + band, 2 * half), BF16),
            pltpu.VMEM((cols + band, width), F32),
            pltpu.VMEM((cols, width), BF16),
            pltpu.VMEM((1, width + 128), F32),
            pltpu.VMEM((toks, 1, width + 128), F32),
            pltpu.VMEM((2, 4, part, keep), F32),
            pltpu.VMEM((4, part, keep), F32),
            pltpu.VMEM((4, part, keep), F32),
            pltpu.VMEM((3, part, keep), F32),
            pltpu.VMEM((part, keep), F32),
            pltpu.VMEM((4, share, width), F32),
            pltpu.VMEM((4, share, width), F32),
            pltpu.VMEM((2, share // 2, width), F32),
            pltpu.VMEM((2, share, width), F32),
            pltpu.SemaphoreType.DMA((copies,)),
            pltpu.SemaphoreType.DMA((copies,)),
            pltpu.SemaphoreType.DMA((2,)),
            pltpu.SemaphoreType.DMA((toks,)),
            pltpu.SemaphoreType.DMA((toks,)),
        ],
        compiler_params=pltpu.CompilerParams(collective_id=0, has_side_effects=True, vmem_limit_bytes=60 << 20),
        name="build",
    )(tokens, ids, weight)
    return system.reshape(width, keep), right


def spread_kernel(a_ref, out, send, recv, own):
    e = lax.axis_index("expert")
    y, c = e // 2, e % 2
    share = a_ref.shape[0]
    rc = functools.partial(remote, (send, recv))

    def chip(yy):
        return {"expert": yy * 2 + c}

    partner = {"expert": e + 1 - 2 * c}
    up, down, across = near(y, 1), near(y, -1), near(y, 2)
    meet([partner, chip(up), chip(down)])
    half = share // 2

    def part(at, h):
        return out.at[at, c, pl.ds(half * h, half)]

    mine = [a_ref.at[pl.ds(half * h, half)] for h in range(2)]
    to_up = [rc(h, mine[h], part(y, h), chip(up)) for h in range(2)]
    to_down = [rc(2 + h, mine[h], part(y, h), chip(down)) for h in range(2)]
    onward = [rc(4, part(down, 0), part(down, 0), chip(up)), rc(5, part(up, 1), part(up, 1), chip(down))]
    pairs = []

    def hand(source, target):
        copy = rc(6 + len(pairs), source, target, partner)
        copy.start()
        pairs.append(copy)

    for copy in (to_up[0], to_down[1], to_up[1], to_down[0]):
        copy.start()
    hand(a_ref, out.at[y, c])
    keep = pltpu.make_async_copy(a_ref, out.at[y, c], own.at[0])
    keep.start()
    to_up[0].wait_recv()
    onward[0].start()
    to_down[1].wait_recv()
    onward[1].start()
    hand(part(down, 0), part(down, 0))
    hand(part(up, 1), part(up, 1))
    to_up[1].wait_recv()
    hand(part(down, 1), part(down, 1))
    to_down[0].wait_recv()
    hand(part(up, 0), part(up, 0))
    for h in range(2):
        onward[h].wait_recv()
        hand(part(across, h), part(across, h))
    keep.wait()
    for copy in pairs:
        copy.wait_recv()
    for copy in to_up + to_down + onward + pairs:
        copy.wait_send()


def spread(answer):
    share, width = answer.shape
    out = pl.pallas_call(
        spread_kernel,
        out_shape=jax.ShapeDtypeStruct((4, 2, share, width), F32),
        in_specs=[pl.BlockSpec(memory_space=pltpu.VMEM)],
        out_specs=pl.BlockSpec(memory_space=pl.ANY),
        scratch_shapes=[pltpu.SemaphoreType.DMA((13,)), pltpu.SemaphoreType.DMA((13,)), pltpu.SemaphoreType.DMA((1,))],
        compiler_params=pltpu.CompilerParams(collective_id=1, has_side_effects=True),
        name="spread",
    )(answer)
    return out.reshape(8 * share, width)


def solve_kernel(width, cols, t_hbm, b_ref, x_ref, stage, full, sh, sm, sl, dvec, dinv, stack, r, ri, p, d, q, rz, goal, nn, xx, sems):
    blk = width // sems.shape[0]
    loads = [
        pltpu.make_async_copy(t_hbm.at[pl.ds(i * blk, blk)], stage.at[pl.ds(i * blk, blk)], sems.at[i])
        for i in range(width // blk)
    ]
    for load in loads:
        load.start()
    band = 128
    bands = width // band
    eye = lax.broadcasted_iota(jnp.int32, (band, band), 0) == lax.broadcasted_iota(jnp.int32, (band, band), 1)

    def block(i):
        return pl.ds(pl.multiple_of(i * band, band), band)

    for i, load in enumerate(loads):
        load.wait()

        def unfold(t, c):
            for o in range(bands // 2 + 1):
                j = (t + o) % bands
                tile = stage[block(t), o * band : (o + 1) * band]
                full[block(t), block(j)] = tile
                sh[block(t), block(j)] = tile.astype(BF16)
                if o == 0:
                    dvec[:, block(t)] = jnp.sum(jnp.where(eye, tile, 0.0), axis=0, keepdims=True)
                elif o < bands // 2:
                    turned = tile.T
                    full[block(j), block(t)] = turned
                    sh[block(j), block(t)] = turned.astype(BF16)
            return c

        lax.fori_loop(i * blk // band, (i + 1) * blk // band, unfold, 0)
    dinv[...] = 1.0 / dvec[...]

    parts = cols // ROWS

    def at(i, which=0):
        return slice(which * cols + i * ROWS, which * cols + (i + 1) * ROWS)

    def lanes(v):
        return jnp.broadcast_to(v, (ROWS, 128))

    def total(v):
        return jnp.sum(v, axis=1, keepdims=True)

    def halves(i, v):
        high = v.astype(BF16)
        low = (v - high.astype(F32)).astype(BF16)
        stack[at(i), :] = high
        stack[at(i, 1), :] = low
        return high.astype(F32) + low.astype(F32)

    def dot(rows, piece):
        return jnp.dot(stack[:rows, :], piece[...], preferred_element_type=F32)

    for i in range(parts):
        b = b_ref[at(i), :]
        x_ref[at(i), :] = jnp.zeros_like(b)
        r[at(i), :] = b
        nn[at(i), :] = lanes(total(b * b * dinv[...]))
        xx[at(i), :] = jnp.zeros((ROWS, 128), F32)

    def outer(carry):
        k, _ = carry
        for i in range(parts):
            v = r[at(i), :]
            ri[at(i), :] = v
            p[at(i), :] = halves(i, v * dinv[...])
            d[at(i), :] = jnp.zeros_like(v)
            rz[at(i), :] = nn[at(i), :]
            goal[at(i), :] = jnp.maximum(nn[at(i), :] * (INNER_TOL * INNER_TOL), xx[at(i), :] * (0.25 * OUTER_TOL * OUTER_TOL))

        def inner(carry):
            it, _ = carry
            wide = dot(2 * cols, sh)
            q[...] = 0.9 * (wide[:cols] + wide[cols:])

            @pl.when(k >= 2)
            def _():
                q[...] += 0.9 * dot(cols, sm)

            each = range(parts)
            pq = []
            for i in each:
                v = p[at(i), :]
                w = q[at(i), :] + 0.1 * dvec[...] * v
                q[at(i), :] = w
                pq.append(total(v * w))
            alpha = [jnp.where(pq[i] > 0, rz[at(i), :1] / jnp.where(pq[i] > 0, pq[i], 1.0), 0.0) for i in each]
            new = []
            for i in each:
                d[at(i), :] += alpha[i] * p[at(i), :]
                res = ri[at(i), :] - alpha[i] * q[at(i), :]
                ri[at(i), :] = res
                new.append(total(res * res * dinv[...]))
            worst = jnp.float32(-1.0)
            for i in each:
                old = rz[at(i), :1]
                beta = jnp.where(old > 0, new[i] / jnp.where(old > 0, old, 1.0), 0.0)
                p[at(i), :] = halves(i, ri[at(i), :] * dinv[...] + beta * p[at(i), :])
                rz[at(i), :] = lanes(new[i])
                worst = jnp.maximum(worst, jnp.max(new[i] - goal[at(i), :1]))
            return it + 1, worst

        cap = jnp.where(k < 2, 64, 4000)
        lax.while_loop(lambda c: jnp.logical_and(c[0] < cap, c[1] > 0), inner, (jnp.int32(0), jnp.float32(1.0)))

        @pl.when(k == 0)
        def _():
            def rest(j, c):
                at = pl.ds(pl.multiple_of(j * 32, 32), 32)
                sm[at, :] = (full[at, :] - sh[at, :].astype(F32)).astype(BF16)
                return c

            lax.fori_loop(0, width // 32, rest, 0)

        @pl.when(k == 2)
        def _():
            def rest(j, c):
                at = pl.ds(pl.multiple_of(j * 32, 32), 32)
                sl[at, :] = (full[at, :] - sh[at, :].astype(F32) - sm[at, :].astype(F32)).astype(BF16)
                return c

            lax.fori_loop(0, width // 32, rest, 0)

        for i in range(parts):
            halves(i, d[at(i), :])
            d[at(i), :] += x_ref[at(i), :]

        @pl.when(k < 2)
        def _():
            wide = dot(2 * cols, sm)
            q[...] = ri[...] - 0.9 * (wide[:cols] + wide[cols:])

        @pl.when(k >= 2)
        def _():
            for i in range(parts):
                v = d[at(i), :]
                stack[at(i, 2), :] = (v - halves(i, v)).astype(BF16)
                q[at(i), :] = b_ref[at(i), :] - 0.1 * dvec[...] * v
            wide = dot(3 * cols, sh)
            q[...] -= 0.9 * (wide[:cols] + wide[cols : 2 * cols] + wide[2 * cols :])
            wide = dot(2 * cols, sm)
            q[...] -= 0.9 * (wide[:cols] + wide[cols:])
            q[...] -= 0.9 * dot(cols, sl)

        worst = jnp.float32(-1.0)
        for i in range(parts):
            new = q[at(i), :]
            size = total(new * new * dinv[...])
            better = size < nn[at(i), :1]
            x = jnp.where(better, d[at(i), :], x_ref[at(i), :])
            x_ref[at(i), :] = x
            r[at(i), :] = jnp.where(better, new, r[at(i), :])
            kept = jnp.where(better, size, nn[at(i), :1])
            nn[at(i), :] = lanes(kept)
            norm = total(x * x * dvec[...])
            xx[at(i), :] = lanes(norm)
            worst = jnp.maximum(worst, jnp.max(kept - (OUTER_TOL * OUTER_TOL) * norm))
        return k + 1, worst

    def more(carry):
        return jnp.logical_and(carry[0] < 20, carry[1] > 0)

    lax.while_loop(more, outer, (jnp.int32(0), jnp.float32(1.0)))


def solve(system, right):
    width, keep = system.shape
    cols = right.shape[0]
    vec = pltpu.VMEM((cols, width), F32)
    col = pltpu.VMEM((cols, 128), F32)
    piece = pltpu.VMEM((width, width), BF16)
    row = pltpu.VMEM((1, width), F32)
    return pl.pallas_call(
        functools.partial(solve_kernel, width, cols),
        out_shape=jax.ShapeDtypeStruct((cols, width), F32),
        in_specs=[pl.BlockSpec(memory_space=pl.ANY), pl.BlockSpec(memory_space=pltpu.VMEM)],
        out_specs=pl.BlockSpec(memory_space=pltpu.VMEM),
        scratch_shapes=[
            pltpu.VMEM((width, keep), F32),
            pltpu.VMEM((width, width), F32),
            piece, piece, piece,
            row, row,
            pltpu.VMEM((3 * cols, width), BF16),
            vec, vec, vec, vec, vec,
            col, col, col, col,
            pltpu.SemaphoreType.DMA((8,)),
        ],
        compiler_params=pltpu.CompilerParams(vmem_limit_bytes=60 << 20),
        name="solve",
    )(system, right)


def local(hidden, token_ids, weights):
    system, right = build(hidden[0], token_ids.reshape(-1, 128), weights[0], lax.axis_size("tok"))
    return spread(solve(system, right)).T


def solution(mesh):
    return jax.shard_map(
        local,
        mesh=mesh,
        in_specs=(P("expert", "tok", None), P("expert", "tok"), P("expert", None, "tok")),
        out_specs=P(None, "tok"),
        check_vma=False,
    )
```

```python
import functools

import jax
import jax.numpy as jnp
from jax import lax
from jax.experimental import pallas as pl
from jax.experimental.pallas import tpu as pltpu
from jax.sharding import PartitionSpec as P

F32, BF16 = jnp.float32, jnp.bfloat16
MESH = pl.DeviceIdType.MESH
SIDE = 4
INNER_TOL = 8e-3
OUTER_TOL = 5e-5
ROWS = 16


def near(i, step):
    return (i + step + SIDE) % SIDE


def remote(sems, index, source, target, device):
    send, recv = sems
    return pltpu.make_async_remote_copy(
        src_ref=source, dst_ref=target, send_sem=send.at[index], recv_sem=recv.at[index],
        device_id=device, device_id_type=MESH,
    )


def meet(devices):
    barrier = pltpu.get_barrier_semaphore()
    for device in devices:
        pl.semaphore_signal(barrier, inc=1, device_id=device, device_id_type=MESH)
    pl.semaphore_wait(barrier, len(devices))


def build_kernel(toks, x_hbm, ids_ref, w_ref, s, b_ref, raw, X, cat, acc, wt, stat, stats, gr, pg, hg, rg, sg, pt, ht, far, close,
                 send, recv, own, stat_send, stat_recv):
    e, t = lax.axis_index("expert"), lax.axis_index("tok")
    y, c = e // 2, e % 2
    z, x = t // SIDE, t % SIDE
    width, cols = w_ref.shape
    band = width // toks
    half = x_hbm.shape[0] // 2
    count = iter(range(send.shape[0]))

    def rc(source, target, device):
        return remote((send, recv), next(count), source, target, device)

    def tok(zz, xx):
        return {"tok": zz * SIDE + xx}

    def chip(yy):
        return {"expert": yy * 2 + c}

    partner = {"expert": e + 1 - 2 * c}
    up, down, across = near(y, 1), near(y, -1), near(y, 2)
    loads = [pltpu.make_async_copy(x_hbm.at[pl.ds(k * half, half)], raw.at[k], own.at[k]) for k in range(2)]
    for load in loads:
        load.start()
    eye = lax.broadcasted_iota(jnp.int32, (half, half), 0) == lax.broadcasted_iota(jnp.int32, (half, half), 1)
    alive = [
        jnp.sum(jnp.where(eye, jnp.where(ids_ref[k : k + 1, :] != 128004, 1.0, 0.0), 0.0), axis=1, keepdims=True)
        for k in range(2)
    ]
    meet([{"tok": (t + k) % toks} for k in range(1, toks)] + [partner, chip(up), chip(down), chip(across)])
    mine = (X.at[z, x], X.at[SIDE + x, z])

    def stage(block, part, to, here):
        above, below = near(here, 1), near(here, -1)
        first = [rc(block(here), block(here), to(above)), rc(block(here), block(here), to(below))]
        onward = [rc(part(below, 0), part(below, 0), to(above)), rc(part(above, 1), part(above, 1), to(below))]
        return first, onward

    quarter = half // 2
    a_first, a_onward = stage(
        lambda i: X.at[z, i], lambda i, h: X.at[z, i, pl.ds(h * quarter, quarter)], lambda i: tok(z, i), x)
    b_first, b_onward = stage(
        lambda i: X.at[SIDE + x, i], lambda i, h: X.at[SIDE + x, i, pl.ds(h * quarter, quarter)], lambda i: tok(i, x), z)

    for k in range(2):
        loads[k].wait()
        for i in range(0, half, 2 * ROWS):
            keep = alive[k][i : i + 2 * ROWS] > 0
            mine[k][i : i + 2 * ROWS, :] = jnp.where(keep, raw[k, i : i + 2 * ROWS, :].astype(F32), 0.0).astype(BF16)
    for copy in a_first + b_first:
        copy.start()

    def clear(i, k):
        at = pl.ds(pl.multiple_of(i * ROWS, ROWS), ROWS)
        acc[at, :] = jnp.zeros((ROWS, width), F32)
        return k

    lax.fori_loop(0, acc.shape[0] // ROWS, clear, 0)

    live = jnp.sum(jnp.where(ids_ref[...] != 128004, 1.0, 0.0), axis=(0, 1), keepdims=True)

    def square(i, total):
        at = pl.ds(pl.multiple_of(i * ROWS, ROWS), ROWS)
        a = X[z, x, at, :].astype(F32)
        b = X[SIDE + x, z, at, :].astype(F32)
        return total + jnp.sum(a * a + b * b, axis=0, keepdims=True)

    stat[:, :width] = lax.fori_loop(0, half // ROWS, square, jnp.zeros((1, width), F32))
    stat[:, width:] = jnp.broadcast_to(live, (1, 128))

    def turn(i, k):
        at = pl.ds(pl.multiple_of(i * 256, 256), 256)
        wt[:, at] = w_ref[at, :].T
        return k

    lax.fori_loop(0, width // 256, turn, 0)

    def group(pair_of, slot_of, to, here, inner):
        above, below = near(here, 1), near(here, -1)
        first, onward = [], []
        for part in range(2):
            h = pair_at(part, inner)
            block = pair_of(here, h)
            first.append([rc(block, block, to(above)), rc(block, block, to(below))])
            lower, upper = slot_of(below, 2 * h), slot_of(above, 2 * h + 1)
            onward.append([rc(lower, lower, to(above)), rc(upper, upper, to(below))])
        return first, onward

    def pair_at(part, inner):
        return inner // 2 * (1 - part) + (1 - inner // 2) * part

    a_near, a_far = group(lambda i, h: X.at[i, pl.ds(2 * h, 2)], lambda i, j: X.at[i, j], lambda i: tok(i, x), z, x)
    b_near, b_far = group(
        lambda i, h: X.at[SIDE + i, pl.ds(2 * h, 2)], lambda i, j: X.at[SIDE + i, j], lambda i: tok(z, i), x, z)

    for got, copy in zip(a_first + b_first, a_onward + b_onward):
        got.wait_recv()
        copy.start()
    for copy in a_near[0] + b_near[0]:
        copy.start()

    def share(k):
        return pltpu.make_async_remote_copy(
            src_ref=stat, dst_ref=stats.at[k], send_sem=stat_send.at[k], recv_sem=stat_recv.at[k],
            device_id={"tok": (t + k) % toks}, device_id_type=MESH,
        )

    for copy in a_onward + b_onward:
        copy.wait_recv()

    for copy in a_near[1] + b_near[1]:
        copy.start()

    lax.fori_loop(1, toks, lambda k, v: (share(k).start(), v)[1], 0)

    pair = 2 * half

    def blocks(kind, off, part):
        here = z * (1 - kind) + x * kind
        h = pair_at(part, x * (1 - kind) + z * kind)
        return X.at[kind * SIDE + (here + off) % SIDE, pl.ds(2 * h, 2)]

    def put_up(block):
        rows = block[...].reshape(pair, width)
        cat[:cols, :] = jnp.dot(rows, w_ref[...], preferred_element_type=F32).astype(BF16).T

    def put_own(block):
        cat[cols:, :] = block[:, :, pl.ds(pl.multiple_of(t * band, band), band)].reshape(pair, band).T

    def add(block, low, high):
        def tile(n, k):
            at = pl.ds(pl.multiple_of(n * 512, 512), 512)
            acc[low:high, at] += jnp.dot(cat[low:high, :], block[:, :, at].reshape(pair, 512), preferred_element_type=F32)
            return k

        lax.fori_loop(0, width // 512, tile, 0)

    def both(block):
        put_up(block)
        put_own(block)
        add(block, 0, cols + band)

    def step(i, k):
        for h in range(2):
            @pl.when(i == 4 + 4 * h)
            def _(h=h):
                for got, copy in zip(a_near[h] + b_near[h], a_far[h] + b_far[h]):
                    got.wait_recv()
                    copy.start()

        q, m = i // 4, i % 4
        a = m % 2
        close_by = (q + 1) // 2
        both(blocks(m // 2, close_by * (3 - 2 * a), (1 - close_by) * a + close_by * (q // 2)))
        return k

    lax.fori_loop(0, 12, step, 0)

    def last(i, k):
        for kind, copies in enumerate((a_far[0], b_far[0])):
            @pl.when(i == kind)
            def _(copies=copies):
                for copy in copies:
                    copy.wait_recv()

        both(blocks(i, 2, 0))
        return k

    lax.fori_loop(0, 2, last, 0)

    lax.fori_loop(1, toks, lambda k, v: (share(k).wait_recv(), v)[1], 0)
    total = stat[...]
    for k in range(1, toks):
        total = total + stats[k]
    inverse = 1.0 / total[:, width : width + 1]
    squares = total[:, :width] * (0.1 * inverse)

    for kind, copies in enumerate((a_far[1], b_far[1])):
        for copy in copies:
            copy.wait_recv()
        put_own(blocks(kind, 2, 1))
        add(blocks(kind, 2, 1), cols, cols + band)

    def pack(i, k):
        at = pl.ds(pl.multiple_of(cols + i * ROWS, ROWS), ROWS)
        for o in range(toks // 2 + 1):
            block = pl.ds(pl.multiple_of((t + o) % toks * band, band), band)
            gr[i // 4, i % 4, :, o * band : (o + 1) * band] = acc[at, block] * inverse
        return k

    lax.fori_loop(0, band // ROWS, pack, 0)

    swap_g = rc(gr.at[1 - c], pg, partner)
    swap_g.start()

    def finish_up(kind):
        put_up(blocks(kind, 2, 1))
        add(blocks(kind, 2, 1), 0, cols)

    finish_up(0)

    swap_g.wait_recv()
    for k in range(4):
        hg[k] = gr[c, k] + pg[k]
    scatter = [rc(hg.at[near(y, k)], rg.at[k - 1], chip(near(y, k))) for k in range(1, 4)]
    for copy in scatter:
        copy.start()

    finish_up(1)

    for copy in scatter:
        copy.wait_recv()
    sg[...] = hg[y] + rg[0] + rg[1] + rg[2]
    rows = s.at[z, x, c, y // 2, pl.ds((y % 2) * ROWS, ROWS)]
    keep = pltpu.make_async_copy(sg, rows, own.at[0])
    keep.start()
    spread_g = [rc(sg, rows, chip(near(y, k))) for k in range(1, 4)]
    for copy in spread_g:
        copy.start()

    share_rows = cols // 8

    def rows_of(yy, cc):
        return pl.ds(pl.multiple_of(yy * 2 * share_rows + cc * share_rows, share_rows), share_rows)

    def finish(cc):
        def tile(i, k):
            per = share_rows // ROWS
            at = pl.ds(pl.multiple_of(i // per * 2 * share_rows + cc * share_rows + i % per * ROWS, ROWS), ROWS)
            acc[at, :] = acc[at, :] * (0.9 * inverse) + squares * wt[at, :].astype(F32)
            return k

        lax.fori_loop(0, 4 * share_rows // ROWS, tile, 0)

    finish(1 - c)
    swap_t = [rc(acc.at[rows_of(k, 1 - c)], pt.at[k], partner) for k in range(4)]
    for copy in swap_t:
        copy.start()

    keep.wait()
    for copy in spread_g:
        copy.wait_recv()

    a_first_g, a_onward_g = stage(lambda i: s.at[z, i, c, 0], lambda i, h: s.at[z, i, c, 0, pl.ds(16 * h, 16)], lambda i: tok(z, i), x)
    b_first_g, b_onward_g = stage(lambda i: s.at[i, x, c, 1], lambda i, h: s.at[i, x, c, 1, pl.ds(16 * h, 16)], lambda i: tok(i, x), z)
    for copy in a_first_g + b_first_g:
        copy.start()

    finish(c)

    a_near_g, a_far_g = group(
        lambda i, h: s.at[i, pl.ds(2 * h, 2), c, 0], lambda i, j: s.at[i, j, c, 0], lambda i: tok(i, x), z, x)
    b_near_g, b_far_g = group(
        lambda i, h: s.at[pl.ds(2 * h, 2), i, c, 1], lambda i, j: s.at[j, i, c, 1], lambda i: tok(z, i), x, z)

    for got, copy in zip(a_first_g + b_first_g, a_onward_g + b_onward_g):
        got.wait_recv()
        copy.start()
    for copy in a_near_g[0] + b_near_g[0]:
        copy.start()

    for k in range(4):
        swap_t[k].wait_recv()
        ht[k] = acc[rows_of(k, c), :] + pt[k]
    mid = share_rows // 2
    first_t = [
        rc(ht.at[across, pl.ds(0, mid)], far.at[0], chip(up)),
        rc(ht.at[across, pl.ds(mid, mid)], far.at[1], chip(down)),
    ]
    for copy in first_t:
        copy.start()

    for copy in a_onward_g + b_onward_g:
        copy.wait_recv()
    for copy in a_near_g[1] + b_near_g[1]:
        copy.start()

    def hand(block):
        copy = rc(block, block, partner)
        copy.start()
        return copy

    hands = [hand(s.at[z, :, c, 0]), hand(s.at[:, x, c, 1])]

    first_t[0].wait_recv()
    ht[up, :mid] = ht[up, :mid] + far[0]
    first_t[1].wait_recv()
    ht[down, mid:] = ht[down, mid:] + far[1]
    second_t = [rc(ht.at[up], close.at[0], chip(up)), rc(ht.at[down], close.at[1], chip(down))]
    for copy in second_t:
        copy.start()

    for part in range(2):
        for got, copy in zip(a_near_g[part] + b_near_g[part], a_far_g[part] + b_far_g[part]):
            got.wait_recv()
            copy.start()
    hands += [hand(s.at[near(z, -1), :, c, 0]), hand(s.at[near(z, 1), :, c, 0])]
    hands += [hand(s.at[:, near(x, -1), c, 1]), hand(s.at[:, near(x, 1), c, 1])]

    for part in range(2):
        for copy in a_far_g[part] + b_far_g[part]:
            copy.wait_recv()
        hands += [
            hand(s.at[near(z, 2), pl.ds(2 * pair_at(part, x), 2), c, 0]),
            hand(s.at[pl.ds(2 * pair_at(part, z), 2), near(x, 2), c, 1]),
        ]

    for copy in second_t:
        copy.wait_recv()
    b_ref[...] = ht[y] + close[0] + close[1]

    for copy in hands:
        copy.wait_recv()

    sent = a_first + b_first + a_onward + b_onward
    for h in range(2):
        sent += a_near[h] + b_near[h] + a_far[h] + b_far[h]
        sent += a_near_g[h] + b_near_g[h] + a_far_g[h] + b_far_g[h]
    sent += [swap_g] + scatter + spread_g + swap_t + first_t + second_t
    sent += a_first_g + b_first_g + a_onward_g + b_onward_g + hands
    for copy in sent:
        copy.wait_send()
    lax.fori_loop(1, toks, lambda k, v: (share(k).wait_send(), v)[1], 0)


def build(tokens, ids, weight, toks):
    count, width = tokens.shape
    cols = weight.shape[1]
    band = width // toks
    half = count // 2
    keep = (toks // 2 + 1) * band
    part, share = band // 8, cols // 8
    copies = 80
    vmem = pl.BlockSpec(memory_space=pltpu.VMEM)
    system, right = pl.pallas_call(
        functools.partial(build_kernel, toks),
        out_shape=(
            jax.ShapeDtypeStruct((SIDE, SIDE, 2, 2, 2 * part, keep), F32),
            jax.ShapeDtypeStruct((share, width), F32),
        ),
        in_specs=[pl.BlockSpec(memory_space=pl.ANY), vmem, vmem],
        out_specs=(pl.BlockSpec(memory_space=pl.ANY), vmem),
        scratch_shapes=[
            pltpu.VMEM((2, half, width), BF16),
            pltpu.VMEM((2 * SIDE, SIDE, half, width), BF16),
            pltpu.VMEM((cols + band, 2 * half), BF16),
            pltpu.VMEM((cols + band, width), F32),
            pltpu.VMEM((cols, width), BF16),
            pltpu.VMEM((1, width + 128), F32),
            pltpu.VMEM((toks, 1, width + 128), F32),
            pltpu.VMEM((2, 4, part, keep), F32),
            pltpu.VMEM((4, part, keep), F32),
            pltpu.VMEM((4, part, keep), F32),
            pltpu.VMEM((3, part, keep), F32),
            pltpu.VMEM((part, keep), F32),
            pltpu.VMEM((4, share, width), F32),
            pltpu.VMEM((4, share, width), F32),
            pltpu.VMEM((2, share // 2, width), F32),
            pltpu.VMEM((2, share, width), F32),
            pltpu.SemaphoreType.DMA((copies,)),
            pltpu.SemaphoreType.DMA((copies,)),
            pltpu.SemaphoreType.DMA((2,)),
            pltpu.SemaphoreType.DMA((toks,)),
            pltpu.SemaphoreType.DMA((toks,)),
        ],
        compiler_params=pltpu.CompilerParams(collective_id=0, has_side_effects=True, vmem_limit_bytes=60 << 20),
        name="build",
    )(tokens, ids, weight)
    return system.reshape(width, keep), right


def spread_kernel(a_ref, out, send, recv, own):
    e = lax.axis_index("expert")
    y, c = e // 2, e % 2
    share = a_ref.shape[0]
    rc = functools.partial(remote, (send, recv))

    def chip(yy):
        return {"expert": yy * 2 + c}

    partner = {"expert": e + 1 - 2 * c}
    up, down, across = near(y, 1), near(y, -1), near(y, 2)
    meet([partner, chip(up), chip(down)])
    half = share // 2

    def part(at, h):
        return out.at[at, c, pl.ds(half * h, half)]

    mine = [a_ref.at[pl.ds(half * h, half)] for h in range(2)]
    to_up = [rc(h, mine[h], part(y, h), chip(up)) for h in range(2)]
    to_down = [rc(2 + h, mine[h], part(y, h), chip(down)) for h in range(2)]
    onward = [rc(4, part(down, 0), part(down, 0), chip(up)), rc(5, part(up, 1), part(up, 1), chip(down))]
    pairs = []

    def hand(source, target):
        copy = rc(6 + len(pairs), source, target, partner)
        copy.start()
        pairs.append(copy)

    for copy in (to_up[0], to_down[1], to_up[1], to_down[0]):
        copy.start()
    hand(a_ref, out.at[y, c])
    keep = pltpu.make_async_copy(a_ref, out.at[y, c], own.at[0])
    keep.start()
    to_up[0].wait_recv()
    onward[0].start()
    to_down[1].wait_recv()
    onward[1].start()
    hand(part(down, 0), part(down, 0))
    hand(part(up, 1), part(up, 1))
    to_up[1].wait_recv()
    hand(part(down, 1), part(down, 1))
    to_down[0].wait_recv()
    hand(part(up, 0), part(up, 0))
    for h in range(2):
        onward[h].wait_recv()
        hand(part(across, h), part(across, h))
    keep.wait()
    for copy in pairs:
        copy.wait_recv()
    for copy in to_up + to_down + onward + pairs:
        copy.wait_send()


def spread(answer):
    share, width = answer.shape
    out = pl.pallas_call(
        spread_kernel,
        out_shape=jax.ShapeDtypeStruct((4, 2, share, width), F32),
        in_specs=[pl.BlockSpec(memory_space=pltpu.VMEM)],
        out_specs=pl.BlockSpec(memory_space=pl.ANY),
        scratch_shapes=[pltpu.SemaphoreType.DMA((13,)), pltpu.SemaphoreType.DMA((13,)), pltpu.SemaphoreType.DMA((1,))],
        compiler_params=pltpu.CompilerParams(collective_id=1, has_side_effects=True),
        name="spread",
    )(answer)
    return out.reshape(8 * share, width)


def solve_kernel(width, cols, t_hbm, b_ref, x_ref, stage, full, sh, sm, sl, dvec, dinv, stack, r, ri, p, d, q, rz, goal, nn, xx, sems):
    blk = width // sems.shape[0]
    loads = [
        pltpu.make_async_copy(t_hbm.at[pl.ds(i * blk, blk)], stage.at[pl.ds(i * blk, blk)], sems.at[i])
        for i in range(width // blk)
    ]
    for load in loads:
        load.start()
    band = 128
    bands = width // band
    eye = lax.broadcasted_iota(jnp.int32, (band, band), 0) == lax.broadcasted_iota(jnp.int32, (band, band), 1)

    def block(i):
        return pl.ds(pl.multiple_of(i * band, band), band)

    for i, load in enumerate(loads):
        load.wait()

        def unfold(t, c):
            for o in range(bands // 2 + 1):
                j = (t + o) % bands
                tile = stage[block(t), o * band : (o + 1) * band]
                full[block(t), block(j)] = tile
                sh[block(t), block(j)] = tile.astype(BF16)
                if o == 0:
                    dvec[:, block(t)] = jnp.sum(jnp.where(eye, tile, 0.0), axis=0, keepdims=True)
                elif o < bands // 2:
                    turned = tile.T
                    full[block(j), block(t)] = turned
                    sh[block(j), block(t)] = turned.astype(BF16)
            return c

        lax.fori_loop(i * blk // band, (i + 1) * blk // band, unfold, 0)
    dinv[...] = 1.0 / dvec[...]

    parts = cols // ROWS

    def at(i, which=0):
        return slice(which * cols + i * ROWS, which * cols + (i + 1) * ROWS)

    def lanes(v):
        return jnp.broadcast_to(v, (ROWS, 128))

    def total(v):
        return jnp.sum(v, axis=1, keepdims=True)

    def halves(i, v):
        high = v.astype(BF16)
        low = (v - high.astype(F32)).astype(BF16)
        stack[at(i), :] = high
        stack[at(i, 1), :] = low
        return high.astype(F32) + low.astype(F32)

    def dot(rows, piece):
        return jnp.dot(stack[:rows, :], piece[...], preferred_element_type=F32)

    for i in range(parts):
        b = b_ref[at(i), :]
        x_ref[at(i), :] = jnp.zeros_like(b)
        r[at(i), :] = b
        nn[at(i), :] = lanes(total(b * b * dinv[...]))
        xx[at(i), :] = jnp.zeros((ROWS, 128), F32)

    def outer(carry):
        k, _ = carry
        for i in range(parts):
            v = r[at(i), :]
            ri[at(i), :] = v
            p[at(i), :] = halves(i, v * dinv[...])
            d[at(i), :] = jnp.zeros_like(v)
            rz[at(i), :] = nn[at(i), :]
            goal[at(i), :] = jnp.maximum(nn[at(i), :] * (INNER_TOL * INNER_TOL), xx[at(i), :] * (0.25 * OUTER_TOL * OUTER_TOL))

        def inner(carry):
            it, _ = carry
            wide = dot(2 * cols, sh)
            q[...] = 0.9 * (wide[:cols] + wide[cols:])

            @pl.when(k >= 2)
            def _():
                q[...] += 0.9 * dot(cols, sm)

            each = range(parts)
            pq = []
            for i in each:
                v = p[at(i), :]
                w = q[at(i), :] + 0.1 * dvec[...] * v
                q[at(i), :] = w
                pq.append(total(v * w))
            alpha = [jnp.where(pq[i] > 0, rz[at(i), :1] / jnp.where(pq[i] > 0, pq[i], 1.0), 0.0) for i in each]
            new = []
            for i in each:
                d[at(i), :] += alpha[i] * p[at(i), :]
                res = ri[at(i), :] - alpha[i] * q[at(i), :]
                ri[at(i), :] = res
                new.append(total(res * res * dinv[...]))
            worst = jnp.float32(-1.0)
            for i in each:
                old = rz[at(i), :1]
                beta = jnp.where(old > 0, new[i] / jnp.where(old > 0, old, 1.0), 0.0)
                p[at(i), :] = halves(i, ri[at(i), :] * dinv[...] + beta * p[at(i), :])
                rz[at(i), :] = lanes(new[i])
                worst = jnp.maximum(worst, jnp.max(new[i] - goal[at(i), :1]))
            return it + 1, worst

        cap = jnp.where(k < 2, 64, 4000)
        lax.while_loop(lambda c: jnp.logical_and(c[0] < cap, c[1] > 0), inner, (jnp.int32(0), jnp.float32(1.0)))

        @pl.when(k == 0)
        def _():
            def rest(j, c):
                at = pl.ds(pl.multiple_of(j * 32, 32), 32)
                sm[at, :] = (full[at, :] - sh[at, :].astype(F32)).astype(BF16)
                return c

            lax.fori_loop(0, width // 32, rest, 0)

        @pl.when(k == 2)
        def _():
            def rest(j, c):
                at = pl.ds(pl.multiple_of(j * 32, 32), 32)
                sl[at, :] = (full[at, :] - sh[at, :].astype(F32) - sm[at, :].astype(F32)).astype(BF16)
                return c

            lax.fori_loop(0, width // 32, rest, 0)

        for i in range(parts):
            halves(i, d[at(i), :])
            d[at(i), :] += x_ref[at(i), :]

        @pl.when(k < 2)
        def _():
            wide = dot(2 * cols, sm)
            q[...] = ri[...] - 0.9 * (wide[:cols] + wide[cols:])

        @pl.when(k >= 2)
        def _():
            for i in range(parts):
                v = d[at(i), :]
                stack[at(i, 2), :] = (v - halves(i, v)).astype(BF16)
                q[at(i), :] = b_ref[at(i), :] - 0.1 * dvec[...] * v
            wide = dot(3 * cols, sh)
            q[...] -= 0.9 * (wide[:cols] + wide[cols : 2 * cols] + wide[2 * cols :])
            wide = dot(2 * cols, sm)
            q[...] -= 0.9 * (wide[:cols] + wide[cols:])
            q[...] -= 0.9 * dot(cols, sl)

        worst = jnp.float32(-1.0)
        for i in range(parts):
            new = q[at(i), :]
            size = total(new * new * dinv[...])
            better = size < nn[at(i), :1]
            x = jnp.where(better, d[at(i), :], x_ref[at(i), :])
            x_ref[at(i), :] = x
            r[at(i), :] = jnp.where(better, new, r[at(i), :])
            kept = jnp.where(better, size, nn[at(i), :1])
            nn[at(i), :] = lanes(kept)
            norm = total(x * x * dvec[...])
            xx[at(i), :] = lanes(norm)
            worst = jnp.maximum(worst, jnp.max(kept - (OUTER_TOL * OUTER_TOL) * norm))
        return k + 1, worst

    def more(carry):
        return jnp.logical_and(carry[0] < 20, carry[1] > 0)

    lax.while_loop(more, outer, (jnp.int32(0), jnp.float32(1.0)))


def solve(system, right):
    width, keep = system.shape
    cols = right.shape[0]
    vec = pltpu.VMEM((cols, width), F32)
    col = pltpu.VMEM((cols, 128), F32)
    piece = pltpu.VMEM((width, width), BF16)
    row = pltpu.VMEM((1, width), F32)
    return pl.pallas_call(
        functools.partial(solve_kernel, width, cols),
        out_shape=jax.ShapeDtypeStruct((cols, width), F32),
        in_specs=[pl.BlockSpec(memory_space=pl.ANY), pl.BlockSpec(memory_space=pltpu.VMEM)],
        out_specs=pl.BlockSpec(memory_space=pltpu.VMEM),
        scratch_shapes=[
            pltpu.VMEM((width, keep), F32),
            pltpu.VMEM((width, width), F32),
            piece, piece, piece,
            row, row,
            pltpu.VMEM((3 * cols, width), BF16),
            vec, vec, vec, vec, vec,
            col, col, col, col,
            pltpu.SemaphoreType.DMA((8,)),
        ],
        compiler_params=pltpu.CompilerParams(vmem_limit_bytes=60 << 20),
        name="solve",
    )(system, right)


def local(hidden, token_ids, weights):
    system, right = build(hidden[0], token_ids.reshape(-1, 128), weights[0], lax.axis_size("tok"))
    return spread(solve(system, right)).T


def solution(mesh):
    return jax.shard_map(
        local,
        mesh=mesh,
        in_specs=(P("expert", "tok", None), P("expert", "tok"), P("expert", None, "tok")),
        out_specs=P(None, "tok"),
        check_vma=False,
    )
```

```python
import functools

import jax
import jax.numpy as jnp
from jax import lax
from jax.experimental import pallas as pl
from jax.experimental.pallas import tpu as pltpu
from jax.sharding import PartitionSpec as P

F32, BF16 = jnp.float32, jnp.bfloat16
MESH = pl.DeviceIdType.MESH
SIDE = 4
INNER_TOL = 8e-3
OUTER_TOL = 5e-5
ROWS = 16


def near(i, step):
    return (i + step + SIDE) % SIDE


def remote(sems, index, source, target, device):
    send, recv = sems
    return pltpu.make_async_remote_copy(
        src_ref=source, dst_ref=target, send_sem=send.at[index], recv_sem=recv.at[index],
        device_id=device, device_id_type=MESH,
    )


def meet(devices):
    barrier = pltpu.get_barrier_semaphore()
    for device in devices:
        pl.semaphore_signal(barrier, inc=1, device_id=device, device_id_type=MESH)
    pl.semaphore_wait(barrier, len(devices))


def build_kernel(toks, x_hbm, ids_ref, w_hbm, s, b_ref, w_ref, raw, X, cat, acc, wt, stat, stats, gr, pg, hg, rg, sg, pt, ht, far, close,
                 send, recv, own, stat_send, stat_recv):
    e, t = lax.axis_index("expert"), lax.axis_index("tok")
    y, c = e // 2, e % 2
    z, x = t // SIDE, t % SIDE
    width, cols = w_ref.shape
    band = width // toks
    half = x_hbm.shape[0] // 2
    count = iter(range(send.shape[0]))

    def rc(source, target, device):
        return remote((send, recv), next(count), source, target, device)

    def tok(zz, xx):
        return {"tok": zz * SIDE + xx}

    def chip(yy):
        return {"expert": yy * 2 + c}

    partner = {"expert": e + 1 - 2 * c}
    up, down, across = near(y, 1), near(y, -1), near(y, 2)
    loads = [pltpu.make_async_copy(x_hbm.at[pl.ds(k * half, half)], raw.at[k], own.at[k]) for k in range(2)]
    for load in loads:
        load.start()
    weights = pltpu.make_async_copy(w_hbm, w_ref, own.at[2])
    weights.start()
    eye = lax.broadcasted_iota(jnp.int32, (half, half), 0) == lax.broadcasted_iota(jnp.int32, (half, half), 1)
    alive = [
        jnp.sum(jnp.where(eye, jnp.where(ids_ref[k : k + 1, :] != 128004, 1.0, 0.0), 0.0), axis=1, keepdims=True)
        for k in range(2)
    ]
    meet([{"tok": (t + k) % toks} for k in range(1, toks)] + [partner, chip(up), chip(down), chip(across)])
    mine = (X.at[z, x], X.at[SIDE + x, z])

    def stage(block, part, to, here):
        above, below = near(here, 1), near(here, -1)
        first = [rc(block(here), block(here), to(above)), rc(block(here), block(here), to(below))]
        onward = [rc(part(below, 0), part(below, 0), to(above)), rc(part(above, 1), part(above, 1), to(below))]
        return first, onward

    quarter = half // 2
    a_first, a_onward = stage(
        lambda i: X.at[z, i], lambda i, h: X.at[z, i, pl.ds(h * quarter, quarter)], lambda i: tok(z, i), x)
    b_first, b_onward = stage(
        lambda i: X.at[SIDE + x, i], lambda i, h: X.at[SIDE + x, i, pl.ds(h * quarter, quarter)], lambda i: tok(i, x), z)

    for k in range(2):
        loads[k].wait()
        for i in range(0, half, 2 * ROWS):
            keep = alive[k][i : i + 2 * ROWS] > 0
            mine[k][i : i + 2 * ROWS, :] = jnp.where(keep, raw[k, i : i + 2 * ROWS, :].astype(F32), 0.0).astype(BF16)
    for copy in a_first + b_first:
        copy.start()

    def clear(i, k):
        at = pl.ds(pl.multiple_of(i * ROWS, ROWS), ROWS)
        acc[at, :] = jnp.zeros((ROWS, width), F32)
        return k

    lax.fori_loop(0, acc.shape[0] // ROWS, clear, 0)

    live = jnp.sum(jnp.where(ids_ref[...] != 128004, 1.0, 0.0), axis=(0, 1), keepdims=True)

    def square(i, total):
        at = pl.ds(pl.multiple_of(i * ROWS, ROWS), ROWS)
        a = X[z, x, at, :].astype(F32)
        b = X[SIDE + x, z, at, :].astype(F32)
        return total + jnp.sum(a * a + b * b, axis=0, keepdims=True)

    stat[:, :width] = lax.fori_loop(0, half // ROWS, square, jnp.zeros((1, width), F32))
    stat[:, width:] = jnp.broadcast_to(live, (1, 128))

    weights.wait()

    def turn(i, k):
        at = pl.ds(pl.multiple_of(i * 256, 256), 256)
        wt[:, at] = w_ref[at, :].T
        return k

    lax.fori_loop(0, width // 256, turn, 0)

    def group(pair_of, slot_of, to, here, inner):
        above, below = near(here, 1), near(here, -1)
        first, onward = [], []
        for part in range(2):
            h = pair_at(part, inner)
            block = pair_of(here, h)
            first.append([rc(block, block, to(above)), rc(block, block, to(below))])
            lower, upper = slot_of(below, 2 * h), slot_of(above, 2 * h + 1)
            onward.append([rc(lower, lower, to(above)), rc(upper, upper, to(below))])
        return first, onward

    def pair_at(part, inner):
        return inner // 2 * (1 - part) + (1 - inner // 2) * part

    a_near, a_far = group(lambda i, h: X.at[i, pl.ds(2 * h, 2)], lambda i, j: X.at[i, j], lambda i: tok(i, x), z, x)
    b_near, b_far = group(
        lambda i, h: X.at[SIDE + i, pl.ds(2 * h, 2)], lambda i, j: X.at[SIDE + i, j], lambda i: tok(z, i), x, z)

    for got, copy in zip(a_first + b_first, a_onward + b_onward):
        got.wait_recv()
        copy.start()
    for copy in a_near[0] + b_near[0]:
        copy.start()

    def share(k):
        return pltpu.make_async_remote_copy(
            src_ref=stat, dst_ref=stats.at[k], send_sem=stat_send.at[k], recv_sem=stat_recv.at[k],
            device_id={"tok": (t + k) % toks}, device_id_type=MESH,
        )

    for copy in a_onward + b_onward:
        copy.wait_recv()

    for copy in a_near[1] + b_near[1]:
        copy.start()

    lax.fori_loop(1, toks, lambda k, v: (share(k).start(), v)[1], 0)

    pair = 2 * half

    def blocks(kind, off, part):
        here = z * (1 - kind) + x * kind
        h = pair_at(part, x * (1 - kind) + z * kind)
        return X.at[kind * SIDE + (here + off) % SIDE, pl.ds(2 * h, 2)]

    def put_up(block):
        rows = block[...].reshape(pair, width)
        cat[:cols, :] = jnp.dot(rows, w_ref[...], preferred_element_type=F32).astype(BF16).T

    def put_own(block):
        cat[cols:, :] = block[:, :, pl.ds(pl.multiple_of(t * band, band), band)].reshape(pair, band).T

    def add(block, low, high):
        def tile(n, k):
            at = pl.ds(pl.multiple_of(n * 512, 512), 512)
            acc[low:high, at] += jnp.dot(cat[low:high, :], block[:, :, at].reshape(pair, 512), preferred_element_type=F32)
            return k

        lax.fori_loop(0, width // 512, tile, 0)

    def both(block):
        put_up(block)
        put_own(block)
        add(block, 0, cols + band)

    def step(i, k):
        for h in range(2):
            @pl.when(i == 4 + 4 * h)
            def _(h=h):
                for got, copy in zip(a_near[h] + b_near[h], a_far[h] + b_far[h]):
                    got.wait_recv()
                    copy.start()

        q, m = i // 4, i % 4
        a = m % 2
        close_by = (q + 1) // 2
        both(blocks(m // 2, close_by * (3 - 2 * a), (1 - close_by) * a + close_by * (q // 2)))
        return k

    lax.fori_loop(0, 12, step, 0)

    def last(i, k):
        for kind, copies in enumerate((a_far[0], b_far[0])):
            @pl.when(i == kind)
            def _(copies=copies):
                for copy in copies:
                    copy.wait_recv()

        both(blocks(i, 2, 0))
        return k

    lax.fori_loop(0, 2, last, 0)

    lax.fori_loop(1, toks, lambda k, v: (share(k).wait_recv(), v)[1], 0)
    total = stat[...]
    for k in range(1, toks):
        total = total + stats[k]
    inverse = 1.0 / total[:, width : width + 1]
    squares = total[:, :width] * (0.1 * inverse)

    for kind, copies in enumerate((a_far[1], b_far[1])):
        for copy in copies:
            copy.wait_recv()
        put_own(blocks(kind, 2, 1))
        add(blocks(kind, 2, 1), cols, cols + band)

    def pack(i, k):
        at = pl.ds(pl.multiple_of(cols + i * ROWS, ROWS), ROWS)
        for o in range(toks // 2 + 1):
            block = pl.ds(pl.multiple_of((t + o) % toks * band, band), band)
            gr[i // 4, i % 4, :, o * band : (o + 1) * band] = acc[at, block] * inverse
        return k

    lax.fori_loop(0, band // ROWS, pack, 0)

    swap_g = rc(gr.at[1 - c], pg, partner)
    swap_g.start()

    def finish_up(kind):
        put_up(blocks(kind, 2, 1))
        add(blocks(kind, 2, 1), 0, cols)

    finish_up(0)

    swap_g.wait_recv()
    for k in range(4):
        hg[k] = gr[c, k] + pg[k]
    scatter = [rc(hg.at[near(y, k)], rg.at[k - 1], chip(near(y, k))) for k in range(1, 4)]
    for copy in scatter:
        copy.start()

    finish_up(1)

    for copy in scatter:
        copy.wait_recv()
    sg[...] = hg[y] + rg[0] + rg[1] + rg[2]
    rows = s.at[z, x, c, y // 2, pl.ds((y % 2) * ROWS, ROWS)]
    keep = pltpu.make_async_copy(sg, rows, own.at[0])
    keep.start()
    spread_g = [rc(sg, rows, chip(near(y, k))) for k in range(1, 4)]
    for copy in spread_g:
        copy.start()

    share_rows = cols // 8

    def rows_of(yy, cc):
        return pl.ds(pl.multiple_of(yy * 2 * share_rows + cc * share_rows, share_rows), share_rows)

    def finish(cc):
        def tile(i, k):
            per = share_rows // ROWS
            at = pl.ds(pl.multiple_of(i // per * 2 * share_rows + cc * share_rows + i % per * ROWS, ROWS), ROWS)
            acc[at, :] = acc[at, :] * (0.9 * inverse) + squares * wt[at, :].astype(F32)
            return k

        lax.fori_loop(0, 4 * share_rows // ROWS, tile, 0)

    finish(1 - c)
    swap_t = [rc(acc.at[rows_of(k, 1 - c)], pt.at[k], partner) for k in range(4)]
    for copy in swap_t:
        copy.start()

    keep.wait()
    for copy in spread_g:
        copy.wait_recv()

    a_first_g, a_onward_g = stage(lambda i: s.at[z, i, c, 0], lambda i, h: s.at[z, i, c, 0, pl.ds(16 * h, 16)], lambda i: tok(z, i), x)
    b_first_g, b_onward_g = stage(lambda i: s.at[i, x, c, 1], lambda i, h: s.at[i, x, c, 1, pl.ds(16 * h, 16)], lambda i: tok(i, x), z)
    for copy in a_first_g + b_first_g:
        copy.start()

    finish(c)

    a_near_g, a_far_g = group(
        lambda i, h: s.at[i, pl.ds(2 * h, 2), c, 0], lambda i, j: s.at[i, j, c, 0], lambda i: tok(i, x), z, x)
    b_near_g, b_far_g = group(
        lambda i, h: s.at[pl.ds(2 * h, 2), i, c, 1], lambda i, j: s.at[j, i, c, 1], lambda i: tok(z, i), x, z)

    for got, copy in zip(a_first_g + b_first_g, a_onward_g + b_onward_g):
        got.wait_recv()
        copy.start()
    for copy in a_near_g[0] + b_near_g[0]:
        copy.start()

    for k in range(4):
        swap_t[k].wait_recv()
        ht[k] = acc[rows_of(k, c), :] + pt[k]
    mid = share_rows // 2
    first_t = [
        rc(ht.at[across, pl.ds(0, mid)], far.at[0], chip(up)),
        rc(ht.at[across, pl.ds(mid, mid)], far.at[1], chip(down)),
    ]
    for copy in first_t:
        copy.start()

    for copy in a_onward_g + b_onward_g:
        copy.wait_recv()
    for copy in a_near_g[1] + b_near_g[1]:
        copy.start()

    def hand(block):
        copy = rc(block, block, partner)
        copy.start()
        return copy

    hands = [hand(s.at[z, :, c, 0]), hand(s.at[:, x, c, 1])]

    first_t[0].wait_recv()
    ht[up, :mid] = ht[up, :mid] + far[0]
    first_t[1].wait_recv()
    ht[down, mid:] = ht[down, mid:] + far[1]
    second_t = [rc(ht.at[up], close.at[0], chip(up)), rc(ht.at[down], close.at[1], chip(down))]
    for copy in second_t:
        copy.start()

    for part in range(2):
        for got, copy in zip(a_near_g[part] + b_near_g[part], a_far_g[part] + b_far_g[part]):
            got.wait_recv()
            copy.start()
    hands += [hand(s.at[near(z, -1), :, c, 0]), hand(s.at[near(z, 1), :, c, 0])]
    hands += [hand(s.at[:, near(x, -1), c, 1]), hand(s.at[:, near(x, 1), c, 1])]

    for part in range(2):
        for copy in a_far_g[part] + b_far_g[part]:
            copy.wait_recv()
        hands += [
            hand(s.at[near(z, 2), pl.ds(2 * pair_at(part, x), 2), c, 0]),
            hand(s.at[pl.ds(2 * pair_at(part, z), 2), near(x, 2), c, 1]),
        ]

    for copy in second_t:
        copy.wait_recv()
    b_ref[...] = ht[y] + close[0] + close[1]

    for copy in hands:
        copy.wait_recv()

    sent = a_first + b_first + a_onward + b_onward
    for h in range(2):
        sent += a_near[h] + b_near[h] + a_far[h] + b_far[h]
        sent += a_near_g[h] + b_near_g[h] + a_far_g[h] + b_far_g[h]
    sent += [swap_g] + scatter + spread_g + swap_t + first_t + second_t
    sent += a_first_g + b_first_g + a_onward_g + b_onward_g + hands
    for copy in sent:
        copy.wait_send()
    lax.fori_loop(1, toks, lambda k, v: (share(k).wait_send(), v)[1], 0)


def build(tokens, ids, weight, toks):
    count, width = tokens.shape
    cols = weight.shape[1]
    band = width // toks
    half = count // 2
    keep = (toks // 2 + 1) * band
    part, share = band // 8, cols // 8
    copies = 80
    vmem = pl.BlockSpec(memory_space=pltpu.VMEM)
    system, right = pl.pallas_call(
        functools.partial(build_kernel, toks),
        out_shape=(
            jax.ShapeDtypeStruct((SIDE, SIDE, 2, 2, 2 * part, keep), F32),
            jax.ShapeDtypeStruct((share, width), F32),
        ),
        in_specs=[pl.BlockSpec(memory_space=pl.ANY), vmem, pl.BlockSpec(memory_space=pl.ANY)],
        out_specs=(pl.BlockSpec(memory_space=pl.ANY), vmem),
        scratch_shapes=[
            pltpu.VMEM((width, cols), BF16),
            pltpu.VMEM((2, half, width), BF16),
            pltpu.VMEM((2 * SIDE, SIDE, half, width), BF16),
            pltpu.VMEM((cols + band, 2 * half), BF16),
            pltpu.VMEM((cols + band, width), F32),
            pltpu.VMEM((cols, width), BF16),
            pltpu.VMEM((1, width + 128), F32),
            pltpu.VMEM((toks, 1, width + 128), F32),
            pltpu.VMEM((2, 4, part, keep), F32),
            pltpu.VMEM((4, part, keep), F32),
            pltpu.VMEM((4, part, keep), F32),
            pltpu.VMEM((3, part, keep), F32),
            pltpu.VMEM((part, keep), F32),
            pltpu.VMEM((4, share, width), F32),
            pltpu.VMEM((4, share, width), F32),
            pltpu.VMEM((2, share // 2, width), F32),
            pltpu.VMEM((2, share, width), F32),
            pltpu.SemaphoreType.DMA((copies,)),
            pltpu.SemaphoreType.DMA((copies,)),
            pltpu.SemaphoreType.DMA((3,)),
            pltpu.SemaphoreType.DMA((toks,)),
            pltpu.SemaphoreType.DMA((toks,)),
        ],
        compiler_params=pltpu.CompilerParams(collective_id=0, has_side_effects=True, vmem_limit_bytes=60 << 20),
        name="build",
    )(tokens, ids, weight)
    return system.reshape(width, keep), right


def spread_kernel(a_ref, out, send, recv, own):
    e = lax.axis_index("expert")
    y, c = e // 2, e % 2
    share = a_ref.shape[0]
    rc = functools.partial(remote, (send, recv))

    def chip(yy):
        return {"expert": yy * 2 + c}

    partner = {"expert": e + 1 - 2 * c}
    up, down, across = near(y, 1), near(y, -1), near(y, 2)
    meet([partner, chip(up), chip(down)])
    half = share // 2

    def part(at, h):
        return out.at[at, c, pl.ds(half * h, half)]

    mine = [a_ref.at[pl.ds(half * h, half)] for h in range(2)]
    to_up = [rc(h, mine[h], part(y, h), chip(up)) for h in range(2)]
    to_down = [rc(2 + h, mine[h], part(y, h), chip(down)) for h in range(2)]
    onward = [rc(4, part(down, 0), part(down, 0), chip(up)), rc(5, part(up, 1), part(up, 1), chip(down))]
    pairs = []

    def hand(source, target):
        copy = rc(6 + len(pairs), source, target, partner)
        copy.start()
        pairs.append(copy)

    for copy in (to_up[0], to_down[1], to_up[1], to_down[0]):
        copy.start()
    hand(a_ref, out.at[y, c])
    keep = pltpu.make_async_copy(a_ref, out.at[y, c], own.at[0])
    keep.start()
    to_up[0].wait_recv()
    onward[0].start()
    to_down[1].wait_recv()
    onward[1].start()
    hand(part(down, 0), part(down, 0))
    hand(part(up, 1), part(up, 1))
    to_up[1].wait_recv()
    hand(part(down, 1), part(down, 1))
    to_down[0].wait_recv()
    hand(part(up, 0), part(up, 0))
    for h in range(2):
        onward[h].wait_recv()
        hand(part(across, h), part(across, h))
    keep.wait()
    for copy in pairs:
        copy.wait_recv()
    for copy in to_up + to_down + onward + pairs:
        copy.wait_send()


def spread(answer):
    share, width = answer.shape
    out = pl.pallas_call(
        spread_kernel,
        out_shape=jax.ShapeDtypeStruct((4, 2, share, width), F32),
        in_specs=[pl.BlockSpec(memory_space=pltpu.VMEM)],
        out_specs=pl.BlockSpec(memory_space=pl.ANY),
        scratch_shapes=[pltpu.SemaphoreType.DMA((13,)), pltpu.SemaphoreType.DMA((13,)), pltpu.SemaphoreType.DMA((1,))],
        compiler_params=pltpu.CompilerParams(collective_id=1, has_side_effects=True),
        name="spread",
    )(answer)
    return out.reshape(8 * share, width)


def solve_kernel(width, cols, t_hbm, b_ref, x_ref, stage, sh, sm, sl, dvec, dinv, stack, r, ri, p, d, q, rz, goal, nn, xx, sems):
    blk = width // sems.shape[0]
    loads = [
        pltpu.make_async_copy(t_hbm.at[pl.ds(i * blk, blk)], stage.at[pl.ds(i * blk, blk)], sems.at[i])
        for i in range(width // blk)
    ]
    for load in loads:
        load.start()
    band = 128
    bands = width // band
    eye = lax.broadcasted_iota(jnp.int32, (band, band), 0) == lax.broadcasted_iota(jnp.int32, (band, band), 1)

    def block(i):
        return pl.ds(pl.multiple_of(i * band, band), band)

    def pieces(row, column, tile):
        high = tile.astype(BF16)
        sh[row, column] = high
        sm[row, column] = (tile - high.astype(F32)).astype(BF16)

    def lowest(row, column, tile):
        sl[row, column] = (tile - sh[row, column].astype(F32) - sm[row, column].astype(F32)).astype(BF16)

    for i, load in enumerate(loads):
        load.wait()

        def unfold(t, c):
            for o in range(bands // 2 + 1):
                j = (t + o) % bands
                tile = stage[block(t), o * band : (o + 1) * band]
                pieces(block(t), block(j), tile)
                if o == 0:
                    dvec[:, block(t)] = jnp.sum(jnp.where(eye, tile, 0.0), axis=0, keepdims=True)
                elif o < bands // 2:
                    pieces(block(j), block(t), tile.T)
            return c

        lax.fori_loop(i * blk // band, (i + 1) * blk // band, unfold, 0)
    dinv[...] = 1.0 / dvec[...]

    parts = cols // ROWS

    def at(i, which=0):
        return slice(which * cols + i * ROWS, which * cols + (i + 1) * ROWS)

    def lanes(v):
        return jnp.broadcast_to(v, (ROWS, 128))

    def total(v):
        return jnp.sum(v, axis=1, keepdims=True)

    def halves(i, v):
        high = v.astype(BF16)
        low = (v - high.astype(F32)).astype(BF16)
        stack[at(i), :] = high
        stack[at(i, 1), :] = low
        return high.astype(F32) + low.astype(F32)

    def dot(rows, piece):
        return jnp.dot(stack[:rows, :], piece[...], preferred_element_type=F32)

    for i in range(parts):
        b = b_ref[at(i), :]
        x_ref[at(i), :] = jnp.zeros_like(b)
        r[at(i), :] = b
        nn[at(i), :] = lanes(total(b * b * dinv[...]))
        xx[at(i), :] = jnp.zeros((ROWS, 128), F32)

    def outer(carry):
        k, _ = carry
        for i in range(parts):
            v = r[at(i), :]
            ri[at(i), :] = v
            p[at(i), :] = halves(i, v * dinv[...])
            d[at(i), :] = jnp.zeros_like(v)
            rz[at(i), :] = nn[at(i), :]
            goal[at(i), :] = jnp.maximum(nn[at(i), :] * (INNER_TOL * INNER_TOL), xx[at(i), :] * (0.25 * OUTER_TOL * OUTER_TOL))

        def inner(carry):
            it, _ = carry
            wide = dot(2 * cols, sh)
            q[...] = 0.9 * (wide[:cols] + wide[cols:])

            @pl.when(k >= 2)
            def _():
                q[...] += 0.9 * dot(cols, sm)

            each = range(parts)
            pq = []
            for i in each:
                v = p[at(i), :]
                w = q[at(i), :] + 0.1 * dvec[...] * v
                q[at(i), :] = w
                pq.append(total(v * w))
            alpha = [jnp.where(pq[i] > 0, rz[at(i), :1] / jnp.where(pq[i] > 0, pq[i], 1.0), 0.0) for i in each]
            new = []
            for i in each:
                d[at(i), :] += alpha[i] * p[at(i), :]
                res = ri[at(i), :] - alpha[i] * q[at(i), :]
                ri[at(i), :] = res
                new.append(total(res * res * dinv[...]))
            worst = jnp.float32(-1.0)
            for i in each:
                old = rz[at(i), :1]
                beta = jnp.where(old > 0, new[i] / jnp.where(old > 0, old, 1.0), 0.0)
                p[at(i), :] = halves(i, ri[at(i), :] * dinv[...] + beta * p[at(i), :])
                rz[at(i), :] = lanes(new[i])
                worst = jnp.maximum(worst, jnp.max(new[i] - goal[at(i), :1]))
            return it + 1, worst

        cap = jnp.where(k < 2, 64, 4000)
        lax.while_loop(lambda c: jnp.logical_and(c[0] < cap, c[1] > 0), inner, (jnp.int32(0), jnp.float32(1.0)))

        @pl.when(k == 2)
        def _():
            def unfold(t, c):
                for o in range(bands // 2 + 1):
                    j = (t + o) % bands
                    tile = stage[block(t), o * band : (o + 1) * band]
                    lowest(block(t), block(j), tile)
                    if 0 < o < bands // 2:
                        lowest(block(j), block(t), tile.T)
                return c

            lax.fori_loop(0, bands, unfold, 0)

        for i in range(parts):
            halves(i, d[at(i), :])
            d[at(i), :] += x_ref[at(i), :]

        @pl.when(k < 2)
        def _():
            wide = dot(2 * cols, sm)
            q[...] = ri[...] - 0.9 * (wide[:cols] + wide[cols:])

        @pl.when(k >= 2)
        def _():
            for i in range(parts):
                v = d[at(i), :]
                stack[at(i, 2), :] = (v - halves(i, v)).astype(BF16)
                q[at(i), :] = b_ref[at(i), :] - 0.1 * dvec[...] * v
            wide = dot(3 * cols, sh)
            q[...] -= 0.9 * (wide[:cols] + wide[cols : 2 * cols] + wide[2 * cols :])
            wide = dot(2 * cols, sm)
            q[...] -= 0.9 * (wide[:cols] + wide[cols:])
            q[...] -= 0.9 * dot(cols, sl)

        worst = jnp.float32(-1.0)
        for i in range(parts):
            new = q[at(i), :]
            size = total(new * new * dinv[...])
            better = size < nn[at(i), :1]
            x = jnp.where(better, d[at(i), :], x_ref[at(i), :])
            x_ref[at(i), :] = x
            r[at(i), :] = jnp.where(better, new, r[at(i), :])
            kept = jnp.where(better, size, nn[at(i), :1])
            nn[at(i), :] = lanes(kept)
            norm = total(x * x * dvec[...])
            xx[at(i), :] = lanes(norm)
            worst = jnp.maximum(worst, jnp.max(kept - (OUTER_TOL * OUTER_TOL) * norm))
        return k + 1, worst

    def more(carry):
        return jnp.logical_and(carry[0] < 20, carry[1] > 0)

    lax.while_loop(more, outer, (jnp.int32(0), jnp.float32(1.0)))


def solve(system, right):
    width, keep = system.shape
    cols = right.shape[0]
    vec = pltpu.VMEM((cols, width), F32)
    col = pltpu.VMEM((cols, 128), F32)
    piece = pltpu.VMEM((width, width), BF16)
    row = pltpu.VMEM((1, width), F32)
    return pl.pallas_call(
        functools.partial(solve_kernel, width, cols),
        out_shape=jax.ShapeDtypeStruct((cols, width), F32),
        in_specs=[pl.BlockSpec(memory_space=pl.ANY), pl.BlockSpec(memory_space=pltpu.VMEM)],
        out_specs=pl.BlockSpec(memory_space=pltpu.VMEM),
        scratch_shapes=[
            pltpu.VMEM((width, keep), F32),
            piece, piece, piece,
            row, row,
            pltpu.VMEM((3 * cols, width), BF16),
            vec, vec, vec, vec, vec,
            col, col, col, col,
            pltpu.SemaphoreType.DMA((8,)),
        ],
        compiler_params=pltpu.CompilerParams(vmem_limit_bytes=60 << 20),
        name="solve",
    )(system, right)


def local(hidden, token_ids, weights):
    system, right = build(hidden[0], token_ids.reshape(-1, 128), weights[0], lax.axis_size("tok"))
    return spread(solve(system, right)).T


def solution(mesh):
    return jax.shard_map(
        local,
        mesh=mesh,
        in_specs=(P("expert", "tok", None), P("expert", "tok"), P("expert", None, "tok")),
        out_specs=P(None, "tok"),
        check_vma=False,
    )
```

```python
import functools

import jax
import jax.numpy as jnp
from jax import lax
from jax.experimental import pallas as pl
from jax.experimental.pallas import tpu as pltpu
from jax.sharding import PartitionSpec as P

F32, BF16 = jnp.float32, jnp.bfloat16
MESH = pl.DeviceIdType.MESH
SIDE = 4
INNER_TOL = 8e-3
OUTER_TOL = 5e-5
ROWS = 16


def near(i, step):
    return (i + step + SIDE) % SIDE


def remote(sems, index, source, target, device):
    send, recv = sems
    return pltpu.make_async_remote_copy(
        src_ref=source, dst_ref=target, send_sem=send.at[index], recv_sem=recv.at[index],
        device_id=device, device_id_type=MESH,
    )


def meet(devices):
    barrier = pltpu.get_barrier_semaphore()
    for device in devices:
        pl.semaphore_signal(barrier, inc=1, device_id=device, device_id_type=MESH)
    pl.semaphore_wait(barrier, len(devices))


def build_kernel(toks, x_hbm, ids_ref, w_hbm, s, b_ref, w_ref, raw, X, cat, acc, wt, stat, stats, gr, pg, hg, rg, sg, pt, ht, far, close,
                 send, recv, own, stat_send, stat_recv):
    e, t = lax.axis_index("expert"), lax.axis_index("tok")
    y, c = e // 2, e % 2
    z, x = t // SIDE, t % SIDE
    width, cols = w_ref.shape
    band = width // toks
    half = x_hbm.shape[0] // 2
    count = iter(range(send.shape[0]))

    def rc(source, target, device):
        return remote((send, recv), next(count), source, target, device)

    def tok(zz, xx):
        return {"tok": zz * SIDE + xx}

    def chip(yy):
        return {"expert": yy * 2 + c}

    partner = {"expert": e + 1 - 2 * c}
    up, down, across = near(y, 1), near(y, -1), near(y, 2)
    loads = [pltpu.make_async_copy(x_hbm.at[pl.ds(k * half, half)], raw.at[k], own.at[k]) for k in range(2)]
    for load in loads:
        load.start()
    weights = pltpu.make_async_copy(w_hbm, w_ref, own.at[2])
    weights.start()
    eye = lax.broadcasted_iota(jnp.int32, (half, half), 0) == lax.broadcasted_iota(jnp.int32, (half, half), 1)
    alive = [
        jnp.sum(jnp.where(eye, jnp.where(ids_ref[k : k + 1, :] != 128004, 1.0, 0.0), 0.0), axis=1, keepdims=True)
        for k in range(2)
    ]
    meet([{"tok": (t + k) % toks} for k in range(1, toks)] + [partner, chip(up), chip(down), chip(across)])
    mine = (X.at[z, x], X.at[SIDE + x, z])

    def stage(block, part, to, here):
        above, below = near(here, 1), near(here, -1)
        first = [rc(block(here), block(here), to(above)), rc(block(here), block(here), to(below))]
        onward = [rc(part(below, 0), part(below, 0), to(above)), rc(part(above, 1), part(above, 1), to(below))]
        return first, onward

    quarter = half // 2
    a_first, a_onward = stage(
        lambda i: X.at[z, i], lambda i, h: X.at[z, i, pl.ds(h * quarter, quarter)], lambda i: tok(z, i), x)
    b_first, b_onward = stage(
        lambda i: X.at[SIDE + x, i], lambda i, h: X.at[SIDE + x, i, pl.ds(h * quarter, quarter)], lambda i: tok(i, x), z)

    for k in range(2):
        loads[k].wait()
        for i in range(0, half, 2 * ROWS):
            keep = alive[k][i : i + 2 * ROWS] > 0
            mine[k][i : i + 2 * ROWS, :] = jnp.where(keep, raw[k, i : i + 2 * ROWS, :].astype(F32), 0.0).astype(BF16)
    for copy in a_first + b_first:
        copy.start()

    def clear(i, k):
        at = pl.ds(pl.multiple_of(i * ROWS, ROWS), ROWS)
        acc[at, :] = jnp.zeros((ROWS, width), F32)
        return k

    lax.fori_loop(0, acc.shape[0] // ROWS, clear, 0)

    live = jnp.sum(jnp.where(ids_ref[...] != 128004, 1.0, 0.0), axis=(0, 1), keepdims=True)

    def square(i, total):
        at = pl.ds(pl.multiple_of(i * ROWS, ROWS), ROWS)
        a = X[z, x, at, :].astype(F32)
        b = X[SIDE + x, z, at, :].astype(F32)
        return total + jnp.sum(a * a + b * b, axis=0, keepdims=True)

    stat[:, :width] = lax.fori_loop(0, half // ROWS, square, jnp.zeros((1, width), F32))
    stat[:, width:] = jnp.broadcast_to(live, (1, 128))

    weights.wait()

    def turn(i, k):
        at = pl.ds(pl.multiple_of(i * 256, 256), 256)
        wt[:, at] = w_ref[at, :].T
        return k

    lax.fori_loop(0, width // 256, turn, 0)

    def group(pair_of, slot_of, to, here, inner):
        above, below = near(here, 1), near(here, -1)
        first, onward = [], []
        for part in range(2):
            h = pair_at(part, inner)
            block = pair_of(here, h)
            first.append([rc(block, block, to(above)), rc(block, block, to(below))])
            lower, upper = slot_of(below, 2 * h), slot_of(above, 2 * h + 1)
            onward.append([rc(lower, lower, to(above)), rc(upper, upper, to(below))])
        return first, onward

    def pair_at(part, inner):
        return inner // 2 * (1 - part) + (1 - inner // 2) * part

    a_near, a_far = group(lambda i, h: X.at[i, pl.ds(2 * h, 2)], lambda i, j: X.at[i, j], lambda i: tok(i, x), z, x)
    b_near, b_far = group(
        lambda i, h: X.at[SIDE + i, pl.ds(2 * h, 2)], lambda i, j: X.at[SIDE + i, j], lambda i: tok(z, i), x, z)

    for got, copy in zip(a_first + b_first, a_onward + b_onward):
        got.wait_recv()
        copy.start()
    for copy in a_near[0] + b_near[0]:
        copy.start()

    def share(k):
        return pltpu.make_async_remote_copy(
            src_ref=stat, dst_ref=stats.at[k], send_sem=stat_send.at[k], recv_sem=stat_recv.at[k],
            device_id={"tok": (t + k) % toks}, device_id_type=MESH,
        )

    for copy in a_onward + b_onward:
        copy.wait_recv()

    for copy in a_near[1] + b_near[1]:
        copy.start()

    lax.fori_loop(1, toks, lambda k, v: (share(k).start(), v)[1], 0)

    pair = 2 * half

    def blocks(kind, off, part):
        here = z * (1 - kind) + x * kind
        h = pair_at(part, x * (1 - kind) + z * kind)
        return X.at[kind * SIDE + (here + off) % SIDE, pl.ds(2 * h, 2)]

    def put_up(block):
        rows = block[...].reshape(pair, width)
        cat[:cols, :] = jnp.dot(rows, w_ref[...], preferred_element_type=F32).astype(BF16).T

    def put_own(block):
        cat[cols:, :] = block[:, :, pl.ds(pl.multiple_of(t * band, band), band)].reshape(pair, band).T

    def add(block, low, high):
        def tile(n, k):
            at = pl.ds(pl.multiple_of(n * 512, 512), 512)
            acc[low:high, at] += jnp.dot(cat[low:high, :], block[:, :, at].reshape(pair, 512), preferred_element_type=F32)
            return k

        lax.fori_loop(0, width // 512, tile, 0)

    def both(block):
        put_up(block)
        put_own(block)
        add(block, 0, cols + band)

    def step(i, k):
        for h in range(2):
            @pl.when(i == 4 + 4 * h)
            def _(h=h):
                for got, copy in zip(a_near[h] + b_near[h], a_far[h] + b_far[h]):
                    got.wait_recv()
                    copy.start()

        q, m = i // 4, i % 4
        a = m % 2
        close_by = (q + 1) // 2
        both(blocks(m // 2, close_by * (3 - 2 * a), (1 - close_by) * a + close_by * (q // 2)))
        return k

    lax.fori_loop(0, 12, step, 0)

    def last(i, k):
        for kind, copies in enumerate((a_far[0], b_far[0])):
            @pl.when(i == kind)
            def _(copies=copies):
                for copy in copies:
                    copy.wait_recv()

        both(blocks(i, 2, 0))
        return k

    lax.fori_loop(0, 2, last, 0)

    lax.fori_loop(1, toks, lambda k, v: (share(k).wait_recv(), v)[1], 0)
    total = stat[...]
    for k in range(1, toks):
        total = total + stats[k]
    inverse = 1.0 / total[:, width : width + 1]
    squares = total[:, :width] * (0.1 * inverse)

    for kind, copies in enumerate((a_far[1], b_far[1])):
        for copy in copies:
            copy.wait_recv()
        put_own(blocks(kind, 2, 1))
        add(blocks(kind, 2, 1), cols, cols + band)

    def pack(i, k):
        at = pl.ds(pl.multiple_of(cols + i * ROWS, ROWS), ROWS)
        for o in range(toks // 2 + 1):
            block = pl.ds(pl.multiple_of((t + o) % toks * band, band), band)
            gr[i // 4, i % 4, :, o * band : (o + 1) * band] = acc[at, block] * inverse
        return k

    lax.fori_loop(0, band // ROWS, pack, 0)

    swap_g = rc(gr.at[1 - c], pg, partner)
    swap_g.start()

    put_up(blocks(0, 2, 1))

    swap_g.wait_recv()
    for k in range(4):
        hg[k] = gr[c, k] + pg[k]
    scatter = [rc(hg.at[near(y, k)], rg.at[k - 1], chip(near(y, k))) for k in range(1, 4)]
    for copy in scatter:
        copy.start()

    add(blocks(0, 2, 1), 0, cols)
    put_up(blocks(1, 2, 1))

    for copy in scatter:
        copy.wait_recv()
    sg[...] = hg[y] + rg[0] + rg[1] + rg[2]
    rows = s.at[z, x, c, y // 2, pl.ds((y % 2) * ROWS, ROWS)]
    keep = pltpu.make_async_copy(sg, rows, own.at[0])
    keep.start()
    def rows_at(yy, h):
        return s.at[z, x, c, yy // 2, pl.ds((yy % 2) * ROWS + h * (ROWS // 2), ROWS // 2)]

    spread_g = [rc(sg, rows, chip(up)), rc(sg, rows, chip(down))]
    for copy in spread_g:
        copy.start()
    passed_g = [rc(rows_at(down, 0), rows_at(down, 0), chip(up)), rc(rows_at(up, 1), rows_at(up, 1), chip(down))]

    add(blocks(1, 2, 1), 0, cols)
    share_rows = cols // 8

    def rows_of(yy, cc):
        return pl.ds(pl.multiple_of(yy * 2 * share_rows + cc * share_rows, share_rows), share_rows)

    def finish(cc):
        def tile(i, k):
            per = share_rows // ROWS
            at = pl.ds(pl.multiple_of(i // per * 2 * share_rows + cc * share_rows + i % per * ROWS, ROWS), ROWS)
            acc[at, :] = acc[at, :] * (0.9 * inverse) + squares * wt[at, :].astype(F32)
            return k

        lax.fori_loop(0, 4 * share_rows // ROWS, tile, 0)

    for got, copy in zip(spread_g, passed_g):
        got.wait_recv()
        copy.start()
    finish(1 - c)
    swap_t = [rc(acc.at[rows_of(k, 1 - c)], pt.at[k], partner) for k in range(4)]
    for copy in swap_t:
        copy.start()

    keep.wait()
    for copy in passed_g:
        copy.wait_recv()

    a_first_g, a_onward_g = stage(lambda i: s.at[z, i, c, 0], lambda i, h: s.at[z, i, c, 0, pl.ds(16 * h, 16)], lambda i: tok(z, i), x)
    b_first_g, b_onward_g = stage(lambda i: s.at[i, x, c, 1], lambda i, h: s.at[i, x, c, 1, pl.ds(16 * h, 16)], lambda i: tok(i, x), z)
    for copy in a_first_g + b_first_g:
        copy.start()

    finish(c)

    a_near_g, a_far_g = group(
        lambda i, h: s.at[i, pl.ds(2 * h, 2), c, 0], lambda i, j: s.at[i, j, c, 0], lambda i: tok(i, x), z, x)
    b_near_g, b_far_g = group(
        lambda i, h: s.at[pl.ds(2 * h, 2), i, c, 1], lambda i, j: s.at[j, i, c, 1], lambda i: tok(z, i), x, z)

    for got, copy in zip(a_first_g + b_first_g, a_onward_g + b_onward_g):
        got.wait_recv()
        copy.start()
    for copy in a_near_g[0] + b_near_g[0]:
        copy.start()

    for k in range(4):
        swap_t[k].wait_recv()
        ht[k] = acc[rows_of(k, c), :] + pt[k]
    mid = share_rows // 2
    first_t = [
        rc(ht.at[across, pl.ds(0, mid)], far.at[0], chip(up)),
        rc(ht.at[across, pl.ds(mid, mid)], far.at[1], chip(down)),
    ]
    for copy in first_t:
        copy.start()

    for copy in a_onward_g + b_onward_g:
        copy.wait_recv()
    for copy in a_near_g[1] + b_near_g[1]:
        copy.start()

    def hand(block):
        copy = rc(block, block, partner)
        copy.start()
        return copy

    hands = [hand(s.at[z, :, c, 0]), hand(s.at[:, x, c, 1])]

    first_t[0].wait_recv()
    ht[up, :mid] = ht[up, :mid] + far[0]
    first_t[1].wait_recv()
    ht[down, mid:] = ht[down, mid:] + far[1]
    second_t = [rc(ht.at[up], close.at[0], chip(up)), rc(ht.at[down], close.at[1], chip(down))]
    for copy in second_t:
        copy.start()

    for part in range(2):
        for got, copy in zip(a_near_g[part] + b_near_g[part], a_far_g[part] + b_far_g[part]):
            got.wait_recv()
            copy.start()
    hands += [hand(s.at[near(z, -1), :, c, 0]), hand(s.at[near(z, 1), :, c, 0])]
    hands += [hand(s.at[:, near(x, -1), c, 1]), hand(s.at[:, near(x, 1), c, 1])]

    for part in range(2):
        for copy in a_far_g[part] + b_far_g[part]:
            copy.wait_recv()
        hands += [
            hand(s.at[near(z, 2), pl.ds(2 * pair_at(part, x), 2), c, 0]),
            hand(s.at[pl.ds(2 * pair_at(part, z), 2), near(x, 2), c, 1]),
        ]

    for copy in second_t:
        copy.wait_recv()
    b_ref[...] = ht[y] + close[0] + close[1]

    for copy in hands:
        copy.wait_recv()

    sent = a_first + b_first + a_onward + b_onward
    for h in range(2):
        sent += a_near[h] + b_near[h] + a_far[h] + b_far[h]
        sent += a_near_g[h] + b_near_g[h] + a_far_g[h] + b_far_g[h]
    sent += [swap_g] + scatter + spread_g + passed_g + swap_t + first_t + second_t
    sent += a_first_g + b_first_g + a_onward_g + b_onward_g + hands
    for copy in sent:
        copy.wait_send()
    lax.fori_loop(1, toks, lambda k, v: (share(k).wait_send(), v)[1], 0)


def build(tokens, ids, weight, toks):
    count, width = tokens.shape
    cols = weight.shape[1]
    band = width // toks
    half = count // 2
    keep = (toks // 2 + 1) * band
    part, share = band // 8, cols // 8
    copies = 80
    vmem = pl.BlockSpec(memory_space=pltpu.VMEM)
    system, right = pl.pallas_call(
        functools.partial(build_kernel, toks),
        out_shape=(
            jax.ShapeDtypeStruct((SIDE, SIDE, 2, 2, 2 * part, keep), F32),
            jax.ShapeDtypeStruct((share, width), F32),
        ),
        in_specs=[pl.BlockSpec(memory_space=pl.ANY), vmem, pl.BlockSpec(memory_space=pl.ANY)],
        out_specs=(pl.BlockSpec(memory_space=pl.ANY), vmem),
        scratch_shapes=[
            pltpu.VMEM((width, cols), BF16),
            pltpu.VMEM((2, half, width), BF16),
            pltpu.VMEM((2 * SIDE, SIDE, half, width), BF16),
            pltpu.VMEM((cols + band, 2 * half), BF16),
            pltpu.VMEM((cols + band, width), F32),
            pltpu.VMEM((cols, width), BF16),
            pltpu.VMEM((1, width + 128), F32),
            pltpu.VMEM((toks, 1, width + 128), F32),
            pltpu.VMEM((2, 4, part, keep), F32),
            pltpu.VMEM((4, part, keep), F32),
            pltpu.VMEM((4, part, keep), F32),
            pltpu.VMEM((3, part, keep), F32),
            pltpu.VMEM((part, keep), F32),
            pltpu.VMEM((4, share, width), F32),
            pltpu.VMEM((4, share, width), F32),
            pltpu.VMEM((2, share // 2, width), F32),
            pltpu.VMEM((2, share, width), F32),
            pltpu.SemaphoreType.DMA((copies,)),
            pltpu.SemaphoreType.DMA((copies,)),
            pltpu.SemaphoreType.DMA((3,)),
            pltpu.SemaphoreType.DMA((toks,)),
            pltpu.SemaphoreType.DMA((toks,)),
        ],
        compiler_params=pltpu.CompilerParams(collective_id=0, has_side_effects=True, vmem_limit_bytes=60 << 20),
        name="build",
    )(tokens, ids, weight)
    return system.reshape(width, keep), right


def spread_kernel(a_ref, out, send, recv, own):
    e = lax.axis_index("expert")
    y, c = e // 2, e % 2
    share = a_ref.shape[0]
    rc = functools.partial(remote, (send, recv))

    def chip(yy):
        return {"expert": yy * 2 + c}

    partner = {"expert": e + 1 - 2 * c}
    up, down, across = near(y, 1), near(y, -1), near(y, 2)
    meet([partner, chip(up), chip(down)])
    half = share // 2

    def part(at, h):
        return out.at[at, c, pl.ds(half * h, half)]

    mine = [a_ref.at[pl.ds(half * h, half)] for h in range(2)]
    to_up = [rc(h, mine[h], part(y, h), chip(up)) for h in range(2)]
    to_down = [rc(2 + h, mine[h], part(y, h), chip(down)) for h in range(2)]
    onward = [rc(4, part(down, 0), part(down, 0), chip(up)), rc(5, part(up, 1), part(up, 1), chip(down))]
    pairs = []

    def hand(source, target):
        copy = rc(6 + len(pairs), source, target, partner)
        copy.start()
        pairs.append(copy)

    for copy in (to_up[0], to_down[1], to_up[1], to_down[0]):
        copy.start()
    hand(a_ref, out.at[y, c])
    keep = pltpu.make_async_copy(a_ref, out.at[y, c], own.at[0])
    keep.start()
    to_up[0].wait_recv()
    onward[0].start()
    to_down[1].wait_recv()
    onward[1].start()
    hand(part(down, 0), part(down, 0))
    hand(part(up, 1), part(up, 1))
    to_up[1].wait_recv()
    hand(part(down, 1), part(down, 1))
    to_down[0].wait_recv()
    hand(part(up, 0), part(up, 0))
    for h in range(2):
        onward[h].wait_recv()
        hand(part(across, h), part(across, h))
    keep.wait()
    for copy in pairs:
        copy.wait_recv()
    for copy in to_up + to_down + onward + pairs:
        copy.wait_send()


def spread(answer):
    share, width = answer.shape
    out = pl.pallas_call(
        spread_kernel,
        out_shape=jax.ShapeDtypeStruct((4, 2, share, width), F32),
        in_specs=[pl.BlockSpec(memory_space=pltpu.VMEM)],
        out_specs=pl.BlockSpec(memory_space=pl.ANY),
        scratch_shapes=[pltpu.SemaphoreType.DMA((13,)), pltpu.SemaphoreType.DMA((13,)), pltpu.SemaphoreType.DMA((1,))],
        compiler_params=pltpu.CompilerParams(collective_id=1, has_side_effects=True),
        name="spread",
    )(answer)
    return out.reshape(8 * share, width)


def solve_kernel(width, cols, t_hbm, b_ref, x_ref, stage, sh, sm, sl, dvec, dinv, stack, r, ri, p, d, q, rz, goal, nn, xx, sems):
    blk = width // sems.shape[0]
    loads = [
        pltpu.make_async_copy(t_hbm.at[pl.ds(i * blk, blk)], stage.at[pl.ds(i * blk, blk)], sems.at[i])
        for i in range(width // blk)
    ]
    for load in loads:
        load.start()
    band = 128
    bands = width // band
    eye = lax.broadcasted_iota(jnp.int32, (band, band), 0) == lax.broadcasted_iota(jnp.int32, (band, band), 1)

    def block(i):
        return pl.ds(pl.multiple_of(i * band, band), band)

    def pieces(row, column, tile):
        high = tile.astype(BF16)
        sh[row, column] = high
        sm[row, column] = (tile - high.astype(F32)).astype(BF16)

    def lowest(row, column, tile):
        sl[row, column] = (tile - sh[row, column].astype(F32) - sm[row, column].astype(F32)).astype(BF16)

    for i, load in enumerate(loads):
        load.wait()

        def unfold(t, c):
            for o in range(bands // 2 + 1):
                j = (t + o) % bands
                tile = stage[block(t), o * band : (o + 1) * band]
                pieces(block(t), block(j), tile)
                if o == 0:
                    dvec[:, block(t)] = jnp.sum(jnp.where(eye, tile, 0.0), axis=0, keepdims=True)
                elif o < bands // 2:
                    pieces(block(j), block(t), tile.T)
            return c

        lax.fori_loop(i * blk // band, (i + 1) * blk // band, unfold, 0)
    dinv[...] = 1.0 / dvec[...]

    parts = cols // ROWS

    def at(i, which=0):
        return slice(which * cols + i * ROWS, which * cols + (i + 1) * ROWS)

    def lanes(v):
        return jnp.broadcast_to(v, (ROWS, 128))

    def total(v):
        return jnp.sum(v, axis=1, keepdims=True)

    def halves(i, v):
        high = v.astype(BF16)
        low = (v - high.astype(F32)).astype(BF16)
        stack[at(i), :] = high
        stack[at(i, 1), :] = low
        return high.astype(F32) + low.astype(F32)

    def dot(rows, piece):
        return jnp.dot(stack[:rows, :], piece[...], preferred_element_type=F32)

    for i in range(parts):
        b = b_ref[at(i), :]
        x_ref[at(i), :] = jnp.zeros_like(b)
        r[at(i), :] = b
        nn[at(i), :] = lanes(total(b * b * dinv[...]))
        xx[at(i), :] = jnp.zeros((ROWS, 128), F32)

    def outer(carry):
        k, _ = carry
        for i in range(parts):
            v = r[at(i), :]
            ri[at(i), :] = v
            p[at(i), :] = halves(i, v * dinv[...])
            d[at(i), :] = jnp.zeros_like(v)
            rz[at(i), :] = nn[at(i), :]
            goal[at(i), :] = jnp.maximum(nn[at(i), :] * (INNER_TOL * INNER_TOL), xx[at(i), :] * (0.25 * OUTER_TOL * OUTER_TOL))

        def inner(carry):
            it, _ = carry
            wide = dot(2 * cols, sh)
            q[...] = 0.9 * (wide[:cols] + wide[cols:])

            @pl.when(k >= 2)
            def _():
                q[...] += 0.9 * dot(cols, sm)

            each = range(parts)
            pq = []
            for i in each:
                v = p[at(i), :]
                w = q[at(i), :] + 0.1 * dvec[...] * v
                q[at(i), :] = w
                pq.append(total(v * w))
            alpha = [jnp.where(pq[i] > 0, rz[at(i), :1] / jnp.where(pq[i] > 0, pq[i], 1.0), 0.0) for i in each]
            new = []
            for i in each:
                d[at(i), :] += alpha[i] * p[at(i), :]
                res = ri[at(i), :] - alpha[i] * q[at(i), :]
                ri[at(i), :] = res
                new.append(total(res * res * dinv[...]))
            worst = jnp.float32(-1.0)
            for i in each:
                old = rz[at(i), :1]
                beta = jnp.where(old > 0, new[i] / jnp.where(old > 0, old, 1.0), 0.0)
                p[at(i), :] = halves(i, ri[at(i), :] * dinv[...] + beta * p[at(i), :])
                rz[at(i), :] = lanes(new[i])
                worst = jnp.maximum(worst, jnp.max(new[i] - goal[at(i), :1]))
            return it + 1, worst

        cap = jnp.where(k < 2, 64, 4000)
        lax.while_loop(lambda c: jnp.logical_and(c[0] < cap, c[1] > 0), inner, (jnp.int32(0), jnp.float32(1.0)))

        @pl.when(k == 2)
        def _():
            def unfold(t, c):
                for o in range(bands // 2 + 1):
                    j = (t + o) % bands
                    tile = stage[block(t), o * band : (o + 1) * band]
                    lowest(block(t), block(j), tile)
                    if 0 < o < bands // 2:
                        lowest(block(j), block(t), tile.T)
                return c

            lax.fori_loop(0, bands, unfold, 0)

        for i in range(parts):
            halves(i, d[at(i), :])
            d[at(i), :] += x_ref[at(i), :]

        @pl.when(k < 2)
        def _():
            wide = dot(2 * cols, sm)
            q[...] = ri[...] - 0.9 * (wide[:cols] + wide[cols:])

        @pl.when(k >= 2)
        def _():
            for i in range(parts):
                v = d[at(i), :]
                stack[at(i, 2), :] = (v - halves(i, v)).astype(BF16)
                q[at(i), :] = b_ref[at(i), :] - 0.1 * dvec[...] * v
            wide = dot(3 * cols, sh)
            q[...] -= 0.9 * (wide[:cols] + wide[cols : 2 * cols] + wide[2 * cols :])
            wide = dot(2 * cols, sm)
            q[...] -= 0.9 * (wide[:cols] + wide[cols:])
            q[...] -= 0.9 * dot(cols, sl)

        worst = jnp.float32(-1.0)
        for i in range(parts):
            new = q[at(i), :]
            size = total(new * new * dinv[...])
            better = size < nn[at(i), :1]
            x = jnp.where(better, d[at(i), :], x_ref[at(i), :])
            x_ref[at(i), :] = x
            r[at(i), :] = jnp.where(better, new, r[at(i), :])
            kept = jnp.where(better, size, nn[at(i), :1])
            nn[at(i), :] = lanes(kept)
            norm = total(x * x * dvec[...])
            xx[at(i), :] = lanes(norm)
            worst = jnp.maximum(worst, jnp.max(kept - (OUTER_TOL * OUTER_TOL) * norm))
        return k + 1, worst

    def more(carry):
        return jnp.logical_and(carry[0] < 20, carry[1] > 0)

    lax.while_loop(more, outer, (jnp.int32(0), jnp.float32(1.0)))


def solve(system, right):
    width, keep = system.shape
    cols = right.shape[0]
    vec = pltpu.VMEM((cols, width), F32)
    col = pltpu.VMEM((cols, 128), F32)
    piece = pltpu.VMEM((width, width), BF16)
    row = pltpu.VMEM((1, width), F32)
    return pl.pallas_call(
        functools.partial(solve_kernel, width, cols),
        out_shape=jax.ShapeDtypeStruct((cols, width), F32),
        in_specs=[pl.BlockSpec(memory_space=pl.ANY), pl.BlockSpec(memory_space=pltpu.VMEM)],
        out_specs=pl.BlockSpec(memory_space=pltpu.VMEM),
        scratch_shapes=[
            pltpu.VMEM((width, keep), F32),
            piece, piece, piece,
            row, row,
            pltpu.VMEM((3 * cols, width), BF16),
            vec, vec, vec, vec, vec,
            col, col, col, col,
            pltpu.SemaphoreType.DMA((8,)),
        ],
        compiler_params=pltpu.CompilerParams(vmem_limit_bytes=60 << 20),
        name="solve",
    )(system, right)


def local(hidden, token_ids, weights):
    system, right = build(hidden[0], token_ids.reshape(-1, 128), weights[0], lax.axis_size("tok"))
    return spread(solve(system, right)).T


def solution(mesh):
    return jax.shard_map(
        local,
        mesh=mesh,
        in_specs=(P("expert", "tok", None), P("expert", "tok"), P("expert", None, "tok")),
        out_specs=P(None, "tok"),
        check_vma=False,
    )
```

```python
import functools

import jax
import jax.numpy as jnp
from jax import lax
from jax.experimental import pallas as pl
from jax.experimental.pallas import tpu as pltpu
from jax.sharding import PartitionSpec as P

F32, BF16 = jnp.float32, jnp.bfloat16
MESH = pl.DeviceIdType.MESH
SIDE = 4
INNER_TOL = 8e-3
OUTER_TOL = 5e-5
ROWS = 16


def near(i, step):
    return (i + step + SIDE) % SIDE


def remote(sems, index, source, target, device):
    send, recv = sems
    return pltpu.make_async_remote_copy(
        src_ref=source, dst_ref=target, send_sem=send.at[index], recv_sem=recv.at[index],
        device_id=device, device_id_type=MESH,
    )


def meet(devices):
    barrier = pltpu.get_barrier_semaphore()
    for device in devices:
        pl.semaphore_signal(barrier, inc=1, device_id=device, device_id_type=MESH)
    pl.semaphore_wait(barrier, len(devices))


def build_kernel(toks, x_hbm, ids_ref, w_hbm, s, b_ref, w_ref, raw, X, cat, acc, wt, stat, stats, gr, pg, hg, rg, sg, pt, ht, far, close,
                 send, recv, own, stat_send, stat_recv):
    e, t = lax.axis_index("expert"), lax.axis_index("tok")
    y, c = e // 2, e % 2
    z, x = t // SIDE, t % SIDE
    width, cols = w_ref.shape
    band = width // toks
    half = x_hbm.shape[0] // 2
    count = iter(range(send.shape[0]))

    def rc(source, target, device):
        return remote((send, recv), next(count), source, target, device)

    def tok(zz, xx):
        return {"tok": zz * SIDE + xx}

    def chip(yy):
        return {"expert": yy * 2 + c}

    partner = {"expert": e + 1 - 2 * c}
    up, down, across = near(y, 1), near(y, -1), near(y, 2)
    loads = [pltpu.make_async_copy(x_hbm.at[pl.ds(k * half, half)], raw.at[k], own.at[k]) for k in range(2)]
    for load in loads:
        load.start()
    weights = pltpu.make_async_copy(w_hbm, w_ref, own.at[2])
    weights.start()
    eye = lax.broadcasted_iota(jnp.int32, (half, half), 0) == lax.broadcasted_iota(jnp.int32, (half, half), 1)
    alive = [
        jnp.sum(jnp.where(eye, jnp.where(ids_ref[k : k + 1, :] != 128004, 1.0, 0.0), 0.0), axis=1, keepdims=True)
        for k in range(2)
    ]
    meet([{"tok": (t + k) % toks} for k in range(1, toks)] + [partner, chip(up), chip(down), chip(across)])
    mine = (X.at[z, x], X.at[SIDE + x, z])

    def stage(block, part, to, here):
        above, below = near(here, 1), near(here, -1)
        first = [rc(block(here), block(here), to(above)), rc(block(here), block(here), to(below))]
        onward = [rc(part(below, 0), part(below, 0), to(above)), rc(part(above, 1), part(above, 1), to(below))]
        return first, onward

    quarter = half // 2
    a_first, a_onward = stage(
        lambda i: X.at[z, i], lambda i, h: X.at[z, i, pl.ds(h * quarter, quarter)], lambda i: tok(z, i), x)
    b_first, b_onward = stage(
        lambda i: X.at[SIDE + x, i], lambda i, h: X.at[SIDE + x, i, pl.ds(h * quarter, quarter)], lambda i: tok(i, x), z)

    for k in range(2):
        loads[k].wait()
        for i in range(0, half, 2 * ROWS):
            keep = alive[k][i : i + 2 * ROWS] > 0
            mine[k][i : i + 2 * ROWS, :] = jnp.where(keep, raw[k, i : i + 2 * ROWS, :].astype(F32), 0.0).astype(BF16)
    for copy in a_first + b_first:
        copy.start()

    def clear(i, k):
        at = pl.ds(pl.multiple_of(i * ROWS, ROWS), ROWS)
        acc[at, :] = jnp.zeros((ROWS, width), F32)
        return k

    lax.fori_loop(0, acc.shape[0] // ROWS, clear, 0)

    live = jnp.sum(jnp.where(ids_ref[...] != 128004, 1.0, 0.0), axis=(0, 1), keepdims=True)

    def square(i, total):
        at = pl.ds(pl.multiple_of(i * ROWS, ROWS), ROWS)
        a = X[z, x, at, :].astype(F32)
        b = X[SIDE + x, z, at, :].astype(F32)
        return total + jnp.sum(a * a + b * b, axis=0, keepdims=True)

    stat[:, :width] = lax.fori_loop(0, half // ROWS, square, jnp.zeros((1, width), F32))
    stat[:, width:] = jnp.broadcast_to(live, (1, 128))

    weights.wait()

    def turn(i, k):
        at = pl.ds(pl.multiple_of(i * 256, 256), 256)
        wt[:, at] = w_ref[at, :].T
        return k

    lax.fori_loop(0, width // 256, turn, 0)

    def group(pair_of, slot_of, to, here, inner):
        above, below = near(here, 1), near(here, -1)
        first, onward = [], []
        for part in range(2):
            h = pair_at(part, inner)
            block = pair_of(here, h)
            first.append([rc(block, block, to(above)), rc(block, block, to(below))])
            lower, upper = slot_of(below, 2 * h), slot_of(above, 2 * h + 1)
            onward.append([rc(lower, lower, to(above)), rc(upper, upper, to(below))])
        return first, onward

    def pair_at(part, inner):
        return inner // 2 * (1 - part) + (1 - inner // 2) * part

    a_near, a_far = group(lambda i, h: X.at[i, pl.ds(2 * h, 2)], lambda i, j: X.at[i, j], lambda i: tok(i, x), z, x)
    b_near, b_far = group(
        lambda i, h: X.at[SIDE + i, pl.ds(2 * h, 2)], lambda i, j: X.at[SIDE + i, j], lambda i: tok(z, i), x, z)

    for got, copy in zip(a_first + b_first, a_onward + b_onward):
        got.wait_recv()
        copy.start()
    for copy in a_near[0] + b_near[0]:
        copy.start()

    def share(k):
        return pltpu.make_async_remote_copy(
            src_ref=stat, dst_ref=stats.at[k], send_sem=stat_send.at[k], recv_sem=stat_recv.at[k],
            device_id={"tok": (t + k) % toks}, device_id_type=MESH,
        )

    for copy in a_onward + b_onward:
        copy.wait_recv()

    for copy in a_near[1] + b_near[1]:
        copy.start()

    lax.fori_loop(1, toks, lambda k, v: (share(k).start(), v)[1], 0)

    pair = 2 * half

    def blocks(kind, off, part):
        here = z * (1 - kind) + x * kind
        h = pair_at(part, x * (1 - kind) + z * kind)
        return X.at[kind * SIDE + (here + off) % SIDE, pl.ds(2 * h, 2)]

    def put_up(block):
        rows = block[...].reshape(pair, width)
        cat[:cols, :] = jnp.dot(rows, w_ref[...], preferred_element_type=F32).astype(BF16).T

    def put_own(block):
        cat[cols:, :] = block[:, :, pl.ds(pl.multiple_of(t * band, band), band)].reshape(pair, band).T

    def add(block, low, high):
        def tile(n, k):
            at = pl.ds(pl.multiple_of(n * 512, 512), 512)
            acc[low:high, at] += jnp.dot(cat[low:high, :], block[:, :, at].reshape(pair, 512), preferred_element_type=F32)
            return k

        lax.fori_loop(0, width // 512, tile, 0)

    def both(block):
        put_up(block)
        put_own(block)
        add(block, 0, cols + band)

    def step(i, k):
        for h in range(2):
            @pl.when(i == 4 + 4 * h)
            def _(h=h):
                for got, copy in zip(a_near[h] + b_near[h], a_far[h] + b_far[h]):
                    got.wait_recv()
                    copy.start()

        q, m = i // 4, i % 4
        a = m % 2
        close_by = (q + 1) // 2
        both(blocks(m // 2, close_by * (3 - 2 * a), (1 - close_by) * a + close_by * (q // 2)))
        return k

    lax.fori_loop(0, 12, step, 0)

    def last(i, k):
        for kind, copies in enumerate((a_far[0], b_far[0])):
            @pl.when(i == kind)
            def _(copies=copies):
                for copy in copies:
                    copy.wait_recv()

        both(blocks(i, 2, 0))
        return k

    lax.fori_loop(0, 2, last, 0)

    lax.fori_loop(1, toks, lambda k, v: (share(k).wait_recv(), v)[1], 0)
    total = stat[...]
    for k in range(1, toks):
        total = total + stats[k]
    inverse = 1.0 / total[:, width : width + 1]
    squares = total[:, :width] * (0.1 * inverse)

    for kind, copies in enumerate((a_far[1], b_far[1])):
        for copy in copies:
            copy.wait_recv()
        put_own(blocks(kind, 2, 1))
        add(blocks(kind, 2, 1), cols, cols + band)

    def pack(i, k):
        at = pl.ds(pl.multiple_of(cols + i * ROWS, ROWS), ROWS)
        for o in range(toks // 2 + 1):
            block = pl.ds(pl.multiple_of((t + o) % toks * band, band), band)
            gr[i // 4, i % 4, :, o * band : (o + 1) * band] = acc[at, block] * inverse
        return k

    lax.fori_loop(0, band // ROWS, pack, 0)

    swap_g = rc(gr.at[1 - c], pg, partner)
    swap_g.start()

    put_up(blocks(0, 2, 1))

    swap_g.wait_recv()
    for k in range(4):
        hg[k] = gr[c, k] + pg[k]
    scatter = [rc(hg.at[near(y, k)], rg.at[k - 1], chip(near(y, k))) for k in range(1, 4)]
    for copy in scatter:
        copy.start()

    add(blocks(0, 2, 1), 0, cols)
    put_up(blocks(1, 2, 1))

    for copy in scatter:
        copy.wait_recv()
    sg[...] = hg[y] + rg[0] + rg[1] + rg[2]
    rows = s.at[z, x, c, y // 2, pl.ds((y % 2) * ROWS, ROWS)]
    keep = pltpu.make_async_copy(sg, rows, own.at[0])
    keep.start()
    spread_g = [rc(sg, rows, chip(near(y, k))) for k in range(1, 4)]
    for copy in spread_g:
        copy.start()

    add(blocks(1, 2, 1), 0, cols)
    share_rows = cols // 8

    def rows_of(yy, cc):
        return pl.ds(pl.multiple_of(yy * 2 * share_rows + cc * share_rows, share_rows), share_rows)

    def finish(cc):
        def tile(i, k):
            per = share_rows // ROWS
            at = pl.ds(pl.multiple_of(i // per * 2 * share_rows + cc * share_rows + i % per * ROWS, ROWS), ROWS)
            acc[at, :] = acc[at, :] * (0.9 * inverse) + squares * wt[at, :].astype(F32)
            return k

        lax.fori_loop(0, 4 * share_rows // ROWS, tile, 0)

    finish(1 - c)
    swap_t = [rc(acc.at[rows_of(k, 1 - c)], pt.at[k], partner) for k in range(4)]
    for copy in swap_t:
        copy.start()

    keep.wait()
    for copy in spread_g:
        copy.wait_recv()

    a_first_g, a_onward_g = stage(lambda i: s.at[z, i, c, 0], lambda i, h: s.at[z, i, c, 0, pl.ds(16 * h, 16)], lambda i: tok(z, i), x)
    b_first_g, b_onward_g = stage(lambda i: s.at[i, x, c, 1], lambda i, h: s.at[i, x, c, 1, pl.ds(16 * h, 16)], lambda i: tok(i, x), z)
    for copy in a_first_g + b_first_g:
        copy.start()

    finish(c)

    a_near_g, a_far_g = group(
        lambda i, h: s.at[i, pl.ds(2 * h, 2), c, 0], lambda i, j: s.at[i, j, c, 0], lambda i: tok(i, x), z, x)
    b_near_g, b_far_g = group(
        lambda i, h: s.at[pl.ds(2 * h, 2), i, c, 1], lambda i, j: s.at[j, i, c, 1], lambda i: tok(z, i), x, z)

    for got, copy in zip(a_first_g + b_first_g, a_onward_g + b_onward_g):
        got.wait_recv()
        copy.start()
    for copy in a_near_g[0] + b_near_g[0]:
        copy.start()

    for k in range(4):
        swap_t[k].wait_recv()
        ht[k] = acc[rows_of(k, c), :] + pt[k]
    mid = share_rows // 2
    first_t = [
        rc(ht.at[across, pl.ds(0, mid)], far.at[0], chip(up)),
        rc(ht.at[across, pl.ds(mid, mid)], far.at[1], chip(down)),
    ]
    for copy in first_t:
        copy.start()

    for copy in a_onward_g + b_onward_g:
        copy.wait_recv()
    for copy in a_near_g[1] + b_near_g[1]:
        copy.start()

    def hand(block):
        copy = rc(block, block, partner)
        copy.start()
        return copy

    hands = [hand(s.at[z, :, c, 0]), hand(s.at[:, x, c, 1])]

    first_t[0].wait_recv()
    ht[up, :mid] = ht[up, :mid] + far[0]
    first_t[1].wait_recv()
    ht[down, mid:] = ht[down, mid:] + far[1]
    second_t = [rc(ht.at[up], close.at[0], chip(up)), rc(ht.at[down], close.at[1], chip(down))]
    for copy in second_t:
        copy.start()

    for part in range(2):
        for got, copy in zip(a_near_g[part] + b_near_g[part], a_far_g[part] + b_far_g[part]):
            got.wait_recv()
            copy.start()
    hands += [hand(s.at[near(z, -1), :, c, 0]), hand(s.at[near(z, 1), :, c, 0])]
    hands += [hand(s.at[:, near(x, -1), c, 1]), hand(s.at[:, near(x, 1), c, 1])]

    for part in range(2):
        for copy in a_far_g[part] + b_far_g[part]:
            copy.wait_recv()
        hands += [
            hand(s.at[near(z, 2), pl.ds(2 * pair_at(part, x), 2), c, 0]),
            hand(s.at[pl.ds(2 * pair_at(part, z), 2), near(x, 2), c, 1]),
        ]

    for copy in second_t:
        copy.wait_recv()
    b_ref[...] = ht[y] + close[0] + close[1]

    for copy in hands:
        copy.wait_recv()

    sent = a_first + b_first + a_onward + b_onward
    for h in range(2):
        sent += a_near[h] + b_near[h] + a_far[h] + b_far[h]
        sent += a_near_g[h] + b_near_g[h] + a_far_g[h] + b_far_g[h]
    sent += [swap_g] + scatter + spread_g + swap_t + first_t + second_t
    sent += a_first_g + b_first_g + a_onward_g + b_onward_g + hands
    for copy in sent:
        copy.wait_send()
    lax.fori_loop(1, toks, lambda k, v: (share(k).wait_send(), v)[1], 0)


def build(tokens, ids, weight, toks):
    count, width = tokens.shape
    cols = weight.shape[1]
    band = width // toks
    half = count // 2
    keep = (toks // 2 + 1) * band
    part, share = band // 8, cols // 8
    copies = 80
    vmem = pl.BlockSpec(memory_space=pltpu.VMEM)
    system, right = pl.pallas_call(
        functools.partial(build_kernel, toks),
        out_shape=(
            jax.ShapeDtypeStruct((SIDE, SIDE, 2, 2, 2 * part, keep), F32),
            jax.ShapeDtypeStruct((share, width), F32),
        ),
        in_specs=[pl.BlockSpec(memory_space=pl.ANY), vmem, pl.BlockSpec(memory_space=pl.ANY)],
        out_specs=(pl.BlockSpec(memory_space=pl.ANY), vmem),
        scratch_shapes=[
            pltpu.VMEM((width, cols), BF16),
            pltpu.VMEM((2, half, width), BF16),
            pltpu.VMEM((2 * SIDE, SIDE, half, width), BF16),
            pltpu.VMEM((cols + band, 2 * half), BF16),
            pltpu.VMEM((cols + band, width), F32),
            pltpu.VMEM((cols, width), BF16),
            pltpu.VMEM((1, width + 128), F32),
            pltpu.VMEM((toks, 1, width + 128), F32),
            pltpu.VMEM((2, 4, part, keep), F32),
            pltpu.VMEM((4, part, keep), F32),
            pltpu.VMEM((4, part, keep), F32),
            pltpu.VMEM((3, part, keep), F32),
            pltpu.VMEM((part, keep), F32),
            pltpu.VMEM((4, share, width), F32),
            pltpu.VMEM((4, share, width), F32),
            pltpu.VMEM((2, share // 2, width), F32),
            pltpu.VMEM((2, share, width), F32),
            pltpu.SemaphoreType.DMA((copies,)),
            pltpu.SemaphoreType.DMA((copies,)),
            pltpu.SemaphoreType.DMA((3,)),
            pltpu.SemaphoreType.DMA((toks,)),
            pltpu.SemaphoreType.DMA((toks,)),
        ],
        compiler_params=pltpu.CompilerParams(collective_id=0, has_side_effects=True, vmem_limit_bytes=60 << 20),
        name="build",
    )(tokens, ids, weight)
    return system.reshape(width, keep), right


def spread_kernel(a_ref, out, send, recv, own):
    e = lax.axis_index("expert")
    y, c = e // 2, e % 2
    share = a_ref.shape[0]
    rc = functools.partial(remote, (send, recv))

    def chip(yy):
        return {"expert": yy * 2 + c}

    partner = {"expert": e + 1 - 2 * c}
    up, down, across = near(y, 1), near(y, -1), near(y, 2)
    meet([partner, chip(up), chip(down)])
    half = share // 2

    def part(at, h):
        return out.at[at, c, pl.ds(half * h, half)]

    mine = [a_ref.at[pl.ds(half * h, half)] for h in range(2)]
    to_up = [rc(h, mine[h], part(y, h), chip(up)) for h in range(2)]
    to_down = [rc(2 + h, mine[h], part(y, h), chip(down)) for h in range(2)]
    onward = [rc(4, part(down, 0), part(down, 0), chip(up)), rc(5, part(up, 1), part(up, 1), chip(down))]
    pairs = []

    def hand(source, target):
        copy = rc(6 + len(pairs), source, target, partner)
        copy.start()
        pairs.append(copy)

    for copy in (to_up[0], to_down[1], to_up[1], to_down[0]):
        copy.start()
    hand(a_ref, out.at[y, c])
    keep = pltpu.make_async_copy(a_ref, out.at[y, c], own.at[0])
    keep.start()
    to_up[0].wait_recv()
    onward[0].start()
    to_down[1].wait_recv()
    onward[1].start()
    hand(part(down, 0), part(down, 0))
    hand(part(up, 1), part(up, 1))
    to_up[1].wait_recv()
    hand(part(down, 1), part(down, 1))
    to_down[0].wait_recv()
    hand(part(up, 0), part(up, 0))
    for h in range(2):
        onward[h].wait_recv()
        hand(part(across, h), part(across, h))
    keep.wait()
    for copy in pairs:
        copy.wait_recv()
    for copy in to_up + to_down + onward + pairs:
        copy.wait_send()


def spread(answer):
    share, width = answer.shape
    out = pl.pallas_call(
        spread_kernel,
        out_shape=jax.ShapeDtypeStruct((4, 2, share, width), F32),
        in_specs=[pl.BlockSpec(memory_space=pltpu.VMEM)],
        out_specs=pl.BlockSpec(memory_space=pl.ANY),
        scratch_shapes=[pltpu.SemaphoreType.DMA((13,)), pltpu.SemaphoreType.DMA((13,)), pltpu.SemaphoreType.DMA((1,))],
        compiler_params=pltpu.CompilerParams(collective_id=1, has_side_effects=True),
        name="spread",
    )(answer)
    return out.reshape(8 * share, width)


def solve_kernel(width, cols, t_hbm, b_ref, x_ref, stage, sh, sm, sl, dvec, dinv, stack, r, ri, p, d, q, rz, goal, nn, xx, sems):
    blk = width // sems.shape[0]
    loads = [
        pltpu.make_async_copy(t_hbm.at[pl.ds(i * blk, blk)], stage.at[pl.ds(i * blk, blk)], sems.at[i])
        for i in range(width // blk)
    ]
    for load in loads:
        load.start()
    band = 128
    bands = width // band
    eye = lax.broadcasted_iota(jnp.int32, (band, band), 0) == lax.broadcasted_iota(jnp.int32, (band, band), 1)

    def block(i):
        return pl.ds(pl.multiple_of(i * band, band), band)

    def pieces(row, column, tile):
        high = tile.astype(BF16)
        sh[row, column] = high
        sm[row, column] = (tile - high.astype(F32)).astype(BF16)

    def lowest(row, column, tile):
        sl[row, column] = (tile - sh[row, column].astype(F32) - sm[row, column].astype(F32)).astype(BF16)

    for i, load in enumerate(loads):
        load.wait()

        def unfold(t, c):
            for o in range(bands // 2 + 1):
                j = (t + o) % bands
                tile = stage[block(t), o * band : (o + 1) * band]
                pieces(block(t), block(j), tile)
                if o == 0:
                    dvec[:, block(t)] = jnp.sum(jnp.where(eye, tile, 0.0), axis=0, keepdims=True)
                elif o < bands // 2:
                    pieces(block(j), block(t), tile.T)
            return c

        lax.fori_loop(i * blk // band, (i + 1) * blk // band, unfold, 0)
    dinv[...] = 1.0 / dvec[...]

    parts = cols // ROWS

    def at(i, which=0):
        return slice(which * cols + i * ROWS, which * cols + (i + 1) * ROWS)

    def lanes(v):
        return jnp.broadcast_to(v, (ROWS, 128))

    def total(v):
        return jnp.sum(v, axis=1, keepdims=True)

    def halves(i, v):
        high = v.astype(BF16)
        low = (v - high.astype(F32)).astype(BF16)
        stack[at(i), :] = high
        stack[at(i, 1), :] = low
        return high.astype(F32) + low.astype(F32)

    def dot(rows, piece):
        return jnp.dot(stack[:rows, :], piece[...], preferred_element_type=F32)

    for i in range(parts):
        b = b_ref[at(i), :]
        x_ref[at(i), :] = jnp.zeros_like(b)
        r[at(i), :] = b
        nn[at(i), :] = lanes(total(b * b * dinv[...]))
        xx[at(i), :] = jnp.zeros((ROWS, 128), F32)

    def outer(carry):
        k, _ = carry
        for i in range(parts):
            v = r[at(i), :]
            ri[at(i), :] = v
            p[at(i), :] = halves(i, v * dinv[...])
            d[at(i), :] = jnp.zeros_like(v)
            rz[at(i), :] = nn[at(i), :]
            goal[at(i), :] = jnp.maximum(nn[at(i), :] * (INNER_TOL * INNER_TOL), xx[at(i), :] * (0.25 * OUTER_TOL * OUTER_TOL))

        def inner(carry):
            it, _ = carry
            wide = dot(2 * cols, sh)
            q[...] = 0.9 * (wide[:cols] + wide[cols:])

            @pl.when(k >= 2)
            def _():
                q[...] += 0.9 * dot(cols, sm)

            each = range(parts)
            pq = []
            for i in each:
                v = p[at(i), :]
                w = q[at(i), :] + 0.1 * dvec[...] * v
                q[at(i), :] = w
                pq.append(total(v * w))
            alpha = [jnp.where(pq[i] > 0, rz[at(i), :1] / jnp.where(pq[i] > 0, pq[i], 1.0), 0.0) for i in each]
            new = []
            for i in each:
                d[at(i), :] += alpha[i] * p[at(i), :]
                res = ri[at(i), :] - alpha[i] * q[at(i), :]
                ri[at(i), :] = res
                new.append(total(res * res * dinv[...]))
            worst = jnp.float32(-1.0)
            for i in each:
                old = rz[at(i), :1]
                beta = jnp.where(old > 0, new[i] / jnp.where(old > 0, old, 1.0), 0.0)
                p[at(i), :] = halves(i, ri[at(i), :] * dinv[...] + beta * p[at(i), :])
                rz[at(i), :] = lanes(new[i])
                worst = jnp.maximum(worst, jnp.max(new[i] - goal[at(i), :1]))
            return it + 1, worst

        cap = jnp.where(k < 2, 64, 4000)
        lax.while_loop(lambda c: jnp.logical_and(c[0] < cap, c[1] > 0), inner, (jnp.int32(0), jnp.float32(1.0)))

        @pl.when(k == 2)
        def _():
            def unfold(t, c):
                for o in range(bands // 2 + 1):
                    j = (t + o) % bands
                    tile = stage[block(t), o * band : (o + 1) * band]
                    lowest(block(t), block(j), tile)
                    if 0 < o < bands // 2:
                        lowest(block(j), block(t), tile.T)
                return c

            lax.fori_loop(0, bands, unfold, 0)

        for i in range(parts):
            halves(i, d[at(i), :])
            d[at(i), :] += x_ref[at(i), :]

        @pl.when(k < 2)
        def _():
            wide = dot(2 * cols, sm)
            q[...] = ri[...] - 0.9 * (wide[:cols] + wide[cols:])

        @pl.when(k >= 2)
        def _():
            for i in range(parts):
                v = d[at(i), :]
                stack[at(i, 2), :] = (v - halves(i, v)).astype(BF16)
                q[at(i), :] = b_ref[at(i), :] - 0.1 * dvec[...] * v
            wide = dot(3 * cols, sh)
            q[...] -= 0.9 * (wide[:cols] + wide[cols : 2 * cols] + wide[2 * cols :])
            wide = dot(2 * cols, sm)
            q[...] -= 0.9 * (wide[:cols] + wide[cols:])
            q[...] -= 0.9 * dot(cols, sl)

        worst = jnp.float32(-1.0)
        for i in range(parts):
            new = q[at(i), :]
            size = total(new * new * dinv[...])
            better = size < nn[at(i), :1]
            x = jnp.where(better, d[at(i), :], x_ref[at(i), :])
            x_ref[at(i), :] = x
            r[at(i), :] = jnp.where(better, new, r[at(i), :])
            kept = jnp.where(better, size, nn[at(i), :1])
            nn[at(i), :] = lanes(kept)
            norm = total(x * x * dvec[...])
            xx[at(i), :] = lanes(norm)
            worst = jnp.maximum(worst, jnp.max(kept - (OUTER_TOL * OUTER_TOL) * norm))
        return k + 1, worst

    def more(carry):
        return jnp.logical_and(carry[0] < 20, carry[1] > 0)

    lax.while_loop(more, outer, (jnp.int32(0), jnp.float32(1.0)))


def solve(system, right):
    width, keep = system.shape
    cols = right.shape[0]
    vec = pltpu.VMEM((cols, width), F32)
    col = pltpu.VMEM((cols, 128), F32)
    piece = pltpu.VMEM((width, width), BF16)
    row = pltpu.VMEM((1, width), F32)
    return pl.pallas_call(
        functools.partial(solve_kernel, width, cols),
        out_shape=jax.ShapeDtypeStruct((cols, width), F32),
        in_specs=[pl.BlockSpec(memory_space=pl.ANY), pl.BlockSpec(memory_space=pltpu.VMEM)],
        out_specs=pl.BlockSpec(memory_space=pltpu.VMEM),
        scratch_shapes=[
            pltpu.VMEM((width, keep), F32),
            piece, piece, piece,
            row, row,
            pltpu.VMEM((3 * cols, width), BF16),
            vec, vec, vec, vec, vec,
            col, col, col, col,
            pltpu.SemaphoreType.DMA((8,)),
        ],
        compiler_params=pltpu.CompilerParams(vmem_limit_bytes=60 << 20),
        name="solve",
    )(system, right)


def local(hidden, token_ids, weights):
    system, right = build(hidden[0], token_ids.reshape(-1, 128), weights[0], lax.axis_size("tok"))
    return spread(solve(system, right)).T


def solution(mesh):
    return jax.shard_map(
        local,
        mesh=mesh,
        in_specs=(P("expert", "tok", None), P("expert", "tok"), P("expert", None, "tok")),
        out_specs=P(None, "tok"),
        check_vma=False,
    )
```
